32 devices in a mesh: parts: 2 (over x), rows: 16 (over z, y, core).
Axes of the slice: x: 2, y: 2, z: 4, core: 2. Of those that a mesh axis runs over, the one named last changes fastest.
Arguments:
- rhs: float32 [3, 12288, 256], P(None, 'rows', 'parts'), parts along dimension 2, may hold values from -6 to 6
- diag_inv: float32 [3, 12288, 768], P(None, 'rows'), may hold values from -0.21875 to 0.21875
- tiles: float32 [2, 32, 768, 768], P(None, 'rows'), may hold values from -0.15625 to 0.15625
- dest: int32 [2, 16, 2], P(None, 'rows'), may hold values from 0 to 15, all different within a row; in each aligned block of 16 rows (0 to 15, 16 to 31, ..., all dimensions but the last counted through in order) at most 4 rows name the same one
- obs_weight: float32 [12288], P('rows'), may hold values from -0.108253175 to 0.108253175, as said below
Outputs:
- solution: float32 [3, 12288, 256], P(None, 'rows', 'parts'), parts along dimension 2
- observed: float32 [256], P('parts'), parts along dimension 0
The draws below stay inside these ranges and needn't reach their ends.
There are 2 independent parts, one for each index of `parts`. The reference program is written for one: setup_inputs(seed, part) draws one part's arguments, and reference() takes and returns one part's arrays. A program takes and returns all parts, laid end to end along the dimension named above; an argument that names none is the same for every part. Nothing has to cross between parts.
Inputs may be any that keep to these rules, and one draw needn't show every extreme that they name: `dest`: in each of the two levels, the two entries of a supernode differ, and no supernode of the next level is named more than 4 times. `obs_weight`: finite weights.
All inputs are finite; a program needn't handle non-finite values.
Results may differ from the reference program's by a relative error of at most 0.00029.
Values sent between devices are 32-bit elements; how exact they have to be, the bound alone decides.
No kernel may reach another device: no remote copies, remote signals or barrier semaphores. Data moves between devices by JAX's collectives and lax.ppermute only.
A program may use at most 128 MiB of HBM per device.

```python
import math
import jax
import jax.numpy as jnp
import numpy as np
from jax import lax

SN = 768
R = 128
CAP = 4
NSN = 16


def draw_obs_weight(key, part):
    total = NSN * SN
    position = jnp.arange(total, dtype=jnp.float32) / jnp.float32(max(total - 1, 1))
    base = jax.random.truncated_normal(key, -4.0, 4.0, (total,), jnp.float32)
    ramp = 1.0 + 2.0 * position
    return base * ramp / (3.0 * jnp.sqrt(jnp.float32(total)))


def block_levels(own_key, extent, pieces, smallest, high):
    loudness, own = 1.0, jax.random.fold_in(own_key, 6)
    for dim, shards_of in pieces:
        draws = jnp.exp(jax.random.uniform(jax.random.fold_in(own, dim), (shards_of,), jnp.float32, smallest / len(pieces), high / len(pieces)))
        loudness = loudness * jnp.repeat(draws, extent[dim] // shards_of).reshape([-1 if axis == dim else 1 for axis in range(len(extent))])
    return loudness


def deal_out(key, own, number, rows, number_of, top, limit, lean):
    sequence = jax.random.permutation(key, number_of)
    heavy_load, usual = shares(number_of, rows * top, limit, lean, True), shares(number_of, rows * top, limit, lean, False)
    places = jnp.arange(number_of)

    def named(lengths, turn):
        used = int((lengths > 0).sum())
        fixed = max(1, used // 4)
        passed = fixed + (places - fixed + turn * (used - fixed)) % max(1, number_of - fixed)
        return jnp.zeros((number_of,), jnp.int32).at[sequence[jnp.where(places < fixed, places, passed)]].set(jnp.asarray(lengths, jnp.int32))

    lengths = jnp.where(number % 4 == 0, named(heavy_load, number // 4), named(usual, number - number // 4 - 1))
    mixed = jax.random.permutation(jax.random.fold_in(own, 3), number_of)
    source_of, sink = mixed[0:number_of // 2 * 2:2], mixed[1:number_of // 2 * 2:2]
    slack = jnp.minimum(lengths[source_of] - 1, limit - lengths[sink]) // 2
    slack = jnp.where((source_of == sequence[0]) | (sink == sequence[0]) | (lengths[sink] == 0), 0, jnp.maximum(slack, 0))
    passed = jax.random.randint(jax.random.fold_in(own, 4), (number_of // 2,), 0, 1 << 20) % (slack + 1)
    lengths = lengths.at[source_of].add(-passed).at[sink].add(passed)
    members = jnp.searchsorted(jnp.cumsum(lengths), jnp.arange(rows * top), side="right").astype(jnp.int32)
    grid = members.reshape(top, rows).T
    grid = grid[jax.random.permutation(jax.random.fold_in(own, 1), rows)]
    turn = jax.random.randint(jax.random.fold_in(own, 2), (rows, 1), 0, top)
    return jnp.take_along_axis(grid, (jnp.arange(top)[None, :] + turn) % top, axis=1)


def shares(count, total, reach, lean, full):
    portions = [(1 << 20) // math.isqrt(rank ** lean) + 1 for rank in range(1, count + 1)]
    largest = reach if full else min(reach, max(-(-total // count), total * portions[0] // sum(portions)))
    least = 1 if total - largest >= count - 1 else 0
    holding, spare = [largest] + [least] * (count - 1), total - largest - least * (count - 1)
    while spare > 0:
        candidates = [i for i in range(1, count) if holding[i] < largest] or [i for i in range(1, count) if holding[i] < reach]
        whole, left = sum([portions[i] for i in candidates]), spare
        for i in candidates:
            extra = min(reach - holding[i], max(1, left * portions[i] // whole), spare)
            holding[i] = holding[i] + extra
            spare = spare - extra
    return np.array(holding)


def bell_draw(key, extent, scale, reach, pieces=(), held_as=jnp.bfloat16):
    drawn = jax.random.normal(key, extent, jnp.float32) * scale
    if len(pieces) > 0:
        drawn = block_levels(key, extent, pieces, -0.22, 0.18) * drawn
    return jnp.clip(drawn, min=-reach, max=reach).astype(held_as)


def setup_inputs(seed: int = 0, part: int = 0) -> dict:
    seeds = jax.random.split(jax.random.key(seed), 6)
    own_keys = jax.random.split(jax.random.fold_in(seeds[5], part), 6)
    rhs = bell_draw(own_keys[0], (3, NSN * SN, R), 1.0, 6.0, ((1, 16),), jnp.float32)
    diag_inv = bell_draw(seeds[1], (3, NSN * SN, SN), SN ** -0.5, 0.21875, ((1, 16),), jnp.float32)
    tiles = bell_draw(seeds[2], (2, NSN * 2, SN, SN), (2 * SN) ** -0.5, 0.15625, ((1, 16),), jnp.float32)
    dest_keys = jax.random.split(jax.random.fold_in(seeds[3], 1), 2 * NSN // NSN)
    dest_turns = jax.random.permutation(jax.random.fold_in(seeds[3], 3), 2 * NSN // NSN)
    dest = jax.vmap(lambda own, number: deal_out(jax.random.fold_in(seeds[3], 2), own, number, NSN, NSN, 2, CAP, 2))(dest_keys, dest_turns).reshape((2, NSN, 2))
    obs_weight = draw_obs_weight(jax.random.fold_in(seeds[5], 71), part)
    return {"rhs": rhs, "diag_inv": diag_inv, "tiles": tiles, "dest": dest, "obs_weight": obs_weight}


def solve_blocks(matrices, rights):
    def one_block(pair):
        return jnp.dot(pair[0], pair[1], precision=lax.Precision.HIGHEST, preferred_element_type=jnp.float32)
    return lax.map(one_block, (matrices, rights))


def reference(rhs, diag_inv, tiles, dest, obs_weight):
    blocks_rhs = rhs.reshape(3, NSN, SN, R)
    inverses = diag_inv.reshape(3, NSN, SN, SN)
    couplings = tiles.reshape(2, NSN, 2, SN, SN)
    solved = solve_blocks(inverses[0], blocks_rhs[0])
    levels = [solved]
    supernodes = jnp.arange(NSN, dtype=jnp.int32)
    for section in range(2):
        def tile_products(pair):
            return jnp.einsum('kab,bc->kac', pair[0], pair[1], precision=lax.Precision.HIGHEST, preferred_element_type=jnp.float32)
        products = lax.map(tile_products, (couplings[section], solved))
        matches = (dest[section][:, :, None] == supernodes[None, None, :]).astype(jnp.float32)
        update = jnp.einsum('jkd,jkac->dac', matches, products, precision=lax.Precision.HIGHEST)
        current = blocks_rhs[section + 1] - update
        solved = solve_blocks(inverses[section + 1], current)
        levels.append(solved)
    solution = jnp.stack(levels).reshape(3, NSN * SN, R)
    observed = jnp.dot(obs_weight, solution[2], precision=lax.Precision.HIGHEST, preferred_element_type=jnp.float32)
    return solution, observed
```

```python
import functools

import jax
import jax.numpy as jnp
from jax import lax
from jax.experimental import pallas as pl
from jax.experimental.pallas import tpu as pltpu
from jax.sharding import PartitionSpec as P

LANES = 128
SUB = 8
ANY = pl.BlockSpec(memory_space=pl.ANY)
VMEM = pl.BlockSpec(memory_space=pltpu.VMEM)
SMEM = pl.BlockSpec(memory_space=pltpu.SMEM)


def split(x):
    hi = x.astype(jnp.bfloat16)
    lo = (x - hi.astype(jnp.float32)).astype(jnp.bfloat16)
    return hi, lo


def split_cols(x):
    hi, lo = split(x)
    return jnp.concatenate([hi, lo], axis=1)


def dot3(a, both):
    width = both.shape[1] // 2
    hi, lo = split(a)
    wide = jnp.dot(hi, both, preferred_element_type=jnp.float32)
    narrow = jnp.dot(lo, both[:, :width], preferred_element_type=jnp.float32)
    return wide[:, :width] + (wide[:, width:] + narrow)


def left_product(vector, matrix, rows):
    columns = vector.T
    total = None
    for r in range(rows // LANES):
        block = matrix[pl.ds(r * LANES, LANES), :]
        term = jnp.sum(columns[:, r : r + 1] * block, axis=0, keepdims=True)
        total = term if total is None else total + term
    return total


def chunked(ref, buf, sem, parts):
    size = buf.shape[0] // parts
    copies = []
    for c in range(parts):
        at = pl.ds(c * size, size)
        copies.append(pltpu.make_async_copy(ref.at[at], buf.at[at], sem.at[c]))
    return copies


def products(tile_bufs, copies, both, pay_ref, group, parts):
    rows = tile_bufs[0].shape[0]
    seg = rows // group
    size = rows // parts
    for k, buf in enumerate(tile_bufs):
        for c in range(parts):
            copies[k][c].wait()
            out = dot3(buf[pl.ds(c * size, size), :], both)
            for s in range(size // seg):
                pay_ref[c * (size // seg) + s, pl.ds(k * seg, seg), :] = out[
                    s * seg : (s + 1) * seg
                ]


def first_kernel(
    group, parts, rhs, diag, tiles, weight, dest, sol, pay,
    b_buf, d_buf, l0_buf, l1_buf, v_buf, y_buf, small, d_sem, l0_sem, l1_sem, v_sem,
):
    rows = b_buf.shape[0]
    seg = rows // group
    d_copies = chunked(diag.at[0], d_buf, d_sem, parts)
    l_copies = [
        chunked(tiles.at[0, 0], l0_buf, l0_sem, parts),
        chunked(tiles.at[0, 1], l1_buf, l1_sem, parts),
    ]
    v_copies = chunked(diag.at[2], v_buf, v_sem, parts)
    b_copy = pltpu.make_async_copy(rhs.at[0], b_buf, small.at[0])
    b_copy.start()
    for copies in (d_copies, *l_copies, v_copies):
        for copy in copies:
            copy.start()
    b_copy.wait()
    both = split_cols(b_buf[...])
    size = rows // parts
    for c in range(parts):
        d_copies[c].wait()
        y_buf[pl.ds(c * size, size), :] = dot3(d_buf[pl.ds(c * size, size), :], both)
    y_copy = pltpu.make_async_copy(y_buf, sol.at[0], small.at[1])
    y_copy.start()
    products([l0_buf, l1_buf], l_copies, split_cols(y_buf[...]), pay, group, parts)
    for copy in v_copies:
        copy.wait()
    vector = left_product(weight[...], v_buf, rows)
    base = 2 * seg
    extra = pay.shape[1] - base
    lines = [jnp.full((1, LANES), dest[0, 0, k].astype(jnp.float32)) for k in range(2)]
    lines += [vector[:, r * LANES : (r + 1) * LANES] for r in range(rows // LANES)]
    if extra > len(lines):
        lines.append(jnp.zeros((extra - len(lines), LANES), jnp.float32))
    meta = jnp.concatenate(lines, axis=0)
    for s in range(group):
        pay[s, pl.ds(base, extra), :] = meta
    y_copy.wait()


def middle_kernel(
    group, parts, sol_in, arrived, rhs, diag, tiles, share, u_vec, dest, sol, pay,
    b_buf, d_buf, l0_buf, l1_buf, y_buf, small, d_sem, l0_sem, l1_sem,
):
    rows = b_buf.shape[0]
    seg = rows // group
    d_copies = chunked(diag.at[1], d_buf, d_sem, parts)
    l_copies = [
        chunked(tiles.at[1, 0], l0_buf, l0_sem, parts),
        chunked(tiles.at[1, 1], l1_buf, l1_sem, parts),
    ]
    b_copy = pltpu.make_async_copy(rhs.at[1], b_buf, small.at[0])
    b_copy.start()
    for copies in (d_copies, *l_copies):
        for copy in copies:
            copy.start()
    b_copy.wait()
    both = split_cols(b_buf[...] - (arrived[0] + arrived[1]))
    size = rows // parts
    for c in range(parts):
        d_copies[c].wait()
        y_buf[pl.ds(c * size, size), :] = dot3(d_buf[pl.ds(c * size, size), :], both)
    y_copy = pltpu.make_async_copy(y_buf, sol.at[1], small.at[1])
    y_copy.start()
    products([l0_buf, l1_buf], l_copies, split_cols(y_buf[...]), pay, group, parts)
    part = share[0:1, :] - left_product(u_vec[...], y_buf, rows)
    base = 2 * seg
    extra = pay.shape[1] - base
    lines = [jnp.full((1, LANES), dest[1, 0, k].astype(jnp.float32)) for k in range(2)]
    lines += [part, jnp.zeros((extra - 3, LANES), jnp.float32)]
    meta = jnp.concatenate(lines, axis=0)
    for s in range(group):
        pay[s, pl.ds(base, extra), :] = meta
    y_copy.wait()


def last_kernel(parts, sol_in, arrived, rhs, diag, sol, b_buf, d_buf, y_buf, small, d_sem):
    rows = b_buf.shape[0]
    d_copies = chunked(diag.at[2], d_buf, d_sem, parts)
    b_copy = pltpu.make_async_copy(rhs.at[2], b_buf, small.at[0])
    b_copy.start()
    for copy in d_copies:
        copy.start()
    b_copy.wait()
    both = split_cols(b_buf[...] - (arrived[0] + arrived[1]))
    size = rows // parts
    outs = []
    for c in range(parts):
        at = pl.ds(c * size, size)
        d_copies[c].wait()
        y_buf[at, :] = dot3(d_buf[at, :], both)
        outs.append(pltpu.make_async_copy(y_buf.at[at], sol.at[2, at], small.at[1 + c]))
        outs[c].start()
    for copy in outs:
        copy.wait()


def sum_kernel(seg, got, out, meta):
    group = got.shape[0]
    base = 2 * seg
    extra = got.shape[1] - base
    for q in range(group):
        meta[q] = got[q, pl.ds(base, extra), :]

    def one(i, carry):
        wanted = i.astype(jnp.float32)
        total = jnp.zeros((seg, LANES), jnp.float32)
        for q in range(group):
            for k in range(2):
                line = got[q, pl.ds(base + k, 1), :]
                mask = jnp.broadcast_to(line, (seg, LANES)) == wanted
                total += jnp.where(mask, got[q, pl.ds(k * seg, seg), :], 0.0)
        out[i] = total
        return carry

    lax.fori_loop(0, out.shape[0], one, 0)


def weights_kernel(group, parts, rhs, tiles, dest, half, mine, other, share, u_vec,
                   b_buf, l0_buf, l1_buf, small, l0_sem, l1_sem):
    rows = b_buf.shape[0]
    count = rows // LANES
    copies = [
        chunked(tiles.at[1, 0], l0_buf, l0_sem, parts),
        chunked(tiles.at[1, 1], l1_buf, l1_sem, parts),
    ]
    b_copy = pltpu.make_async_copy(rhs.at[2], b_buf, small.at[0])
    b_copy.start()
    for per_tile in copies:
        for copy in per_tile:
            copy.start()
    b_copy.wait()
    own = mine[half[1]]
    share[...] = jnp.broadcast_to(
        left_product(own[2 : 2 + count, :], b_buf, rows), share.shape
    )
    total = None
    for k, buf in enumerate((l0_buf, l1_buf)):
        target = dest[1, 0, k]
        place = lax.rem(target, group)
        same = (target >= group) == (half[0] > 0)
        vector = jnp.where(same, mine[place], other[place])
        for copy in copies[k]:
            copy.wait()
        term = left_product(vector[2 : 2 + count, :], buf, rows)
        total = term if total is None else total + term
    lines = [total[:, r * LANES : (r + 1) * LANES] for r in range(count)]
    pad = u_vec.shape[0] - count
    if pad:
        lines.append(jnp.zeros((pad, LANES), jnp.float32))
    u_vec[...] = jnp.concatenate(lines, axis=0)


def cost(flops, size):
    return pl.CostEstimate(flops=flops, bytes_accessed=size, transcendentals=0)


def body(rhs, diag_inv, tiles, dest, obs_weight):
    count = lax.axis_size("rows")
    group = count // 2
    levels, rows, width = rhs.shape
    seg = rows // group
    lines = rows // LANES
    extra = -(-(lines + 2) // SUB) * SUB
    parts = 4
    f32 = jnp.float32
    place = lax.axis_index("rows")
    halves = [list(range(group)), list(range(group, count))]
    across = [(i, (i + group) % count) for i in range(count)]
    half = jnp.stack([place // group, place % group]).astype(jnp.int32)

    block = pltpu.VMEM((rows, width), f32)
    square = pltpu.VMEM((rows, rows), f32)
    sems = pltpu.SemaphoreType.DMA((parts,))
    params = pltpu.CompilerParams(vmem_limit_bytes=48 << 20)
    sol_shape = jax.ShapeDtypeStruct(rhs.shape, f32)
    mat_flops = 2 * rows * rows * width
    mat_bytes = 4 * rows * rows

    def exchange(pay):
        return lax.all_to_all(
            pay, "rows", split_axis=0, concat_axis=0, tiled=True, axis_index_groups=halves
        )

    def spread(partial_sums):
        back = lax.all_to_all(partial_sums, "rows", split_axis=0, concat_axis=0, tiled=True)
        return back.reshape(2, rows, width)

    def summed(got, extra):
        return pl.pallas_call(
            functools.partial(sum_kernel, seg),
            out_shape=(
                jax.ShapeDtypeStruct((count, seg, width), f32),
                jax.ShapeDtypeStruct((group, extra, width), f32),
            ),
            in_specs=[VMEM],
            out_specs=(VMEM, VMEM),
            cost_estimate=cost(2 * count * rows * width, 4 * 4 * rows * width),
            name="sum_parts",
        )(got)

    pad = -(-lines // SUB) * SUB - lines
    weight = jnp.pad(obs_weight.reshape(lines, LANES), ((0, pad), (0, 0)))
    sol, pay = pl.pallas_call(
        functools.partial(first_kernel, group, parts),
        out_shape=(sol_shape, jax.ShapeDtypeStruct((group, 2 * seg + extra, width), f32)),
        in_specs=[ANY, ANY, ANY, VMEM, SMEM],
        out_specs=(ANY, VMEM),
        scratch_shapes=[
            block, square, square, square, square, block,
            pltpu.SemaphoreType.DMA((2,)), sems, sems, sems, sems,
        ],
        compiler_params=params,
        cost_estimate=cost(3 * mat_flops, 4 * mat_bytes),
        name="level_first",
    )(rhs, diag_inv, tiles, weight, dest)

    got = exchange(pay)
    sums, mine = summed(got, extra)
    other = lax.ppermute(mine, "rows", across)
    arrived = spread(sums)

    share, u_vec = pl.pallas_call(
        functools.partial(weights_kernel, group, parts),
        out_shape=(
            jax.ShapeDtypeStruct((SUB, width), f32),
            jax.ShapeDtypeStruct((lines + pad, LANES), f32),
        ),
        in_specs=[ANY, ANY, SMEM, SMEM, VMEM, VMEM],
        out_specs=(VMEM, VMEM),
        scratch_shapes=[block, square, square, pltpu.SemaphoreType.DMA((1,)), sems, sems],
        compiler_params=params,
        cost_estimate=cost(4 * rows * rows, 2 * mat_bytes),
        name="weights",
    )(rhs, tiles, dest, half, mine, other)

    sol, pay = pl.pallas_call(
        functools.partial(middle_kernel, group, parts),
        out_shape=(sol_shape, jax.ShapeDtypeStruct((group, 2 * seg + SUB, width), f32)),
        in_specs=[ANY, VMEM, ANY, ANY, ANY, VMEM, VMEM, SMEM],
        out_specs=(ANY, VMEM),
        scratch_shapes=[
            block, square, square, square, block,
            pltpu.SemaphoreType.DMA((2,)), sems, sems, sems,
        ],
        input_output_aliases={0: 0},
        compiler_params=params,
        cost_estimate=cost(3 * mat_flops, 3 * mat_bytes),
        name="level_middle",
    )(sol, arrived, rhs, diag_inv, tiles, share, u_vec, dest)

    got = exchange(pay)
    sums, mine = summed(got, SUB)
    near = jnp.sum(mine[:, 2, :], axis=0)
    far = lax.ppermute(near, "rows", across)
    observed = near + far
    arrived = spread(sums)

    sol = pl.pallas_call(
        functools.partial(last_kernel, parts),
        out_shape=sol_shape,
        in_specs=[ANY, VMEM, ANY, ANY],
        out_specs=ANY,
        scratch_shapes=[block, square, block, pltpu.SemaphoreType.DMA((1 + parts,)), sems],
        input_output_aliases={0: 0},
        compiler_params=params,
        cost_estimate=cost(mat_flops, mat_bytes),
        name="level_last",
    )(sol, arrived, rhs, diag_inv)
    return sol, observed


def solution(mesh):
    in_specs = (
        P(None, "rows", "parts"),
        P(None, "rows", None),
        P(None, "rows", None, None),
        P(None, "rows", None),
        P("rows"),
    )
    out_specs = (P(None, "rows", "parts"), P("parts"))
    return jax.shard_map(body, mesh=mesh, in_specs=in_specs, out_specs=out_specs, check_vma=False)
```

```python
import functools

import jax
import jax.numpy as jnp
from jax import lax
from jax.experimental import pallas as pl
from jax.experimental.pallas import tpu as pltpu
from jax.sharding import PartitionSpec as P

LANES = 128
SUB = 8
HBM = pl.BlockSpec(memory_space=pltpu.HBM)
ANY = pl.BlockSpec(memory_space=pl.ANY)
VMEM = pl.BlockSpec(memory_space=pltpu.VMEM)
SMEM = pl.BlockSpec(memory_space=pltpu.SMEM)


def split(x):
    hi = x.astype(jnp.bfloat16)
    lo = (x - hi.astype(jnp.float32)).astype(jnp.bfloat16)
    return hi, lo


def split_cols(x):
    hi, lo = split(x)
    return jnp.concatenate([hi, lo], axis=1)


def dot_terms(hi, lo, both):
    width = both.shape[1] // 2
    wide = jnp.dot(hi, both, preferred_element_type=jnp.float32)
    narrow = jnp.dot(lo, both[:, :width], preferred_element_type=jnp.float32)
    return wide[:, :width] + (wide[:, width:] + narrow)


def dot_late(hi, lo_ref, lo_copy, both):
    width = both.shape[1] // 2
    wide = jnp.dot(hi, both, preferred_element_type=jnp.float32)
    lo_copy.wait()
    narrow = jnp.dot(lo_ref[...], both[:, :width], preferred_element_type=jnp.float32)
    return wide[:, :width] + (wide[:, width:] + narrow)


def left_product(vector, matrix, rows):
    columns = vector.T
    total = None
    for r in range(rows // LANES):
        block = matrix[r * LANES : (r + 1) * LANES, :]
        term = jnp.sum(columns[:, r : r + 1] * block, axis=0, keepdims=True)
        total = term if total is None else total + term
    return total


def chunked(ref, buf, sem, parts):
    size = buf.shape[0] // parts
    copies = []
    for c in range(parts):
        at = pl.ds(c * size, size)
        copies.append(pltpu.make_async_copy(ref.at[at], buf.at[at], sem.at[c]))
    return copies


def put_slots(pay, k, seg, first, out):
    for s in range(out.shape[0] // seg):
        pay[first + s, pl.ds(k * seg, seg), :] = out[s * seg : (s + 1) * seg]


def first_kernel(
    group, parts, rhs, diag, tiles, weight, dest, sol, pay,
    b_buf, d_buf, l0_buf, l1_buf, v_buf, y_buf, w_buf, i_buf, small, d_sem, l0_sem, l1_sem, v_sem,
):
    rows = b_buf.shape[0]
    seg = rows // group
    size = rows // parts
    d_copies = chunked(diag.at[0], d_buf, d_sem, parts)
    l_copies = [
        chunked(tiles.at[0, 0], l0_buf, l0_sem, parts),
        chunked(tiles.at[0, 1], l1_buf, l1_sem, parts),
    ]
    v_copies = chunked(diag.at[2], v_buf, v_sem, parts)
    b_copy = pltpu.make_async_copy(rhs.at[0], b_buf, small.at[0])
    w_copy = pltpu.make_async_copy(weight, w_buf, small.at[2])
    i_copy = pltpu.make_async_copy(dest, i_buf, small.at[3])
    b_copy.start()
    for copies in (d_copies, *l_copies, v_copies):
        for copy in copies:
            copy.start()
    w_copy.start()
    i_copy.start()
    b_copy.wait()
    both = split_cols(b_buf[...])
    for c in range(parts):
        at = pl.ds(c * size, size)
        d_copies[c].wait()
        y_buf[at, :] = dot_terms(*split(d_buf[at, :]), both)
    y_copy = pltpu.make_async_copy(y_buf, sol.at[0], small.at[1])
    y_copy.start()
    both = split_cols(y_buf[...])
    for k, buf in enumerate((l0_buf, l1_buf)):
        for c in range(parts):
            l_copies[k][c].wait()
            out = dot_terms(*split(buf[pl.ds(c * size, size), :]), both)
            put_slots(pay, k, seg, c * (size // seg), out)
    w_copy.wait()
    i_copy.wait()
    for copy in v_copies:
        copy.wait()
    vector = left_product(w_buf[...], v_buf, rows)
    base = 2 * seg
    extra = pay.shape[1] - base
    lines = [jnp.full((1, LANES), i_buf[0, 0, k].astype(jnp.float32)) for k in range(2)]
    lines += [vector[:, r * LANES : (r + 1) * LANES] for r in range(rows // LANES)]
    if extra > len(lines):
        lines.append(jnp.zeros((extra - len(lines), LANES), jnp.float32))
    meta = jnp.concatenate(lines, axis=0)
    for s in range(group):
        pay[s, pl.ds(base, extra), :] = meta
    y_copy.wait()


def fold_kernel(group, rhs, diag, tiles, mine, half, m0_hi, m1_hi, m_lo, bias, share,
                d_buf, l_buf, t_buf, o_hi, o_lo, d_sem, l_sem, small, o_sem):
    rows = d_buf.shape[0]
    parts = d_sem.shape[0]
    size = rows // parts
    d_copies = chunked(diag.at[1], d_buf, d_sem, parts)
    l_copies = [chunked(tiles.at[1, k], l_buf.at[k], l_sem.at[k], parts) for k in range(2)]
    copies = [
        pltpu.make_async_copy(rhs.at[1], bias, small.at[0]),
        pltpu.make_async_copy(rhs.at[2], t_buf, small.at[1]),
    ]
    for copy in (*d_copies, *l_copies[0], *l_copies[1], *copies):
        copy.start()
    for copy in d_copies:
        copy.wait()
    d_hi, d_lo = split(d_buf[...])
    d_both = jnp.concatenate([d_hi, d_lo], axis=1)
    puts = []
    for k in range(2):
        for c in range(parts):
            at = pl.ds(c * size, size)
            l_copies[k][c].wait()
            out = dot_terms(*split(l_buf[k, at, :]), d_both)
            hi, lo = split(out)
            o_lo[k, at, :] = lo
            puts.append(
                pltpu.make_async_copy(o_lo.at[k, at], m_lo.at[k, at], o_sem.at[k, c])
            )
            puts[-1].start()
            if k == 0:
                m0_hi[at, :] = hi
            else:
                o_hi[at, :] = hi
                puts.append(pltpu.make_async_copy(o_hi.at[at], m1_hi.at[at], o_sem.at[2, c]))
                puts[-1].start()
    for copy in copies:
        copy.wait()
    share[...] = left_product(mine[half[1]][2 : 2 + rows // LANES, :], t_buf, rows)
    for copy in puts:
        copy.wait()


def middle_kernel(
    group, arrived, bias, m0_hi, m1_hi, m_lo, share, mine, other, dest, half,
    pay, rest, o_hi, o_lo, sem,
):
    rows = bias.shape[0]
    seg = rows // group
    count = rows // LANES
    lo_copies = [pltpu.make_async_copy(m_lo.at[k], o_lo.at[k], sem.at[k]) for k in range(2)]
    hi_copy = pltpu.make_async_copy(m1_hi, o_hi, sem.at[2])
    for copy in (lo_copies[0], hi_copy, lo_copies[1]):
        copy.start()
    rest[...] = bias[...] - (arrived[0] + arrived[1])
    both = split_cols(rest[...])
    part = share[...]
    for k, hi in enumerate((m0_hi, o_hi)):
        if k == 1:
            hi_copy.wait()
        out = dot_late(hi[...], o_lo.at[k], lo_copies[k], both)
        put_slots(pay, k, seg, 0, out)
        target = dest[1, 0, k]
        place = lax.rem(target, group)
        same = (target >= group) == (half[0] > 0)
        vector = jnp.where(same, mine[place], other[place])
        part = part - left_product(vector[2 : 2 + count, :], out, rows)
    base = 2 * seg
    extra = pay.shape[1] - base
    lines = [jnp.full((1, LANES), dest[1, 0, k].astype(jnp.float32)) for k in range(2)]
    lines += [part, jnp.zeros((extra - 3, LANES), jnp.float32)]
    meta = jnp.concatenate(lines, axis=0)
    for s in range(group):
        pay[s, pl.ds(base, extra), :] = meta


def window_kernel(parts, sol_in, rest, rhs, diag, sol, d_hi, d_lo, bias,
                  d_buf, y_buf, lo_buf, d_sem, small):
    rows = y_buf.shape[0]
    copies = [chunked(diag.at[1 + j], d_buf.at[j], d_sem.at[j], parts) for j in range(2)]
    b_copy = pltpu.make_async_copy(rhs.at[2], bias, small.at[0])
    for copy in (*copies[0], *copies[1], b_copy):
        copy.start()
    both = split_cols(rest[...])
    size = rows // parts
    for c in range(parts):
        at = pl.ds(c * size, size)
        copies[0][c].wait()
        y_buf[at, :] = dot_terms(*split(d_buf[0, at, :]), both)
    y_copy = pltpu.make_async_copy(y_buf, sol.at[1], small.at[1])
    y_copy.start()
    for c in range(parts):
        at = pl.ds(c * size, size)
        copies[1][c].wait()
        hi, lo = split(d_buf[1, at, :])
        d_hi[at, :] = hi
        lo_buf[at, :] = lo
    lo_copy = pltpu.make_async_copy(lo_buf, d_lo, small.at[2])
    lo_copy.start()
    lo_copy.wait()
    b_copy.wait()
    y_copy.wait()


def last_kernel(parts, sol_in, arrived, bias, d_hi, d_lo, near, far, sol, seen,
                y_buf, lo_buf, sem, lo_sem):
    rows = y_buf.shape[0]
    lo_copies = chunked(d_lo, lo_buf, lo_sem, parts)
    for copy in lo_copies:
        copy.start()
    both = split_cols(bias[...] - (arrived[0] + arrived[1]))
    size = rows // parts
    outs = []
    for c in range(parts):
        at = pl.ds(c * size, size)
        y_buf[at, :] = dot_late(d_hi[at, :], lo_buf.at[at], lo_copies[c], both)
        outs.append(pltpu.make_async_copy(y_buf.at[at], sol.at[2, at], sem.at[c]))
        outs[c].start()
    seen[...] = near[...] + far[...]
    for copy in outs:
        copy.wait()


def sum_kernel(seg, got, out, tail, where, sem):
    group = got.shape[0]
    base = 2 * seg
    copies = [
        pltpu.make_async_copy(got.at[q, pl.ds(base, 2)], where.at[q], sem.at[q])
        for q in range(group)
    ]
    for copy in copies:
        copy.start()
    out[...] = jnp.zeros_like(out)
    if tail.shape[0] == 1:
        total = got[0, base + 2 : base + 3, :]
        for q in range(1, group):
            total = total + got[q, base + 2 : base + 3, :]
        tail[...] = total
    else:
        for q in range(group):
            tail[q] = got[q, base:, :]
    for q in range(group):
        copies[q].wait()
        for k in range(2):
            target = where[q, k, 0].astype(jnp.int32)
            out[target] += got[q, pl.ds(k * seg, seg), :]


def cost(flops, size):
    return pl.CostEstimate(flops=flops, bytes_accessed=size, transcendentals=0)


def limit(mib):
    return pltpu.CompilerParams(vmem_limit_bytes=mib << 20)


def body(rhs, diag_inv, tiles, dest, obs_weight):
    count = lax.axis_size("rows")
    group = count // 2
    levels, rows, width = rhs.shape
    seg = rows // group
    lines = rows // LANES
    extra = -(-(lines + 2) // SUB) * SUB
    parts = 2
    f32 = jnp.float32
    place = lax.axis_index("rows")
    halves = [list(range(group)), list(range(group, count))]
    across = [(i, (i + group) % count) for i in range(count)]
    half = jnp.stack([place // group, place % group]).astype(jnp.int32)

    def stay(x):
        return pltpu.with_memory_space_constraint(x, pltpu.HBM)

    block = pltpu.VMEM((rows, width), f32)
    square = pltpu.VMEM((rows, rows), f32)
    sems = pltpu.SemaphoreType.DMA((parts,))
    sol_shape = jax.ShapeDtypeStruct(rhs.shape, f32)
    term = jax.ShapeDtypeStruct((rows, rows), jnp.bfloat16)
    flat = jax.ShapeDtypeStruct((rows, width), f32)
    line = jax.ShapeDtypeStruct((1, width), f32)
    mat_flops = 2 * rows * rows * width
    mat_bytes = 4 * rows * rows

    def exchange(pay):
        return lax.all_to_all(
            pay, "rows", split_axis=0, concat_axis=0, tiled=True, axis_index_groups=halves
        )

    def spread(partial_sums):
        back = lax.all_to_all(partial_sums, "rows", split_axis=0, concat_axis=0, tiled=True)
        return back.reshape(2, rows, width)

    def summed(got, tail):
        return pl.pallas_call(
            functools.partial(sum_kernel, seg),
            out_shape=(
                jax.ShapeDtypeStruct((count, seg, width), f32),
                jax.ShapeDtypeStruct(tail, f32),
            ),
            in_specs=[VMEM],
            out_specs=(VMEM, VMEM),
            scratch_shapes=[
                pltpu.SMEM((group, 2, width), f32),
                pltpu.SemaphoreType.DMA((group,)),
            ],
            compiler_params=limit(6),
            cost_estimate=cost(2 * rows * width, 4 * 4 * rows * width),
            name="sum_parts",
        )(got)

    sol, pay = pl.pallas_call(
        functools.partial(first_kernel, group, parts),
        out_shape=(sol_shape, jax.ShapeDtypeStruct((group, 2 * seg + extra, width), f32)),
        in_specs=[HBM, HBM, HBM, HBM, HBM],
        out_specs=(HBM, VMEM),
        scratch_shapes=[
            block, square, square, square, square, block,
            pltpu.VMEM((lines, LANES), f32), pltpu.SMEM(dest.shape, jnp.int32),
            pltpu.SemaphoreType.DMA((4,)), sems, sems, sems, sems,
        ],
        compiler_params=limit(24),
        cost_estimate=cost(3 * mat_flops, 4 * mat_bytes),
        name="level_first",
    )(stay(rhs), stay(diag_inv), stay(tiles), stay(obs_weight.reshape(lines, LANES)), stay(dest))

    got = exchange(pay)
    sums, mine = summed(got, (group, extra, width))
    sums, diag_later, tiles_later, rhs_later = lax.optimization_barrier(
        (sums, diag_inv, tiles, rhs)
    )
    other = lax.ppermute(mine, "rows", across)
    arrived = spread(sums)
    m0_hi, m1_hi, m_lo, bias, share = pl.pallas_call(
        functools.partial(fold_kernel, group),
        out_shape=(term, term, jax.ShapeDtypeStruct((2, rows, rows), jnp.bfloat16), flat, line),
        in_specs=[HBM, HBM, HBM, VMEM, SMEM],
        out_specs=(VMEM, HBM, HBM, VMEM, VMEM),
        scratch_shapes=[
            square, pltpu.VMEM((2, rows, rows), f32), block,
            pltpu.VMEM((rows, rows), jnp.bfloat16), pltpu.VMEM((2, rows, rows), jnp.bfloat16),
            sems, pltpu.SemaphoreType.DMA((2, parts)), pltpu.SemaphoreType.DMA((2,)),
            pltpu.SemaphoreType.DMA((3, parts)),
        ],
        compiler_params=limit(40),
        cost_estimate=cost(6 * rows * mat_flops // width, 3 * mat_bytes),
        name="fold_levels",
    )(stay(rhs_later), stay(diag_later), stay(tiles_later), mine, half)

    pay, rest = pl.pallas_call(
        functools.partial(middle_kernel, group),
        out_shape=(jax.ShapeDtypeStruct((group, 2 * seg + SUB, width), f32), flat),
        in_specs=[VMEM, VMEM, VMEM, HBM, HBM, VMEM, VMEM, VMEM, SMEM, SMEM],
        out_specs=(VMEM, VMEM),
        scratch_shapes=[
            pltpu.VMEM((rows, rows), jnp.bfloat16), pltpu.VMEM((2, rows, rows), jnp.bfloat16),
            pltpu.SemaphoreType.DMA((3,)),
        ],
        compiler_params=limit(16),
        cost_estimate=cost(2 * mat_flops, 2 * mat_bytes),
        name="level_middle",
    )(arrived, bias, m0_hi, stay(m1_hi), stay(m_lo), share, mine, other, dest, half)

    pay, diag_later, rhs_later = lax.optimization_barrier((pay, diag_inv, rhs))
    got = exchange(pay)
    sums, near = summed(got, (1, width))
    far = lax.ppermute(near, "rows", across)
    arrived = spread(sums)
    sol, d_hi, d_lo, bias = pl.pallas_call(
        functools.partial(window_kernel, parts),
        out_shape=(sol_shape, term, term, flat),
        in_specs=[HBM, VMEM, HBM, HBM],
        out_specs=(HBM, VMEM, HBM, VMEM),
        scratch_shapes=[
            pltpu.VMEM((2, rows, rows), f32), block, pltpu.VMEM((rows, rows), jnp.bfloat16),
            pltpu.SemaphoreType.DMA((2, parts)), pltpu.SemaphoreType.DMA((3,)),
        ],
        input_output_aliases={0: 0},
        compiler_params=limit(32),
        cost_estimate=cost(mat_flops, 2 * mat_bytes),
        name="in_window",
    )(sol, rest, stay(rhs_later), stay(diag_later))

    sol, seen = pl.pallas_call(
        functools.partial(last_kernel, parts),
        out_shape=(sol_shape, jax.ShapeDtypeStruct((1, width), f32)),
        in_specs=[HBM, VMEM, VMEM, VMEM, HBM, VMEM, VMEM],
        out_specs=(HBM, VMEM),
        scratch_shapes=[
            block, pltpu.VMEM((rows, rows), jnp.bfloat16), pltpu.SemaphoreType.DMA((parts,)), sems,
        ],
        input_output_aliases={0: 0},
        compiler_params=limit(16),
        cost_estimate=cost(mat_flops, mat_bytes),
        name="level_last",
    )(sol, arrived, bias, d_hi, stay(d_lo), near, far)
    return sol, seen.reshape(width)


def solution(mesh):
    in_specs = (
        P(None, "rows", "parts"),
        P(None, "rows", None),
        P(None, "rows", None, None),
        P(None, "rows", None),
        P("rows"),
    )
    out_specs = (P(None, "rows", "parts"), P("parts"))
    return jax.shard_map(body, mesh=mesh, in_specs=in_specs, out_specs=out_specs, check_vma=False)
```

```python
import functools

import jax
import jax.numpy as jnp
from jax import lax
from jax.experimental import pallas as pl
from jax.experimental.pallas import tpu as pltpu
from jax.sharding import PartitionSpec as P

LANES = 128
SUB = 8
HBM = pl.BlockSpec(memory_space=pltpu.HBM)
ANY = pl.BlockSpec(memory_space=pl.ANY)
VMEM = pl.BlockSpec(memory_space=pltpu.VMEM)
SMEM = pl.BlockSpec(memory_space=pltpu.SMEM)


def split(x):
    hi = x.astype(jnp.bfloat16)
    lo = (x - hi.astype(jnp.float32)).astype(jnp.bfloat16)
    return hi, lo


def split_cols(x):
    hi, lo = split(x)
    return jnp.concatenate([hi, lo], axis=1)


def dot_terms(hi, lo, both):
    width = both.shape[1] // 2
    wide = jnp.dot(hi, both, preferred_element_type=jnp.float32)
    narrow = jnp.dot(lo, both[:, :width], preferred_element_type=jnp.float32)
    return wide[:, :width] + (wide[:, width:] + narrow)


def dot_late(hi, lo_ref, lo_copy, both):
    width = both.shape[1] // 2
    wide = jnp.dot(hi, both, preferred_element_type=jnp.float32)
    lo_copy.wait()
    narrow = jnp.dot(lo_ref[...], both[:, :width], preferred_element_type=jnp.float32)
    return wide[:, :width] + (wide[:, width:] + narrow)


def left_product(vector, matrix, rows):
    columns = vector.T
    total = None
    for r in range(rows // LANES):
        block = matrix[r * LANES : (r + 1) * LANES, :]
        term = jnp.sum(columns[:, r : r + 1] * block, axis=0, keepdims=True)
        total = term if total is None else total + term
    return total


def chunked(ref, buf, sem, parts):
    size = buf.shape[0] // parts
    copies = []
    for c in range(parts):
        at = pl.ds(c * size, size)
        copies.append(pltpu.make_async_copy(ref.at[at], buf.at[at], sem.at[c]))
    return copies


def put_slots(pay, k, seg, first, out):
    for s in range(out.shape[0] // seg):
        pay[first + s, pl.ds(k * seg, seg), :] = out[s * seg : (s + 1) * seg]


def send_rows(src, dst, first, size, sem):
    at = pl.ds(first, size)
    copy = pltpu.make_async_copy(src.at[:, at], dst.at[:, at], sem)
    copy.start()
    return copy


def first_kernel(
    group, parts, rhs, diag, tiles, weight, dest, sol, out_pay,
    pay, b_buf, d_buf, l0_buf, l1_buf, v_buf, y_buf, w_buf, i_buf, p_sem, small, d_sem, l0_sem, l1_sem, v_sem,
):
    rows = b_buf.shape[0]
    seg = rows // group
    size = rows // parts
    d_copies = chunked(diag.at[0], d_buf, d_sem, parts)
    l_copies = [
        chunked(tiles.at[0, 0], l0_buf, l0_sem, parts),
        chunked(tiles.at[0, 1], l1_buf, l1_sem, parts),
    ]
    v_copies = chunked(diag.at[2], v_buf, v_sem, parts)
    b_copy = pltpu.make_async_copy(rhs.at[0], b_buf, small.at[0])
    w_copy = pltpu.make_async_copy(weight, w_buf, small.at[2])
    i_copy = pltpu.make_async_copy(dest, i_buf, small.at[3])
    b_copy.start()
    for copies in (d_copies, *l_copies, v_copies):
        for copy in copies:
            copy.start()
    w_copy.start()
    i_copy.start()
    b_copy.wait()
    both = split_cols(b_buf[...])
    for c in range(parts):
        at = pl.ds(c * size, size)
        d_copies[c].wait()
        y_buf[at, :] = dot_terms(*split(d_buf[at, :]), both)
    y_copy = pltpu.make_async_copy(y_buf, sol.at[0], small.at[1])
    y_copy.start()
    both = split_cols(y_buf[...])
    puts = []
    for k, buf in enumerate((l0_buf, l1_buf)):
        for c in range(parts):
            l_copies[k][c].wait()
            out = dot_terms(*split(buf[pl.ds(c * size, size), :]), both)
            put_slots(pay, k, seg, c * (size // seg), out)
        puts.append(send_rows(pay, out_pay, k * seg, seg, p_sem.at[k]))
    w_copy.wait()
    i_copy.wait()
    for copy in v_copies:
        copy.wait()
    vector = left_product(w_buf[...], v_buf, rows)
    base = 2 * seg
    extra = pay.shape[1] - base
    lines = [jnp.full((1, LANES), i_buf[0, 0, k].astype(jnp.float32)) for k in range(2)]
    lines += [vector[:, r * LANES : (r + 1) * LANES] for r in range(rows // LANES)]
    if extra > len(lines):
        lines.append(jnp.zeros((extra - len(lines), LANES), jnp.float32))
    meta = jnp.concatenate(lines, axis=0)
    for s in range(group):
        pay[s, pl.ds(base, extra), :] = meta
    puts.append(send_rows(pay, out_pay, base, extra, p_sem.at[2]))
    y_copy.wait()
    for copy in puts:
        copy.wait()


def fold_out_kernel(k, diag, tiles, out_hi, out_lo, hi_buf, lo_buf, o_sem, *refs):
    fold_kernel(k, diag, tiles, hi_buf, lo_buf, *refs)
    copies = [
        pltpu.make_async_copy(hi_buf, out_hi, o_sem.at[0]),
        pltpu.make_async_copy(lo_buf, out_lo, o_sem.at[1]),
    ]
    for copy in copies:
        copy.start()
    for copy in copies:
        copy.wait()


def fold_kernel(k, diag, tiles, m_hi, m_lo, d_buf, l_buf, d_sem, l_sem):
    rows = d_buf.shape[0]
    parts = d_sem.shape[0]
    size = rows // parts
    d_copies = chunked(diag.at[1], d_buf, d_sem, parts)
    l_copies = chunked(tiles.at[1, k], l_buf, l_sem, parts)
    for copy in (*d_copies, *l_copies):
        copy.start()
    for copy in d_copies:
        copy.wait()
    both = split_cols(d_buf[...])
    for c in range(parts):
        at = pl.ds(c * size, size)
        l_copies[c].wait()
        hi, lo = split(dot_terms(*split(l_buf[at, :]), both))
        m_hi[at, :] = hi
        m_lo[at, :] = lo


def share_kernel(rhs, mine, half, share, t_buf, sem):
    rows = t_buf.shape[0]
    copy = pltpu.make_async_copy(rhs.at[2], t_buf, sem)
    copy.start()
    copy.wait()
    share[...] = left_product(mine[half[1]][2 : 2 + rows // LANES, :], t_buf, rows)


def middle_kernel(
    group, arrived, rhs, m1_hi, m1_lo, m0_hi, m0_lo, share, mine, other, dest, half,
    out_pay, out_rest, pay, rest, bias, o_hi, o_lo, v_buf, sem, v_sem, p_sem,
):
    rows = bias.shape[0]
    seg = rows // group
    count = rows // LANES
    bias_copy = pltpu.make_async_copy(rhs.at[1], bias, sem.at[2])
    bias_copy.start()
    hi_copy = pltpu.make_async_copy(m0_hi, o_hi, sem.at[0])
    lo_copy = pltpu.make_async_copy(m0_lo, o_lo, sem.at[1])
    hi_copy.start()
    lo_copy.start()
    picks = []
    for k in range(2):
        place = lax.rem(dest[1, 0, k], group)
        picks.append(pltpu.make_async_copy(mine.at[place], v_buf.at[k], v_sem.at[k]))
    for copy in picks:
        copy.start()
    bias_copy.wait()
    rest[...] = bias[...] - (arrived[0] + arrived[1])
    rest_copy = pltpu.make_async_copy(rest, out_rest, p_sem.at[3])
    rest_copy.start()
    both = split_cols(rest[...])
    part = share[...]
    puts = []
    for copy in picks:
        copy.wait()
    for k in (1, 0):
        if k == 1:
            out = dot_terms(m1_hi[...], m1_lo[...], both)
        else:
            hi_copy.wait()
            out = dot_late(o_hi[...], o_lo, lo_copy, both)
        put_slots(pay, k, seg, 0, out)
        puts.append(send_rows(pay, out_pay, k * seg, seg, p_sem.at[k]))
        same = (dest[1, 0, k] >= group) == (half[0] > 0)
        vector = jnp.where(same, v_buf[k], other[lax.rem(dest[1, 0, k], group)])
        part = part - left_product(vector[2 : 2 + count, :], out, rows)
    base = 2 * seg
    extra = pay.shape[1] - base
    lines = [jnp.full((1, LANES), dest[1, 0, k].astype(jnp.float32)) for k in range(2)]
    lines += [part, jnp.zeros((extra - 3, LANES), jnp.float32)]
    meta = jnp.concatenate(lines, axis=0)
    for s in range(group):
        pay[s, pl.ds(base, extra), :] = meta
    puts.append(send_rows(pay, out_pay, base, extra, p_sem.at[2]))
    for copy in (*puts, rest_copy):
        copy.wait()


def window_kernel(parts, sol_in, rest, diag, sol, d_hi, d_lo,
                  d_buf, y_buf, r_buf, d_sem, small, r_sem):
    rows = y_buf.shape[0]
    copies = [chunked(diag.at[1 + j], d_buf.at[j], d_sem.at[j], parts) for j in range(2)]
    r_copy = pltpu.make_async_copy(rest, r_buf, r_sem)
    for copy in (r_copy, *copies[0], *copies[1]):
        copy.start()
    r_copy.wait()
    both = split_cols(r_buf[...])
    size = rows // parts
    for c in range(parts):
        at = pl.ds(c * size, size)
        copies[0][c].wait()
        y_buf[at, :] = dot_terms(*split(d_buf[0, at, :]), both)
    y_copy = pltpu.make_async_copy(y_buf, sol.at[1], small)
    y_copy.start()
    for c in range(parts):
        at = pl.ds(c * size, size)
        copies[1][c].wait()
        hi, lo = split(d_buf[1, at, :])
        d_hi[at, :] = hi
        d_lo[at, :] = lo
    y_copy.wait()


def last_kernel(parts, sol_in, arrived, rhs, d_hi, d_lo, near, far, sol, seen, y_buf, bias, sem):
    rows = y_buf.shape[0]
    bias_copy = pltpu.make_async_copy(rhs.at[2], bias, sem.at[parts])
    bias_copy.start()
    seen[...] = near[...] + far[...]
    bias_copy.wait()
    both = split_cols(bias[...] - (arrived[0] + arrived[1]))
    size = rows // parts
    outs = []
    for c in range(parts):
        at = pl.ds(c * size, size)
        y_buf[at, :] = dot_terms(d_hi[at, :], d_lo[at, :], both)
        outs.append(pltpu.make_async_copy(y_buf.at[at], sol.at[2, at], sem.at[c]))
        outs[c].start()
    for copy in outs:
        copy.wait()


def sum_kernel(seg, got, whole, tail, out, where, sem, o_sem):
    group = got.shape[0]
    base = 2 * seg
    copies = [
        pltpu.make_async_copy(got.at[q, pl.ds(base, 2)], where.at[q], sem.at[q])
        for q in range(group)
    ]
    for copy in copies:
        copy.start()
    out[...] = jnp.zeros_like(out)
    if tail.shape[0] == 1:
        total = got[0, base + 2 : base + 3, :]
        for q in range(1, group):
            total = total + got[q, base + 2 : base + 3, :]
        tail[...] = total
    else:
        for q in range(group):
            tail[q] = got[q, base:, :]
    for q in range(group):
        copies[q].wait()
        for k in range(2):
            target = where[q, k, 0].astype(jnp.int32)
            out[target] += got[q, pl.ds(k * seg, seg), :]
    copy = pltpu.make_async_copy(out, whole, o_sem)
    copy.start()
    copy.wait()


def cost(flops, size):
    return pl.CostEstimate(flops=flops, bytes_accessed=size, transcendentals=0)


def limit(mib):
    return pltpu.CompilerParams(vmem_limit_bytes=mib << 20)


def body(rhs, diag_inv, tiles, dest, obs_weight):
    count = lax.axis_size("rows")
    group = count // 2
    levels, rows, width = rhs.shape
    seg = rows // group
    lines = rows // LANES
    extra = -(-(lines + 2) // SUB) * SUB
    parts = 2
    f32 = jnp.float32
    place = lax.axis_index("rows")
    halves = [list(range(group)), list(range(group, count))]
    across = [(i, (i + group) % count) for i in range(count)]
    half = jnp.stack([place // group, place % group]).astype(jnp.int32)

    def stay(x):
        return pltpu.with_memory_space_constraint(x, pltpu.HBM)

    block = pltpu.VMEM((rows, width), f32)
    square = pltpu.VMEM((rows, rows), f32)
    sems = pltpu.SemaphoreType.DMA((parts,))
    sol_shape = jax.ShapeDtypeStruct(rhs.shape, f32)
    term = jax.ShapeDtypeStruct((rows, rows), jnp.bfloat16)
    flat = jax.ShapeDtypeStruct((rows, width), f32)
    line = jax.ShapeDtypeStruct((1, width), f32)
    mat_flops = 2 * rows * rows * width
    mat_bytes = 4 * rows * rows

    def exchange(pay):
        return lax.all_to_all(
            pay, "rows", split_axis=0, concat_axis=0, tiled=True, axis_index_groups=halves
        )

    def spread(partial_sums):
        back = lax.all_to_all(partial_sums, "rows", split_axis=0, concat_axis=0, tiled=True)
        return back.reshape(2, rows, width)

    def summed(got, tail):
        return pl.pallas_call(
            functools.partial(sum_kernel, seg),
            out_shape=(
                pltpu.HBM((count, seg, width), f32),
                jax.ShapeDtypeStruct(tail, f32),
            ),
            in_specs=[VMEM],
            out_specs=(HBM, VMEM),
            scratch_shapes=[
                pltpu.VMEM((count, seg, width), f32),
                pltpu.SMEM((group, 2, width), f32),
                pltpu.SemaphoreType.DMA((group,)),
                pltpu.SemaphoreType.DMA,
            ],
            compiler_params=limit(6),
            cost_estimate=cost(2 * rows * width, 4 * 4 * rows * width),
            name="sum_parts",
        )(got)

    sol, pay = pl.pallas_call(
        functools.partial(first_kernel, group, parts),
        out_shape=(pltpu.HBM(rhs.shape, f32), pltpu.HBM((group, 2 * seg + extra, width), f32)),
        in_specs=[HBM, HBM, HBM, HBM, HBM],
        out_specs=(HBM, HBM),
        scratch_shapes=[
            pltpu.VMEM((group, 2 * seg + extra, width), f32),
            block, square, square, square, square, block,
            pltpu.VMEM((lines, LANES), f32), pltpu.SMEM(dest.shape, jnp.int32),
            pltpu.SemaphoreType.DMA((3,)), pltpu.SemaphoreType.DMA((4,)), sems, sems, sems, sems,
        ],
        compiler_params=limit(24),
        cost_estimate=cost(3 * mat_flops, 4 * mat_bytes),
        name="level_first",
    )(stay(rhs), stay(diag_inv), stay(tiles), stay(obs_weight.reshape(lines, LANES)), stay(dest))

    def fold(k, diag_in, tiles_in, leave):
        buffer = pltpu.VMEM((rows, rows), jnp.bfloat16)
        far_term = pltpu.HBM((rows, rows), jnp.bfloat16)
        extra_scratch = [buffer, buffer, pltpu.SemaphoreType.DMA((2,))] if leave else []
        return pl.pallas_call(
            functools.partial(fold_out_kernel if leave else fold_kernel, k),
            out_shape=(far_term, far_term) if leave else (term, term),
            in_specs=[HBM, HBM],
            out_specs=(HBM, HBM) if leave else (VMEM, VMEM),
            scratch_shapes=[*extra_scratch, square, square, sems, sems],
            compiler_params=limit(32),
            cost_estimate=cost(3 * rows * mat_flops // width, 3 * mat_bytes),
            name="fold_levels",
        )(stay(diag_in), stay(tiles_in))

    pay, diag_later, tiles_later = lax.optimization_barrier((pay, diag_inv, tiles))
    got = exchange(pay)
    m0_hi, m0_lo = fold(0, diag_later, tiles_later, True)
    got, m0_hi, m0_lo = lax.optimization_barrier((got, m0_hi, m0_lo))
    sums, mine = summed(got, (group, extra, width))
    sums, diag_later, tiles_later, rhs_later = lax.optimization_barrier(
        (sums, diag_inv, tiles, rhs)
    )
    other = lax.ppermute(mine, "rows", across)
    arrived = spread(sums)
    m1_hi, m1_lo = fold(1, diag_later, tiles_later, False)
    share = pl.pallas_call(
        share_kernel,
        out_shape=line,
        in_specs=[HBM, VMEM, SMEM],
        out_specs=VMEM,
        scratch_shapes=[block, pltpu.SemaphoreType.DMA],
        compiler_params=limit(4),
        cost_estimate=cost(2 * rows * width, 4 * rows * width),
        name="share",
    )(stay(rhs_later), mine, half)

    pay, rest = pl.pallas_call(
        functools.partial(middle_kernel, group),
        out_shape=(pltpu.HBM((group, 2 * seg + SUB, width), f32), pltpu.HBM((rows, width), f32)),
        in_specs=[VMEM, HBM, VMEM, VMEM, HBM, HBM, VMEM, HBM, VMEM, SMEM, SMEM],
        out_specs=(HBM, HBM),
        scratch_shapes=[
            pltpu.VMEM((group, 2 * seg + SUB, width), f32), block,
            block, pltpu.VMEM((rows, rows), jnp.bfloat16), pltpu.VMEM((rows, rows), jnp.bfloat16),
            pltpu.VMEM((2, extra, LANES), f32),
            pltpu.SemaphoreType.DMA((3,)), pltpu.SemaphoreType.DMA((2,)),
            pltpu.SemaphoreType.DMA((4,)),
        ],
        compiler_params=limit(16),
        cost_estimate=cost(2 * mat_flops, 2 * mat_bytes),
        name="level_middle",
    )(
        arrived, stay(rhs), m1_hi, m1_lo, stay(m0_hi), stay(m0_lo), share, stay(mine), other,
        dest, half,
    )

    pay, diag_later = lax.optimization_barrier((pay, diag_inv))
    got = exchange(pay)
    sol, d_hi, d_lo = pl.pallas_call(
        functools.partial(window_kernel, parts),
        out_shape=(sol_shape, term, term),
        in_specs=[HBM, HBM, HBM],
        out_specs=(HBM, VMEM, VMEM),
        scratch_shapes=[
            pltpu.VMEM((2, rows, rows), f32), block, block,
            pltpu.SemaphoreType.DMA((2, parts)), pltpu.SemaphoreType.DMA,
            pltpu.SemaphoreType.DMA,
        ],
        input_output_aliases={0: 0},
        compiler_params=limit(32),
        cost_estimate=cost(mat_flops, 2 * mat_bytes),
        name="in_window",
    )(sol, stay(rest), stay(diag_later))
    got, d_hi, d_lo = lax.optimization_barrier((got, d_hi, d_lo))
    sums, near = summed(got, (1, width))
    far = lax.ppermute(near, "rows", across)
    arrived = spread(sums)

    sol, seen = pl.pallas_call(
        functools.partial(last_kernel, parts),
        out_shape=(sol_shape, jax.ShapeDtypeStruct((1, width), f32)),
        in_specs=[HBM, VMEM, HBM, VMEM, VMEM, VMEM, VMEM],
        out_specs=(HBM, VMEM),
        scratch_shapes=[block, block, pltpu.SemaphoreType.DMA((parts + 1,))],
        input_output_aliases={0: 0},
        compiler_params=limit(16),
        cost_estimate=cost(mat_flops, mat_bytes),
        name="level_last",
    )(sol, arrived, stay(rhs), d_hi, d_lo, near, far)
    return sol, seen.reshape(width)


def solution(mesh):
    in_specs = (
        P(None, "rows", "parts"),
        P(None, "rows", None),
        P(None, "rows", None, None),
        P(None, "rows", None),
        P("rows"),
    )
    out_specs = (P(None, "rows", "parts"), P("parts"))
    return jax.shard_map(body, mesh=mesh, in_specs=in_specs, out_specs=out_specs, check_vma=False)
```

```python
import functools

import jax
import jax.numpy as jnp
from jax import lax
from jax.experimental import pallas as pl
from jax.experimental.pallas import tpu as pltpu
from jax.sharding import PartitionSpec as P

LANES = 128
SUB = 8
HBM = pl.BlockSpec(memory_space=pltpu.HBM)
ANY = pl.BlockSpec(memory_space=pl.ANY)
VMEM = pl.BlockSpec(memory_space=pltpu.VMEM)
SMEM = pl.BlockSpec(memory_space=pltpu.SMEM)


def split(x):
    hi = x.astype(jnp.bfloat16)
    lo = (x - hi.astype(jnp.float32)).astype(jnp.bfloat16)
    return hi, lo


def split_cols(x):
    hi, lo = split(x)
    return jnp.concatenate([hi, lo], axis=1)


def dot_terms(hi, lo, both):
    width = both.shape[1] // 2
    wide = jnp.dot(hi, both, preferred_element_type=jnp.float32)
    narrow = jnp.dot(lo, both[:, :width], preferred_element_type=jnp.float32)
    return wide[:, :width] + (wide[:, width:] + narrow)


def left_product(vector, matrix, rows):
    columns = vector.T
    total = None
    for r in range(rows // LANES):
        block = matrix[r * LANES : (r + 1) * LANES, :]
        term = jnp.sum(columns[:, r : r + 1] * block, axis=0, keepdims=True)
        total = term if total is None else total + term
    return total


def chunked(ref, buf, sem, parts):
    size = buf.shape[0] // parts
    copies = []
    for c in range(parts):
        at = pl.ds(c * size, size)
        copies.append(pltpu.make_async_copy(ref.at[at], buf.at[at], sem.at[c]))
    return copies


def put_slots(pay, k, seg, first, out):
    for s in range(out.shape[0] // seg):
        pay[first + s, pl.ds(k * seg, seg), :] = out[s * seg : (s + 1) * seg]


def send_slots(pay, outs, place, sem):
    copies = []
    for r, out in enumerate(outs):
        copies.append(pltpu.make_async_copy(pay.at[place ^ r], out, sem.at[r]))
        copies[r].start()
    return copies


def tile_of(lines, extra):
    if extra > len(lines):
        lines = [*lines, jnp.zeros((extra - len(lines), LANES), jnp.float32)]
    return jnp.concatenate(lines, axis=0)


def named(dest, level):
    return [jnp.full((1, LANES), dest[level, 0, k].astype(jnp.float32)) for k in range(2)]


def first_kernel(group, parts, rhs, diag, tiles, dest, half, sol, *refs):
    outs, refs = refs[:group], refs[group:]
    pay, b_buf, d_buf, l0_buf, l1_buf, y_buf, i_buf, p_sem, small, d_sem, l0_sem, l1_sem = refs
    rows = b_buf.shape[0]
    seg = rows // group
    size = rows // parts
    d_copies = chunked(diag.at[0], d_buf, d_sem, parts)
    l_copies = [
        chunked(tiles.at[0, 0], l0_buf, l0_sem, parts),
        chunked(tiles.at[0, 1], l1_buf, l1_sem, parts),
    ]
    b_copy = pltpu.make_async_copy(rhs.at[0], b_buf, small.at[0])
    i_copy = pltpu.make_async_copy(dest, i_buf, small.at[2])
    b_copy.start()
    i_copy.start()
    for copies in (d_copies, *l_copies):
        for copy in copies:
            copy.start()
    i_copy.wait()
    base = 2 * seg
    extra = pay.shape[1] - base
    meta = tile_of(named(i_buf, 0), extra)
    for s in range(group):
        pay[s, pl.ds(base, extra), :] = meta
    b_copy.wait()
    both = split_cols(b_buf[...])
    for c in range(parts):
        at = pl.ds(c * size, size)
        d_copies[c].wait()
        y_buf[at, :] = dot_terms(*split(d_buf[at, :]), both)
    y_copy = pltpu.make_async_copy(y_buf, sol.at[0], small.at[1])
    y_copy.start()
    both = split_cols(y_buf[...])
    for k, buf in enumerate((l0_buf, l1_buf)):
        for c in range(parts):
            l_copies[k][c].wait()
            out = dot_terms(*split(buf[pl.ds(c * size, size), :]), both)
            put_slots(pay, k, seg, c * (size // seg), out)
    for copy in send_slots(pay, outs, half[1], p_sem):
        copy.wait()
    y_copy.wait()


def vector_kernel(rhs, diag, weight, v_tile, share, b_buf, v_buf, w_buf, sem):
    rows = b_buf.shape[0]
    copies = [
        pltpu.make_async_copy(weight, w_buf, sem.at[0]),
        pltpu.make_async_copy(rhs.at[2], b_buf, sem.at[1]),
        pltpu.make_async_copy(diag.at[2], v_buf, sem.at[2]),
    ]
    for copy in copies:
        copy.start()
    for copy in copies:
        copy.wait()
    vector = left_product(w_buf[...], v_buf, rows)
    count = rows // LANES
    lines = [vector[:, r * LANES : (r + 1) * LANES] for r in range(count)]
    v_tile[...] = tile_of(lines, v_tile.shape[0])
    share[...] = left_product(v_tile[0:count, :], b_buf, rows)


def fold_kernel(k, diag, tiles, m_hi, m_lo, d_buf, l_buf, d_sem, l_sem):
    rows = d_buf.shape[0]
    parts = d_sem.shape[0]
    size = rows // parts
    d_copies = chunked(diag.at[1], d_buf, d_sem, parts)
    l_copies = chunked(tiles.at[1, k], l_buf, l_sem, parts)
    for copy in (*d_copies, *l_copies):
        copy.start()
    for copy in d_copies:
        copy.wait()
    both = split_cols(d_buf[...])
    for c in range(parts):
        at = pl.ds(c * size, size)
        l_copies[c].wait()
        hi, lo = split(dot_terms(*split(l_buf[at, :]), both))
        m_hi[at, :] = hi
        m_lo[at, :] = lo


def sum_kernel(group, mode, half, *refs):
    refs = list(refs)
    v_tile = refs.pop(0) if mode == "first" else None
    got, refs = refs[:group], refs[group:]
    near = None if mode == "first" else refs.pop(0)
    chips = group
    outs, (out, where, tiles, sem, o_sem) = refs[:chips], refs[chips:]
    seg = out.shape[1]
    base = 2 * seg
    copies = [
        pltpu.make_async_copy(got[r].at[pl.ds(base, 2)], where.at[r], sem.at[r])
        for r in range(group)
    ]
    for copy in copies:
        copy.start()
    out[...] = jnp.zeros_like(out)
    if near is not None:
        for r in range(group):
            tiles[half[1] ^ r] = got[r][base : base + SUB, :]
        total = tiles[0, 2:3, :]
        for q in range(1, group):
            total = total + tiles[q, 2:3, :]
        near[...] = total
    puts = []
    if mode == "first":
        for r in range(chips):
            puts.append(
                pltpu.make_async_copy(
                    v_tile, outs[r].at[pl.ds(base, v_tile.shape[0])], o_sem.at[1, r]
                )
            )
            puts[-1].start()
    for r in range(group):
        copies[r].wait()
        for k in range(2):
            target = where[r, k, 0].astype(jnp.int32)
            out[target] += got[r][pl.ds(k * seg, seg), :]
    chip = half[2]
    for r in (*range(chips // 2, chips), *range(chips // 2)):
        for j in range(2):
            puts.append(
                pltpu.make_async_copy(
                    out.at[2 * (chip ^ r) + j], outs[r].at[pl.ds(j * seg, seg)],
                    o_sem.at[2 + j, r],
                )
            )
            puts[-1].start()
    for copy in puts:
        copy.wait()


def pair_kernel(chips, mode, half, *refs):
    got, refs = refs[:chips], refs[chips:]
    send, own = refs[:2]
    kept = refs[2] if mode == "first" else None
    lanes = chips // 2
    seg = own.shape[1]
    core = half[3]
    mine, theirs = core * seg, (1 - core) * seg
    for r in range(lanes):
        q = (half[2] % lanes) ^ r
        a, b = got[r], got[r + lanes]
        own[q] = a[pl.ds(mine, seg), :] + b[pl.ds(mine, seg), :]
        send[pl.ds(q * seg, seg), :] = a[pl.ds(theirs, seg), :] + b[pl.ds(theirs, seg), :]
    if mode == "first":
        extra = kept.shape[1]
        for r in range(chips):
            tile = got[r][2 * seg :, :]
            kept[half[2] ^ r] = tile
            send[pl.ds(lanes * seg + (half[2] ^ r) * extra, extra), :] = tile


def remainder(bias, own, other, core, rest):
    lanes, seg = own.shape[0], own.shape[1]
    for q in range(lanes):
        at = pl.ds((2 * q + core) * seg, seg)
        rest[at, :] = bias[at, :] - own[q]
        at = pl.ds((2 * q + 1 - core) * seg, seg)
        rest[at, :] = bias[at, :] - other[pl.ds(q * seg, seg), :]


def middle_kernel(group, parts, sol_in, own, other, rhs, diag, tiles, m_hi, m_lo, share, kept,
                  dest, half, sol, *refs):
    outs, refs = refs[:group], refs[group:]
    pay, rest, bias, d_buf, l_buf, y_buf, p_sem, small, d_sem, l_sem = refs
    rows = bias.shape[0]
    seg = rows // group
    size = rows // parts
    count = rows // LANES
    extra_v = kept.shape[1]
    offset = own.shape[0] * seg
    bias_copy = pltpu.make_async_copy(rhs.at[1], bias, small.at[0])
    d_copies = chunked(diag.at[1], d_buf, d_sem, parts)
    l_copies = chunked(tiles.at[1, 0], l_buf, l_sem, parts)
    for copy in (bias_copy, *d_copies, *l_copies):
        copy.start()
    vectors = []
    for k in range(2):
        target = dest[1, 0, k]
        here = kept[target // 2]
        there = other[pl.ds(offset + (target // 2) * extra_v, extra_v), :]
        vectors.append(jnp.where(target % 2 == half[3], here, there))
    part = share[...]
    bias_copy.wait()
    remainder(bias, own, other, half[3], rest)
    both = split_cols(rest[...])
    out = dot_terms(m_hi[...], m_lo[...], both)
    put_slots(pay, 1, seg, 0, out)
    part = part - left_product(vectors[1][0:count, :], out, rows)
    for c in range(parts):
        at = pl.ds(c * size, size)
        d_copies[c].wait()
        y_buf[at, :] = dot_terms(*split(d_buf[at, :]), both)
    y_copy = pltpu.make_async_copy(y_buf, sol.at[1], small.at[1])
    y_copy.start()
    both = split_cols(y_buf[...])
    for copy in l_copies:
        copy.wait()
    out = dot_terms(*split(l_buf[...]), both)
    put_slots(pay, 0, seg, 0, out)
    part = part - left_product(vectors[0][0:count, :], out, rows)
    base = 2 * seg
    extra = pay.shape[1] - base
    meta = tile_of([*named(dest, 1), part], extra)
    for s in range(group):
        pay[s, pl.ds(base, extra), :] = meta
    for copy in send_slots(pay, outs, half[1], p_sem):
        copy.wait()
    y_copy.wait()


def last_terms_kernel(parts, diag, d_hi, d_lo, d_buf, d_sem):
    rows = d_buf.shape[0]
    copies = chunked(diag.at[2], d_buf, d_sem, parts)
    for copy in copies:
        copy.start()
    size = rows // parts
    for c in range(parts):
        at = pl.ds(c * size, size)
        copies[c].wait()
        hi, lo = split(d_buf[at, :])
        d_hi[at, :] = hi
        d_lo[at, :] = lo


def last_kernel(parts, sol_in, own, other, rhs, d_hi, d_lo, near, far, half, sol, seen,
                y_buf, bias, rest, sem):
    rows = y_buf.shape[0]
    bias_copy = pltpu.make_async_copy(rhs.at[2], bias, sem.at[parts])
    bias_copy.start()
    seen[...] = near[...] + far[...]
    bias_copy.wait()
    remainder(bias, own, other, half[3], rest)
    both = split_cols(rest[...])
    size = rows // parts
    outs = []
    for c in range(parts):
        at = pl.ds(c * size, size)
        y_buf[at, :] = dot_terms(d_hi[at, :], d_lo[at, :], both)
        outs.append(pltpu.make_async_copy(y_buf.at[at], sol.at[2, at], sem.at[c]))
        outs[c].start()
    for copy in outs:
        copy.wait()


def cost(flops, size):
    return pl.CostEstimate(flops=flops, bytes_accessed=size, transcendentals=0)


def limit(mib):
    return pltpu.CompilerParams(vmem_limit_bytes=mib << 20)


def stay(x):
    return pltpu.with_memory_space_constraint(x, pltpu.HBM)


def later(first, *others):
    tied = lax.optimization_barrier((tuple(first), tuple(others)))
    return list(tied[0]), tied[1]


def body(rhs, diag_inv, tiles, dest, obs_weight):
    count = lax.axis_size("rows")
    group = count // 2
    chips = count // 2
    levels, rows, width = rhs.shape
    seg = rows // group
    lines = rows // LANES
    extra = -(-lines // SUB) * SUB
    parts = 2
    f32 = jnp.float32
    place = lax.axis_index("rows")
    half = jnp.stack([place // group, place % group, place // 2, place % 2]).astype(jnp.int32)

    def shift(x, bits):
        return lax.ppermute(x, "rows", [(i, i ^ bits) for i in range(count)])

    block = pltpu.VMEM((rows, width), f32)
    square = pltpu.VMEM((rows, rows), f32)
    sems = pltpu.SemaphoreType.DMA((parts,))
    term = jax.ShapeDtypeStruct((rows, rows), jnp.bfloat16)
    line = jax.ShapeDtypeStruct((1, width), f32)
    slot = pltpu.HBM((2 * seg + SUB, width), f32)
    kept_slot = jax.ShapeDtypeStruct((2 * seg + SUB, width), f32)
    mat_flops = 2 * rows * rows * width
    mat_bytes = 4 * rows * rows

    def exchange(pays):
        order = [*range(2, group), 1]
        moved = {r: shift(pays[r], r) for r in order}
        return [pays[0], *(moved[r] for r in range(1, group))]

    def spread(sums):
        order = [*range(chips // 2, chips), *range(1, chips // 2)]
        moved = {r: shift(sums[r], 2 * r) for r in order}
        return [sums[0], *(moved[r] for r in range(1, chips))]

    def summed(got, v_tile):
        mode = "last" if v_tile is None else "first"
        tall = 2 * seg + (0 if v_tile is None else extra)
        shapes = [jax.ShapeDtypeStruct((tall, width), f32)]
        shapes += [pltpu.HBM((tall, width), f32)] * (chips - 1)
        specs = [VMEM, *[HBM] * (chips - 1)]
        given, given_specs = list(got), [VMEM] * group
        if v_tile is None:
            shapes, specs = [line, *shapes], [VMEM, *specs]
        else:
            given, given_specs = [v_tile, *given], [VMEM, *given_specs]
        return pl.pallas_call(
            functools.partial(sum_kernel, group, mode),
            out_shape=tuple(shapes),
            in_specs=[SMEM, *given_specs],
            out_specs=tuple(specs),
            scratch_shapes=[
                pltpu.VMEM((count, seg, width), f32),
                pltpu.SMEM((group, 2, width), f32),
                pltpu.VMEM((group, SUB, width), f32),
                pltpu.SemaphoreType.DMA((group,)),
                pltpu.SemaphoreType.DMA((4, chips)),
            ],
            compiler_params=limit(6),
            cost_estimate=cost(2 * rows * width, 4 * 4 * rows * width),
            name="sum_parts",
        )(half, *given)

    def paired(got, mode):
        lanes = chips // 2
        tall = lanes * seg + (chips * extra if mode == "first" else 0)
        shapes = [jax.ShapeDtypeStruct((tall, width), f32)]
        shapes.append(jax.ShapeDtypeStruct((lanes, seg, width), f32))
        if mode == "first":
            shapes.append(jax.ShapeDtypeStruct((chips, extra, width), f32))
        return pl.pallas_call(
            functools.partial(pair_kernel, chips, mode),
            out_shape=tuple(shapes),
            in_specs=[SMEM] + [VMEM] * chips,
            out_specs=(VMEM,) * len(shapes),
            compiler_params=limit(4),
            cost_estimate=cost(2 * rows * width, 4 * 3 * rows * width),
            name="pair_halves",
        )(half, *got)

    sol, *pays = pl.pallas_call(
        functools.partial(first_kernel, group, parts),
        out_shape=(pltpu.HBM(rhs.shape, f32), kept_slot, *[slot] * (group - 1)),
        in_specs=[HBM, HBM, HBM, HBM, SMEM],
        out_specs=(HBM, VMEM, *[HBM] * (group - 1)),
        scratch_shapes=[
            pltpu.VMEM((group, 2 * seg + SUB, width), f32),
            block, square, square, square, block, pltpu.SMEM(dest.shape, jnp.int32),
            pltpu.SemaphoreType.DMA((group,)), pltpu.SemaphoreType.DMA((3,)), sems, sems, sems,
        ],
        compiler_params=limit(24),
        cost_estimate=cost(3 * mat_flops, 3 * mat_bytes),
        name="level_first",
    )(stay(rhs), stay(diag_inv), stay(tiles), stay(dest), half)

    pays, (diag_later, rhs_later) = later(pays, diag_inv, rhs)
    got = exchange(pays)
    v_tile, share = pl.pallas_call(
        vector_kernel,
        out_shape=(jax.ShapeDtypeStruct((extra, width), f32), line),
        in_specs=[HBM, HBM, HBM],
        out_specs=(VMEM, VMEM),
        scratch_shapes=[
            block, square, pltpu.VMEM((lines, LANES), f32), pltpu.SemaphoreType.DMA((3,)),
        ],
        compiler_params=limit(8),
        cost_estimate=cost(4 * rows * rows, mat_bytes),
        name="vector",
    )(stay(rhs_later), stay(diag_later), stay(obs_weight.reshape(lines, LANES)))
    sums = summed(got, v_tile)

    sums, (diag_later, tiles_later) = later(sums, diag_inv, tiles)
    got = spread(sums)
    m_hi, m_lo = pl.pallas_call(
        functools.partial(fold_kernel, 1),
        out_shape=(term, term),
        in_specs=[HBM, HBM],
        out_specs=(VMEM, VMEM),
        scratch_shapes=[square, square, sems, sems],
        compiler_params=limit(32),
        cost_estimate=cost(3 * rows * mat_flops // width, 2 * mat_bytes),
        name="fold_levels",
    )(stay(diag_later), stay(tiles_later))
    got, (m_hi, m_lo) = later(got, m_hi, m_lo)
    send, own, kept = paired(got, "first")
    other = shift(send, 1)

    sol, *pays = pl.pallas_call(
        functools.partial(middle_kernel, group, parts),
        out_shape=(pltpu.HBM(rhs.shape, f32), kept_slot, *[slot] * (group - 1)),
        in_specs=[HBM, VMEM, VMEM, HBM, HBM, HBM, VMEM, VMEM, VMEM, VMEM, SMEM, SMEM],
        out_specs=(HBM, VMEM, *[HBM] * (group - 1)),
        scratch_shapes=[
            pltpu.VMEM((group, 2 * seg + SUB, width), f32),
            block, block, square, square, block,
            pltpu.SemaphoreType.DMA((group,)), pltpu.SemaphoreType.DMA((2,)), sems, sems,
        ],
        input_output_aliases={0: 0},
        compiler_params=limit(24),
        cost_estimate=cost(3 * mat_flops, 2 * mat_bytes),
        name="level_middle",
    )(sol, own, other, stay(rhs), stay(diag_inv), stay(tiles), m_hi, m_lo, share, kept, dest, half)

    pays, (diag_later,) = later(pays, diag_inv)
    got = exchange(pays)
    near, *sums = summed(got, None)
    sums, (diag_later,) = later(sums, diag_later)
    got = spread(sums)
    far = shift(near, group)
    d_hi, d_lo = pl.pallas_call(
        functools.partial(last_terms_kernel, parts),
        out_shape=(term, term),
        in_specs=[HBM],
        out_specs=(VMEM, VMEM),
        scratch_shapes=[square, sems],
        compiler_params=limit(12),
        cost_estimate=cost(rows * rows, 2 * mat_bytes),
        name="last_terms",
    )(stay(diag_later))
    got, (d_hi, d_lo, far) = later(got, d_hi, d_lo, far)
    send, own = paired(got, "last")
    other = shift(send, 1)

    sol, seen = pl.pallas_call(
        functools.partial(last_kernel, parts),
        out_shape=(pltpu.HBM(rhs.shape, f32), line),
        in_specs=[HBM, VMEM, VMEM, HBM, VMEM, VMEM, VMEM, VMEM, SMEM],
        out_specs=(HBM, VMEM),
        scratch_shapes=[block, block, block, pltpu.SemaphoreType.DMA((parts + 1,))],
        input_output_aliases={0: 0},
        compiler_params=limit(16),
        cost_estimate=cost(mat_flops, mat_bytes),
        name="level_last",
    )(sol, own, other, stay(rhs), d_hi, d_lo, near, far, half)
    return sol, seen.reshape(width)


def solution(mesh):
    in_specs = (
        P(None, "rows", "parts"),
        P(None, "rows", None),
        P(None, "rows", None, None),
        P(None, "rows", None),
        P("rows"),
    )
    out_specs = (P(None, "rows", "parts"), P("parts"))
    return jax.shard_map(body, mesh=mesh, in_specs=in_specs, out_specs=out_specs, check_vma=False)
```

```python
import functools

import jax
import jax.numpy as jnp
from jax import lax
from jax.experimental import pallas as pl
from jax.experimental.pallas import tpu as pltpu
from jax.sharding import PartitionSpec as P

LANES = 128
SUB = 8
HBM = pl.BlockSpec(memory_space=pltpu.HBM)
ANY = pl.BlockSpec(memory_space=pl.ANY)
VMEM = pl.BlockSpec(memory_space=pltpu.VMEM)
SMEM = pl.BlockSpec(memory_space=pltpu.SMEM)


def split(x):
    hi = x.astype(jnp.bfloat16)
    lo = (x - hi.astype(jnp.float32)).astype(jnp.bfloat16)
    return hi, lo


def split_cols(x):
    hi, lo = split(x)
    return jnp.concatenate([hi, lo], axis=1)


def dot_terms(hi, lo, both):
    width = both.shape[1] // 2
    wide = jnp.dot(hi, both, preferred_element_type=jnp.float32)
    narrow = jnp.dot(lo, both[:, :width], preferred_element_type=jnp.float32)
    return wide[:, :width] + (wide[:, width:] + narrow)


def left_product(vector, matrix, rows):
    columns = vector.T
    total = None
    for r in range(rows // LANES):
        block = matrix[r * LANES : (r + 1) * LANES, :]
        term = jnp.sum(columns[:, r : r + 1] * block, axis=0, keepdims=True)
        total = term if total is None else total + term
    return total


def chunked(ref, buf, sem, parts):
    size = buf.shape[0] // parts
    copies = []
    for c in range(parts):
        at = pl.ds(c * size, size)
        copies.append(pltpu.make_async_copy(ref.at[at], buf.at[at], sem.at[c]))
    return copies


def position(group):
    place = lax.axis_index("rows")
    return lax.rem(place, group), place // 2, lax.rem(place, 2)


def deal(product, k, outs, spot, seg):
    for r, out in enumerate(outs):
        at = pl.ds(pl.multiple_of((spot ^ r) * seg, SUB), seg)
        out[pl.ds(k * seg, seg), :] = product[at, :]


def tile_of(lines, extra):
    if extra > len(lines):
        lines = [*lines, jnp.zeros((extra - len(lines), LANES), jnp.float32)]
    return jnp.concatenate(lines, axis=0)


def named(dest, level):
    return [jnp.full((1, LANES), dest[level, 0, k].astype(jnp.float32)) for k in range(2)]


def first_kernel(group, parts, rhs, diag, tiles, dest, sol, *refs):
    outs, refs = refs[:group], refs[group:]
    b_buf, d_buf, l0_buf, l1_buf, y_buf, p_buf, i_buf, small, d_sem, l0_sem, l1_sem = refs
    rows = b_buf.shape[0]
    seg = rows // group
    size = rows // parts
    spot, _, _ = position(group)
    d_copies = chunked(diag.at[0], d_buf, d_sem, parts)
    l_copies = [
        chunked(tiles.at[0, 0], l0_buf, l0_sem, parts),
        chunked(tiles.at[0, 1], l1_buf, l1_sem, parts),
    ]
    b_copy = pltpu.make_async_copy(rhs.at[0], b_buf, small.at[0])
    i_copy = pltpu.make_async_copy(dest, i_buf, small.at[2])
    b_copy.start()
    i_copy.start()
    for copies in (d_copies, *l_copies):
        for copy in copies:
            copy.start()
    b_copy.wait()
    both = split_cols(b_buf[...])
    for c in range(parts):
        at = pl.ds(c * size, size)
        d_copies[c].wait()
        y_buf[at, :] = dot_terms(*split(d_buf[at, :]), both)
    y_copy = pltpu.make_async_copy(y_buf, sol.at[0], small.at[1])
    y_copy.start()
    i_copy.wait()
    base = 2 * seg
    extra = outs[0].shape[0] - base
    meta = tile_of(named(i_buf, 0), extra)
    for out in outs:
        out[pl.ds(base, extra), :] = meta
    both = split_cols(y_buf[...])
    for k, buf in enumerate((l0_buf, l1_buf)):
        for c in range(parts):
            at = pl.ds(c * size, size)
            l_copies[k][c].wait()
            p_buf[k, at, :] = dot_terms(*split(buf[at, :]), both)
        deal(p_buf.at[k], k, outs, spot, seg)
    y_copy.wait()


def vector_kernel(rhs, diag, weight, v_tile, share, b_buf, v_buf, w_buf, sem):
    rows = b_buf.shape[0]
    copies = [
        pltpu.make_async_copy(weight, w_buf, sem.at[0]),
        pltpu.make_async_copy(rhs.at[2], b_buf, sem.at[1]),
        pltpu.make_async_copy(diag.at[2], v_buf, sem.at[2]),
    ]
    for copy in copies:
        copy.start()
    for copy in copies:
        copy.wait()
    vector = left_product(w_buf[...], v_buf, rows)
    count = rows // LANES
    lines = [vector[:, r * LANES : (r + 1) * LANES] for r in range(count)]
    v_tile[...] = tile_of(lines, v_tile.shape[0])
    share[...] = left_product(v_tile[0:count, :], b_buf, rows)


def fold_kernel(k, rhs, diag, tiles, m_hi, m_lo, bias, d_buf, l_buf, d_sem, l_sem, b_sem):
    rows = d_buf.shape[0]
    parts = d_sem.shape[0]
    size = rows // parts
    d_copies = chunked(diag.at[1], d_buf, d_sem, parts)
    l_copies = chunked(tiles.at[1, k], l_buf, l_sem, parts)
    b_copy = pltpu.make_async_copy(rhs.at[1], bias, b_sem)
    for copy in (*d_copies, *l_copies, b_copy):
        copy.start()
    for copy in d_copies:
        copy.wait()
    both = split_cols(d_buf[...])
    for c in range(parts):
        at = pl.ds(c * size, size)
        l_copies[c].wait()
        hi, lo = split(dot_terms(*split(l_buf[at, :]), both))
        m_hi[at, :] = hi
        m_lo[at, :] = lo
    b_copy.wait()


def sum_kernel(group, mode, *refs):
    refs = list(refs)
    v_tile = refs.pop(0) if mode == "first" else None
    got, refs = refs[:group], refs[group:]
    near = None if mode == "first" else refs.pop(0)
    chips = group
    outs, (out, where, tiles, sem) = refs[:chips], refs[chips:]
    seg = out.shape[1]
    base = 2 * seg
    spot, chip, _ = position(group)
    copies = [
        pltpu.make_async_copy(got[r].at[pl.ds(base, 2)], where.at[r], sem.at[r])
        for r in range(group)
    ]
    for copy in copies:
        copy.start()
    out[...] = jnp.zeros_like(out)
    if near is None:
        for r in range(chips):
            outs[r][pl.ds(base, v_tile.shape[0]), :] = v_tile[...]
    else:
        for r in range(group):
            tiles[spot ^ r] = got[r][base : base + SUB, :]
        total = tiles[0, 2:3, :]
        for q in range(1, group):
            total = total + tiles[q, 2:3, :]
        near[...] = total
        outs[chips // 2][pl.ds(base, SUB), :] = jnp.broadcast_to(total, (SUB, LANES))
    for copy in copies:
        copy.wait()
    for r in range(group):
        for k in range(2):
            target = where[r, k, 0].astype(jnp.int32)
            out[target] += got[r][pl.ds(k * seg, seg), :]
    for r in range(chips):
        for j in range(2):
            outs[r][pl.ds(j * seg, seg), :] = out[2 * (chip ^ r) + j]


def pair_kernel(chips, mode, *refs):
    near = None if mode == "first" else refs[0]
    refs = refs if mode == "first" else refs[1:]
    got, refs = refs[:chips], refs[chips:]
    send, own, more = refs
    lanes = chips // 2
    seg = own.shape[1]
    _, chip, core = position(chips)
    mine, theirs = pl.multiple_of(core * seg, SUB), pl.multiple_of((1 - core) * seg, SUB)
    for r in range(lanes):
        q = lax.rem(chip, lanes) ^ r
        a, b = got[r], got[r + lanes]
        own[q] = a[pl.ds(mine, seg), :] + b[pl.ds(mine, seg), :]
        at = pl.ds(pl.multiple_of(q * seg, SUB), seg)
        send[at, :] = a[pl.ds(theirs, seg), :] + b[pl.ds(theirs, seg), :]
    if mode == "first":
        extra = more.shape[1]
        for r in range(chips):
            tile = got[r][2 * seg :, :]
            more[chip ^ r] = tile
            at = pl.ds(pl.multiple_of(lanes * seg + (chip ^ r) * extra, SUB), extra)
            send[at, :] = tile
    else:
        more[...] = near[...] + got[lanes][2 * seg : 2 * seg + 1, :]


def remainder(bias, own, other, core, rest):
    lanes, seg = own.shape[0], own.shape[1]
    for q in range(lanes):
        at = pl.ds(pl.multiple_of((2 * q + core) * seg, SUB), seg)
        rest[at, :] = bias[at, :] - own[q]
        at = pl.ds(pl.multiple_of((2 * q + 1 - core) * seg, SUB), seg)
        rest[at, :] = bias[at, :] - other[pl.ds(q * seg, seg), :]


def middle_kernel(group, parts, sol_in, own, other, bias, diag, tiles, m_hi, m_lo, share, kept,
                  dest, sol, *refs):
    outs, refs = refs[:group], refs[group:]
    rest, d_buf, l_buf, y_buf, p_buf, i_buf, small, d_sem, l_sem = refs
    rows = bias.shape[0]
    seg = rows // group
    size = rows // parts
    count = rows // LANES
    extra_v = kept.shape[1]
    offset = own.shape[0] * seg
    spot, _, core = position(group)
    i_copy = pltpu.make_async_copy(dest, i_buf, small.at[0])
    d_copies = chunked(diag.at[1], d_buf, d_sem, parts)
    l_copies = chunked(tiles.at[1, 0], l_buf, l_sem, parts)
    for copy in (i_copy, *d_copies, *l_copies):
        copy.start()
    remainder(bias, own, other, core, rest)
    both = split_cols(rest[...])
    p_buf[1] = dot_terms(m_hi[...], m_lo[...], both)
    deal(p_buf.at[1], 1, outs, spot, seg)
    i_copy.wait()
    vectors = []
    for k in range(2):
        target = i_buf[1, 0, k]
        here = kept[target // 2]
        at = pl.ds(pl.multiple_of(offset + (target // 2) * extra_v, SUB), extra_v)
        vectors.append(jnp.where(lax.rem(target, 2) == core, here, other[at, :]))
    part = share[...] - left_product(vectors[1][0:count, :], p_buf.at[1], rows)
    for c in range(parts):
        at = pl.ds(c * size, size)
        d_copies[c].wait()
        y_buf[at, :] = dot_terms(*split(d_buf[at, :]), both)
    y_copy = pltpu.make_async_copy(y_buf, sol.at[1], small.at[1])
    y_copy.start()
    both = split_cols(y_buf[...])
    for copy in l_copies:
        copy.wait()
    p_buf[0] = dot_terms(*split(l_buf[...]), both)
    deal(p_buf.at[0], 0, outs, spot, seg)
    part = part - left_product(vectors[0][0:count, :], p_buf.at[0], rows)
    base = 2 * seg
    extra = outs[0].shape[0] - base
    meta = tile_of([*named(i_buf, 1), part], extra)
    for out in outs:
        out[pl.ds(base, extra), :] = meta
    y_copy.wait()


def last_terms_kernel(parts, rhs, diag, d_hi, d_lo, bias, d_buf, d_sem, b_sem):
    rows = d_buf.shape[0]
    copies = chunked(diag.at[2], d_buf, d_sem, parts)
    b_copy = pltpu.make_async_copy(rhs.at[2], bias, b_sem)
    for copy in (*copies, b_copy):
        copy.start()
    size = rows // parts
    for c in range(parts):
        at = pl.ds(c * size, size)
        copies[c].wait()
        hi, lo = split(d_buf[at, :])
        d_hi[at, :] = hi
        d_lo[at, :] = lo
    b_copy.wait()


def last_kernel(group, parts, sol_in, own, other, bias, d_hi, d_lo, sol, y_buf, rest, sem):
    rows = y_buf.shape[0]
    _, _, core = position(group)
    remainder(bias, own, other, core, rest)
    both = split_cols(rest[...])
    size = rows // parts
    outs = []
    for c in range(parts):
        at = pl.ds(c * size, size)
        y_buf[at, :] = dot_terms(d_hi[at, :], d_lo[at, :], both)
        outs.append(pltpu.make_async_copy(y_buf.at[at], sol.at[2, at], sem.at[c]))
        outs[c].start()
    for copy in outs:
        copy.wait()


def cost(flops, size):
    return pl.CostEstimate(flops=flops, bytes_accessed=size, transcendentals=0)


def limit(mib):
    return pltpu.CompilerParams(vmem_limit_bytes=mib << 20)


def stay(x):
    return pltpu.with_memory_space_constraint(x, pltpu.HBM)


def later(first, *others):
    tied = lax.optimization_barrier((tuple(first), tuple(others)))
    return list(tied[0]), tied[1]


def body(rhs, diag_inv, tiles, dest, obs_weight):
    count = lax.axis_size("rows")
    group = count // 2
    chips = count // 2
    levels, rows, width = rhs.shape
    seg = rows // group
    lines = rows // LANES
    extra = -(-lines // SUB) * SUB
    parts = 2
    f32 = jnp.float32
    def shift(x, bits):
        return lax.ppermute(x, "rows", [(i, i ^ bits) for i in range(count)])

    block = pltpu.VMEM((rows, width), f32)
    square = pltpu.VMEM((rows, rows), f32)
    sems = pltpu.SemaphoreType.DMA((parts,))
    term = jax.ShapeDtypeStruct((rows, rows), jnp.bfloat16)
    line = jax.ShapeDtypeStruct((1, width), f32)
    flat = jax.ShapeDtypeStruct((rows, width), f32)
    slot = jax.ShapeDtypeStruct((2 * seg + SUB, width), f32)
    mat_flops = 2 * rows * rows * width
    mat_bytes = 4 * rows * rows

    def exchange(pays):
        order = [*range(2, group), 1]
        moved = {r: shift(pays[r], r) for r in order}
        return [pays[0], *(moved[r] for r in range(1, group))]

    def spread(sums):
        order = [*range(chips // 2, chips), *range(1, chips // 2)]
        moved = {r: shift(sums[r], 2 * r) for r in order}
        return [sums[0], *(moved[r] for r in range(1, chips))]

    def summed(got, v_tile):
        mode = "last" if v_tile is None else "first"
        tall = [2 * seg + (0 if v_tile is None else extra)] * chips
        if v_tile is None:
            tall[chips // 2] += SUB
        shapes = [jax.ShapeDtypeStruct((t, width), f32) for t in tall]
        given = list(got)
        if v_tile is None:
            shapes = [line, *shapes]
        else:
            given = [v_tile, *given]
        return pl.pallas_call(
            functools.partial(sum_kernel, group, mode),
            out_shape=tuple(shapes),
            in_specs=[VMEM] * len(given),
            out_specs=(VMEM,) * len(shapes),
            scratch_shapes=[
                pltpu.VMEM((count, seg, width), f32),
                pltpu.SMEM((group, 2, width), f32),
                pltpu.VMEM((group, SUB, width), f32),
                pltpu.SemaphoreType.DMA((group,)),
            ],
            compiler_params=limit(6),
            cost_estimate=cost(2 * rows * width, 4 * 4 * rows * width),
            name="sum_parts",
        )(*given)

    def paired(got, near):
        mode = "first" if near is None else "last"
        lanes = chips // 2
        tall = lanes * seg + (chips * extra if near is None else 0)
        shapes = [jax.ShapeDtypeStruct((tall, width), f32)]
        shapes.append(jax.ShapeDtypeStruct((lanes, seg, width), f32))
        more = jax.ShapeDtypeStruct((chips, extra, width), f32)
        shapes.append(more if near is None else line)
        given = got if near is None else [near, *got]
        return pl.pallas_call(
            functools.partial(pair_kernel, chips, mode),
            out_shape=tuple(shapes),
            in_specs=[VMEM] * len(given),
            out_specs=(VMEM,) * len(shapes),
            compiler_params=limit(4),
            cost_estimate=cost(2 * rows * width, 4 * 3 * rows * width),
            name="pair_halves",
        )(*given)

    sol, *pays = pl.pallas_call(
        functools.partial(first_kernel, group, parts),
        out_shape=(pltpu.HBM(rhs.shape, f32), *[slot] * group),
        in_specs=[HBM, HBM, HBM, HBM],
        out_specs=(HBM, *[VMEM] * group),
        scratch_shapes=[
            block, square, square, square, block, pltpu.VMEM((2, rows, width), f32),
            pltpu.SMEM(dest.shape, jnp.int32),
            pltpu.SemaphoreType.DMA((3,)), sems, sems, sems,
        ],
        compiler_params=limit(24),
        cost_estimate=cost(3 * mat_flops, 3 * mat_bytes),
        name="level_first",
    )(stay(rhs), stay(diag_inv), stay(tiles), stay(dest))

    pays, (diag_later, rhs_later) = later(pays, diag_inv, rhs)
    got = exchange(pays)
    v_tile, share = pl.pallas_call(
        vector_kernel,
        out_shape=(jax.ShapeDtypeStruct((extra, width), f32), line),
        in_specs=[HBM, HBM, HBM],
        out_specs=(VMEM, VMEM),
        scratch_shapes=[
            block, square, pltpu.VMEM((lines, LANES), f32), pltpu.SemaphoreType.DMA((3,)),
        ],
        compiler_params=limit(8),
        cost_estimate=cost(4 * rows * rows, mat_bytes),
        name="vector",
    )(stay(rhs_later), stay(diag_later), stay(obs_weight.reshape(lines, LANES)))
    sums = summed(got, v_tile)

    sums, (diag_later, tiles_later, rhs_later) = later(sums, diag_inv, tiles, rhs)
    got = spread(sums)
    m_hi, m_lo, bias = pl.pallas_call(
        functools.partial(fold_kernel, 1),
        out_shape=(term, term, flat),
        in_specs=[HBM, HBM, HBM],
        out_specs=(VMEM, VMEM, VMEM),
        scratch_shapes=[square, square, sems, sems, pltpu.SemaphoreType.DMA],
        compiler_params=limit(32),
        cost_estimate=cost(3 * rows * mat_flops // width, 2 * mat_bytes),
        name="fold_levels",
    )(stay(rhs_later), stay(diag_later), stay(tiles_later))
    got, (m_hi, m_lo, bias) = later(got, m_hi, m_lo, bias)
    send, own, kept = paired(got, None)
    other = shift(send, 1)

    sol, *pays = pl.pallas_call(
        functools.partial(middle_kernel, group, parts),
        out_shape=(pltpu.HBM(rhs.shape, f32), *[slot] * group),
        in_specs=[HBM, VMEM, VMEM, VMEM, HBM, HBM, VMEM, VMEM, VMEM, VMEM, HBM],
        out_specs=(HBM, *[VMEM] * group),
        scratch_shapes=[
            block, square, square, block, pltpu.VMEM((2, rows, width), f32),
            pltpu.SMEM(dest.shape, jnp.int32), pltpu.SemaphoreType.DMA((2,)), sems, sems,
        ],
        input_output_aliases={0: 0},
        compiler_params=limit(24),
        cost_estimate=cost(3 * mat_flops, 2 * mat_bytes),
        name="level_middle",
    )(sol, own, other, bias, stay(diag_inv), stay(tiles), m_hi, m_lo, share, kept, stay(dest))

    pays, (diag_later,) = later(pays, diag_inv)
    got = exchange(pays)
    near, *sums = summed(got, None)
    sums, (diag_later, rhs_later) = later(sums, diag_later, rhs)
    got = spread(sums)
    d_hi, d_lo, bias = pl.pallas_call(
        functools.partial(last_terms_kernel, parts),
        out_shape=(term, term, flat),
        in_specs=[HBM, HBM],
        out_specs=(VMEM, VMEM, VMEM),
        scratch_shapes=[square, sems, pltpu.SemaphoreType.DMA],
        compiler_params=limit(12),
        cost_estimate=cost(rows * rows, 2 * mat_bytes),
        name="last_terms",
    )(stay(rhs_later), stay(diag_later))
    got, (d_hi, d_lo, bias) = later(got, d_hi, d_lo, bias)
    send, own, seen = paired(got, near)
    other = shift(send, 1)

    sol = pl.pallas_call(
        functools.partial(last_kernel, group, parts),
        out_shape=pltpu.HBM(rhs.shape, f32),
        in_specs=[HBM] + [VMEM] * 5,
        out_specs=HBM,
        scratch_shapes=[block, block, sems],
        input_output_aliases={0: 0},
        compiler_params=limit(8),
        cost_estimate=cost(mat_flops, mat_bytes),
        name="level_last",
    )(sol, own, other, bias, d_hi, d_lo)
    return sol, seen.reshape(width)


def solution(mesh):
    in_specs = (
        P(None, "rows", "parts"),
        P(None, "rows", None),
        P(None, "rows", None, None),
        P(None, "rows", None),
        P("rows"),
    )
    out_specs = (P(None, "rows", "parts"), P("parts"))
    return jax.shard_map(body, mesh=mesh, in_specs=in_specs, out_specs=out_specs, check_vma=False)
```

```python
import functools

import jax
import jax.numpy as jnp
from jax import lax
from jax.experimental import pallas as pl
from jax.experimental.pallas import tpu as pltpu
from jax.sharding import PartitionSpec as P

LANES = 128
SUB = 8
HBM = pl.BlockSpec(memory_space=pltpu.HBM)
ANY = pl.BlockSpec(memory_space=pl.ANY)
VMEM = pl.BlockSpec(memory_space=pltpu.VMEM)
SMEM = pl.BlockSpec(memory_space=pltpu.SMEM)


def split(x):
    hi = x.astype(jnp.bfloat16)
    lo = (x - hi.astype(jnp.float32)).astype(jnp.bfloat16)
    return hi, lo


def split_cols(x):
    hi, lo = split(x)
    return jnp.concatenate([hi, lo], axis=1)


def dot_terms(hi, lo, both):
    width = both.shape[1] // 2
    wide = jnp.dot(hi, both, preferred_element_type=jnp.float32)
    narrow = jnp.dot(lo, both[:, :width], preferred_element_type=jnp.float32)
    return wide[:, :width] + (wide[:, width:] + narrow)


def left_product(vector, matrix, rows):
    columns = vector.T
    total = None
    for r in range(rows // LANES):
        block = matrix[r * LANES : (r + 1) * LANES, :]
        term = jnp.sum(columns[:, r : r + 1] * block, axis=0, keepdims=True)
        total = term if total is None else total + term
    return total


def chunked(ref, buf, sem, parts):
    size = buf.shape[0] // parts
    copies = []
    for c in range(parts):
        at = pl.ds(c * size, size)
        copies.append(pltpu.make_async_copy(ref.at[at], buf.at[at], sem.at[c]))
    return copies


def position(group):
    place = lax.axis_index("rows")
    return lax.rem(place, group), place // 2, lax.rem(place, 2)


def deal(product, k, outs, spot, seg):
    for r, out in enumerate(outs):
        at = pl.ds(pl.multiple_of((spot ^ r) * seg, SUB), seg)
        out[pl.ds(k * seg, seg), :] = product[at, :]


def tile_of(lines, extra):
    if extra > len(lines):
        lines = [*lines, jnp.zeros((extra - len(lines), LANES), jnp.float32)]
    return jnp.concatenate(lines, axis=0)


def named(dest, level):
    return [jnp.full((1, LANES), dest[level, 0, k].astype(jnp.float32)) for k in range(2)]


def first_kernel(group, parts, rhs, diag, tiles, dest, sol, *refs):
    outs, refs = refs[:group], refs[group:]
    b_buf, d_buf, l0_buf, l1_buf, y_buf, p_buf, i_buf, small, d_sem, l0_sem, l1_sem = refs
    rows = b_buf.shape[0]
    seg = rows // group
    size = rows // parts
    spot, _, _ = position(group)
    d_copies = chunked(diag.at[0], d_buf, d_sem, parts)
    l_copies = [
        chunked(tiles.at[0, 0], l0_buf, l0_sem, parts),
        chunked(tiles.at[0, 1], l1_buf, l1_sem, parts),
    ]
    b_copy = pltpu.make_async_copy(rhs.at[0], b_buf, small.at[0])
    i_copy = pltpu.make_async_copy(dest, i_buf, small.at[2])
    b_copy.start()
    i_copy.start()
    for copies in (d_copies, *l_copies):
        for copy in copies:
            copy.start()
    b_copy.wait()
    both = split_cols(b_buf[...])
    for c in range(parts):
        at = pl.ds(c * size, size)
        d_copies[c].wait()
        y_buf[at, :] = dot_terms(*split(d_buf[at, :]), both)
    y_copy = pltpu.make_async_copy(y_buf, sol.at[0], small.at[1])
    y_copy.start()
    i_copy.wait()
    base = 2 * seg
    extra = outs[0].shape[0] - base
    meta = tile_of(named(i_buf, 0), extra)
    for out in outs:
        out[pl.ds(base, extra), :] = meta
    both = split_cols(y_buf[...])
    for k, buf in enumerate((l0_buf, l1_buf)):
        for c in range(parts):
            at = pl.ds(c * size, size)
            l_copies[k][c].wait()
            p_buf[k, at, :] = dot_terms(*split(buf[at, :]), both)
        deal(p_buf.at[k], k, outs, spot, seg)
    y_copy.wait()


def vector_kernel(rhs, diag, weight, v_tile, share, b_buf, v_buf, w_buf, sem):
    rows = b_buf.shape[0]
    copies = [
        pltpu.make_async_copy(weight, w_buf, sem.at[0]),
        pltpu.make_async_copy(rhs.at[2], b_buf, sem.at[1]),
        pltpu.make_async_copy(diag.at[2], v_buf, sem.at[2]),
    ]
    for copy in copies:
        copy.start()
    for copy in copies:
        copy.wait()
    vector = left_product(w_buf[...], v_buf, rows)
    count = rows // LANES
    lines = [vector[:, r * LANES : (r + 1) * LANES] for r in range(count)]
    v_tile[...] = tile_of(lines, v_tile.shape[0])
    share[...] = left_product(v_tile[0:count, :], b_buf, rows)


def fold_kernel(k, rhs, diag, tiles, m_hi, m_lo, bias, d_buf, l_buf, d_sem, l_sem, b_sem):
    rows = d_buf.shape[0]
    parts = d_sem.shape[0]
    size = rows // parts
    d_copies = chunked(diag.at[1], d_buf, d_sem, parts)
    l_copies = chunked(tiles.at[1, k], l_buf, l_sem, parts)
    b_copy = pltpu.make_async_copy(rhs.at[1], bias, b_sem)
    for copy in (*d_copies, *l_copies, b_copy):
        copy.start()
    for copy in d_copies:
        copy.wait()
    both = split_cols(d_buf[...])
    for c in range(parts):
        at = pl.ds(c * size, size)
        l_copies[c].wait()
        hi, lo = split(dot_terms(*split(l_buf[at, :]), both))
        m_hi[at, :] = hi
        m_lo[at, :] = lo
    b_copy.wait()


def sum_kernel(group, mode, *refs):
    refs = list(refs)
    v_tile = refs.pop(0) if mode == "first" else None
    order = [*near_order(group), 0]
    got, refs = [refs[order.index(r)] for r in range(group)], refs[group:]
    near = None if mode == "first" else refs.pop(0)
    chips = group
    outs, (out, where, tiles, sem) = refs[:chips], refs[chips:]
    seg = out.shape[1]
    base = 2 * seg
    spot, chip, _ = position(group)
    copies = [
        pltpu.make_async_copy(got[r].at[pl.ds(base, 2)], where.at[r], sem.at[r])
        for r in range(group)
    ]
    for copy in copies:
        copy.start()
    out[...] = jnp.zeros_like(out)
    if near is None:
        for r in range(chips):
            outs[r][pl.ds(base, v_tile.shape[0]), :] = v_tile[...]
    else:
        for r in range(group):
            tiles[spot ^ r] = got[r][base : base + SUB, :]
        total = tiles[0, 2:3, :]
        for q in range(1, group):
            total = total + tiles[q, 2:3, :]
        near[...] = total
        outs[chips - 1][pl.ds(base, SUB), :] = jnp.broadcast_to(total, (SUB, LANES))
    for copy in copies:
        copy.wait()
    for r in range(group):
        for k in range(2):
            target = where[r, k, 0].astype(jnp.int32)
            out[target] += got[r][pl.ds(k * seg, seg), :]
    for r in range(chips):
        for j in range(2):
            outs[r][pl.ds(j * seg, seg), :] = out[2 * (chip ^ r) + j]


def pair_kernel(chips, mode, *refs):
    near = None if mode == "first" else refs[0]
    refs = refs if mode == "first" else refs[1:]
    got, refs = refs[:chips][::-1], refs[chips:]
    send, own, more = refs
    lanes = chips // 2
    seg = own.shape[1]
    _, chip, core = position(chips)
    mine, theirs = pl.multiple_of(core * seg, SUB), pl.multiple_of((1 - core) * seg, SUB)
    for r in range(lanes):
        q = lax.rem(chip, lanes) ^ r
        a, b = got[r], got[r + lanes]
        own[q] = a[pl.ds(mine, seg), :] + b[pl.ds(mine, seg), :]
        at = pl.ds(pl.multiple_of(q * seg, SUB), seg)
        send[at, :] = a[pl.ds(theirs, seg), :] + b[pl.ds(theirs, seg), :]
    if mode == "first":
        extra = more.shape[1]
        for r in range(chips):
            tile = got[r][2 * seg :, :]
            more[chip ^ r] = tile
            at = pl.ds(pl.multiple_of(lanes * seg + (chip ^ r) * extra, SUB), extra)
            send[at, :] = tile
    else:
        more[...] = near[...] + got[chips - 1][2 * seg : 2 * seg + 1, :]


def remainder(bias, own, other, core, rest):
    lanes, seg = own.shape[0], own.shape[1]
    for q in range(lanes):
        at = pl.ds(pl.multiple_of((2 * q + core) * seg, SUB), seg)
        rest[at, :] = bias[at, :] - own[q]
        at = pl.ds(pl.multiple_of((2 * q + 1 - core) * seg, SUB), seg)
        rest[at, :] = bias[at, :] - other[pl.ds(q * seg, seg), :]


def middle_kernel(group, parts, sol_in, own, other, bias, diag, tiles, m_hi, m_lo, share, kept,
                  dest, sol, *refs):
    outs, refs = refs[:group], refs[group:]
    rest, d_buf, l_buf, y_buf, p_buf, i_buf, small, d_sem, l_sem = refs
    rows = bias.shape[0]
    seg = rows // group
    size = rows // parts
    count = rows // LANES
    extra_v = kept.shape[1]
    offset = own.shape[0] * seg
    spot, _, core = position(group)
    i_copy = pltpu.make_async_copy(dest, i_buf, small.at[0])
    d_copies = chunked(diag.at[1], d_buf, d_sem, parts)
    l_copies = chunked(tiles.at[1, 0], l_buf, l_sem, parts)
    for copy in (i_copy, *d_copies, *l_copies):
        copy.start()
    remainder(bias, own, other, core, rest)
    both = split_cols(rest[...])
    p_buf[1] = dot_terms(m_hi[...], m_lo[...], both)
    deal(p_buf.at[1], 1, outs, spot, seg)
    i_copy.wait()
    vectors = []
    for k in range(2):
        target = i_buf[1, 0, k]
        here = kept[target // 2]
        at = pl.ds(pl.multiple_of(offset + (target // 2) * extra_v, SUB), extra_v)
        vectors.append(jnp.where(lax.rem(target, 2) == core, here, other[at, :]))
    part = share[...] - left_product(vectors[1][0:count, :], p_buf.at[1], rows)
    for c in range(parts):
        at = pl.ds(c * size, size)
        d_copies[c].wait()
        y_buf[at, :] = dot_terms(*split(d_buf[at, :]), both)
    y_copy = pltpu.make_async_copy(y_buf, sol.at[1], small.at[1])
    y_copy.start()
    both = split_cols(y_buf[...])
    for copy in l_copies:
        copy.wait()
    p_buf[0] = dot_terms(*split(l_buf[...]), both)
    deal(p_buf.at[0], 0, outs, spot, seg)
    part = part - left_product(vectors[0][0:count, :], p_buf.at[0], rows)
    base = 2 * seg
    extra = outs[0].shape[0] - base
    meta = tile_of([*named(i_buf, 1), part], extra)
    for out in outs:
        out[pl.ds(base, extra), :] = meta
    y_copy.wait()


def last_terms_kernel(parts, rhs, diag, d_hi, d_lo, bias, d_buf, d_sem, b_sem):
    rows = d_buf.shape[0]
    copies = chunked(diag.at[2], d_buf, d_sem, parts)
    b_copy = pltpu.make_async_copy(rhs.at[2], bias, b_sem)
    for copy in (*copies, b_copy):
        copy.start()
    size = rows // parts
    for c in range(parts):
        at = pl.ds(c * size, size)
        copies[c].wait()
        hi, lo = split(d_buf[at, :])
        d_hi[at, :] = hi
        d_lo[at, :] = lo
    b_copy.wait()


def last_kernel(group, parts, sol_in, own, other, bias, d_hi, d_lo, sol, y_buf, rest, sem):
    rows = y_buf.shape[0]
    _, _, core = position(group)
    remainder(bias, own, other, core, rest)
    both = split_cols(rest[...])
    size = rows // parts
    outs = []
    for c in range(parts):
        at = pl.ds(c * size, size)
        y_buf[at, :] = dot_terms(d_hi[at, :], d_lo[at, :], both)
        outs.append(pltpu.make_async_copy(y_buf.at[at], sol.at[2, at], sem.at[c]))
        outs[c].start()
    for copy in outs:
        copy.wait()


def cost(flops, size):
    return pl.CostEstimate(flops=flops, bytes_accessed=size, transcendentals=0)


def limit(mib):
    return pltpu.CompilerParams(vmem_limit_bytes=mib << 20)


def stay(x):
    return pltpu.with_memory_space_constraint(x, pltpu.HBM)


def near_order(group):
    chips = (group - 2, *range(2, group - 2, 2))
    return [r + c for c in range(2) for r in chips] + [1]


def later(first, *others):
    tied = lax.optimization_barrier((tuple(first), tuple(others)))
    return list(tied[0]), tied[1]


def body(rhs, diag_inv, tiles, dest, obs_weight):
    count = lax.axis_size("rows")
    group = count // 2
    chips = count // 2
    levels, rows, width = rhs.shape
    seg = rows // group
    lines = rows // LANES
    extra = -(-lines // SUB) * SUB
    parts = 2
    f32 = jnp.float32
    def shift(x, bits):
        return lax.ppermute(x, "rows", [(i, i ^ bits) for i in range(count)])

    block = pltpu.VMEM((rows, width), f32)
    square = pltpu.VMEM((rows, rows), f32)
    sems = pltpu.SemaphoreType.DMA((parts,))
    term = jax.ShapeDtypeStruct((rows, rows), jnp.bfloat16)
    line = jax.ShapeDtypeStruct((1, width), f32)
    flat = jax.ShapeDtypeStruct((rows, width), f32)
    slot = jax.ShapeDtypeStruct((2 * seg + SUB, width), f32)
    mat_flops = 2 * rows * rows * width
    mat_bytes = 4 * rows * rows

    def exchange(pays):
        return [shift(pays[r], r) for r in near_order(group)] + [pays[0]]

    def spread(sums):
        return [shift(sums[r], 2 * r) for r in range(chips - 1, 0, -1)] + [sums[0]]

    def summed(got, v_tile):
        mode = "last" if v_tile is None else "first"
        tall = [2 * seg + (0 if v_tile is None else extra)] * chips
        if v_tile is None:
            tall[chips - 1] += SUB
        shapes = [jax.ShapeDtypeStruct((t, width), f32) for t in tall]
        given = list(got)
        if v_tile is None:
            shapes = [line, *shapes]
        else:
            given = [v_tile, *given]
        return pl.pallas_call(
            functools.partial(sum_kernel, group, mode),
            out_shape=tuple(shapes),
            in_specs=[VMEM] * len(given),
            out_specs=(VMEM,) * len(shapes),
            scratch_shapes=[
                pltpu.VMEM((count, seg, width), f32),
                pltpu.SMEM((group, 2, width), f32),
                pltpu.VMEM((group, SUB, width), f32),
                pltpu.SemaphoreType.DMA((group,)),
            ],
            compiler_params=limit(6),
            cost_estimate=cost(2 * rows * width, 4 * 4 * rows * width),
            name="sum_parts",
        )(*given)

    def paired(got, near):
        mode = "first" if near is None else "last"
        lanes = chips // 2
        tall = lanes * seg + (chips * extra if near is None else 0)
        shapes = [jax.ShapeDtypeStruct((tall, width), f32)]
        shapes.append(jax.ShapeDtypeStruct((lanes, seg, width), f32))
        more = jax.ShapeDtypeStruct((chips, extra, width), f32)
        shapes.append(more if near is None else line)
        given = got if near is None else [near, *got]
        return pl.pallas_call(
            functools.partial(pair_kernel, chips, mode),
            out_shape=tuple(shapes),
            in_specs=[VMEM] * len(given),
            out_specs=(VMEM,) * len(shapes),
            compiler_params=limit(4),
            cost_estimate=cost(2 * rows * width, 4 * 3 * rows * width),
            name="pair_halves",
        )(*given)

    sol, *pays = pl.pallas_call(
        functools.partial(first_kernel, group, parts),
        out_shape=(pltpu.HBM(rhs.shape, f32), *[slot] * group),
        in_specs=[HBM, HBM, HBM, HBM],
        out_specs=(HBM, *[VMEM] * group),
        scratch_shapes=[
            block, square, square, square, block, pltpu.VMEM((2, rows, width), f32),
            pltpu.SMEM(dest.shape, jnp.int32),
            pltpu.SemaphoreType.DMA((3,)), sems, sems, sems,
        ],
        compiler_params=limit(24),
        cost_estimate=cost(3 * mat_flops, 3 * mat_bytes),
        name="level_first",
    )(stay(rhs), stay(diag_inv), stay(tiles), stay(dest))

    pays, (diag_later, rhs_later) = later(pays, diag_inv, rhs)
    got = exchange(pays)
    v_tile, share = pl.pallas_call(
        vector_kernel,
        out_shape=(jax.ShapeDtypeStruct((extra, width), f32), line),
        in_specs=[HBM, HBM, HBM],
        out_specs=(VMEM, VMEM),
        scratch_shapes=[
            block, square, pltpu.VMEM((lines, LANES), f32), pltpu.SemaphoreType.DMA((3,)),
        ],
        compiler_params=limit(8),
        cost_estimate=cost(4 * rows * rows, mat_bytes),
        name="vector",
    )(stay(rhs_later), stay(diag_later), stay(obs_weight.reshape(lines, LANES)))
    sums = summed(got, v_tile)

    sums, (diag_later, tiles_later, rhs_later) = later(sums, diag_inv, tiles, rhs)
    got = spread(sums)
    m_hi, m_lo, bias = pl.pallas_call(
        functools.partial(fold_kernel, 1),
        out_shape=(term, term, flat),
        in_specs=[HBM, HBM, HBM],
        out_specs=(VMEM, VMEM, VMEM),
        scratch_shapes=[square, square, sems, sems, pltpu.SemaphoreType.DMA],
        compiler_params=limit(32),
        cost_estimate=cost(3 * rows * mat_flops // width, 2 * mat_bytes),
        name="fold_levels",
    )(stay(rhs_later), stay(diag_later), stay(tiles_later))
    got, (m_hi, m_lo, bias) = later(got, m_hi, m_lo, bias)
    send, own, kept = paired(got, None)
    other = shift(send, 1)

    sol, *pays = pl.pallas_call(
        functools.partial(middle_kernel, group, parts),
        out_shape=(pltpu.HBM(rhs.shape, f32), *[slot] * group),
        in_specs=[HBM, VMEM, VMEM, VMEM, HBM, HBM, VMEM, VMEM, VMEM, VMEM, HBM],
        out_specs=(HBM, *[VMEM] * group),
        scratch_shapes=[
            block, square, square, block, pltpu.VMEM((2, rows, width), f32),
            pltpu.SMEM(dest.shape, jnp.int32), pltpu.SemaphoreType.DMA((2,)), sems, sems,
        ],
        input_output_aliases={0: 0},
        compiler_params=limit(24),
        cost_estimate=cost(3 * mat_flops, 2 * mat_bytes),
        name="level_middle",
    )(sol, own, other, bias, stay(diag_inv), stay(tiles), m_hi, m_lo, share, kept, stay(dest))

    pays, (diag_later,) = later(pays, diag_inv)
    got = exchange(pays)
    near, *sums = summed(got, None)
    sums, (diag_later, rhs_later) = later(sums, diag_later, rhs)
    got = spread(sums)
    d_hi, d_lo, bias = pl.pallas_call(
        functools.partial(last_terms_kernel, parts),
        out_shape=(term, term, flat),
        in_specs=[HBM, HBM],
        out_specs=(VMEM, VMEM, VMEM),
        scratch_shapes=[square, sems, pltpu.SemaphoreType.DMA],
        compiler_params=limit(12),
        cost_estimate=cost(rows * rows, 2 * mat_bytes),
        name="last_terms",
    )(stay(rhs_later), stay(diag_later))
    got, (d_hi, d_lo, bias) = later(got, d_hi, d_lo, bias)
    send, own, seen = paired(got, near)
    other = shift(send, 1)

    sol = pl.pallas_call(
        functools.partial(last_kernel, group, parts),
        out_shape=pltpu.HBM(rhs.shape, f32),
        in_specs=[HBM] + [VMEM] * 5,
        out_specs=HBM,
        scratch_shapes=[block, block, sems],
        input_output_aliases={0: 0},
        compiler_params=limit(8),
        cost_estimate=cost(mat_flops, mat_bytes),
        name="level_last",
    )(sol, own, other, bias, d_hi, d_lo)
    return sol, seen.reshape(width)


def solution(mesh):
    in_specs = (
        P(None, "rows", "parts"),
        P(None, "rows", None),
        P(None, "rows", None, None),
        P(None, "rows", None),
        P("rows"),
    )
    out_specs = (P(None, "rows", "parts"), P("parts"))
    return jax.shard_map(body, mesh=mesh, in_specs=in_specs, out_specs=out_specs, check_vma=False)
```

```python
import functools

import jax
import jax.numpy as jnp
from jax import lax
from jax.experimental import pallas as pl
from jax.experimental.pallas import tpu as pltpu
from jax.sharding import PartitionSpec as P

LANES = 128
SUB = 8
HBM = pl.BlockSpec(memory_space=pltpu.HBM)
ANY = pl.BlockSpec(memory_space=pl.ANY)
VMEM = pl.BlockSpec(memory_space=pltpu.VMEM)
SMEM = pl.BlockSpec(memory_space=pltpu.SMEM)


def split(x):
    hi = x.astype(jnp.bfloat16)
    lo = (x - hi.astype(jnp.float32)).astype(jnp.bfloat16)
    return hi, lo


def split_cols(x):
    hi, lo = split(x)
    return jnp.concatenate([hi, lo], axis=1)


def dot_terms(hi, lo, both):
    width = both.shape[1] // 2
    wide = jnp.dot(hi, both, preferred_element_type=jnp.float32)
    narrow = jnp.dot(lo, both[:, :width], preferred_element_type=jnp.float32)
    return wide[:, :width] + (wide[:, width:] + narrow)


def left_product(vector, matrix, rows):
    columns = vector.T
    total = None
    for r in range(rows // LANES):
        block = matrix[r * LANES : (r + 1) * LANES, :]
        term = jnp.sum(columns[:, r : r + 1] * block, axis=0, keepdims=True)
        total = term if total is None else total + term
    return total


def chunked(ref, buf, sem, parts):
    size = buf.shape[0] // parts
    copies = []
    for c in range(parts):
        at = pl.ds(c * size, size)
        copies.append(pltpu.make_async_copy(ref.at[at], buf.at[at], sem.at[c]))
    return copies


def position(group):
    place = lax.axis_index("rows")
    return lax.rem(place, group), place // 2, lax.rem(place, 2)


def deal(product, k, outs, spot, seg):
    for r, out in enumerate(outs):
        at = pl.ds(pl.multiple_of((spot ^ r) * seg, SUB), seg)
        out[pl.ds(k * seg, seg), :] = product[at, :]


def tile_of(lines, extra):
    if extra > len(lines):
        lines = [*lines, jnp.zeros((extra - len(lines), LANES), jnp.float32)]
    return jnp.concatenate(lines, axis=0)


def named(dest, level):
    return [jnp.full((1, LANES), dest[level, 0, k].astype(jnp.float32)) for k in range(2)]


def first_kernel(group, parts, rhs, diag, tiles, dest, sol, *refs):
    outs, refs = refs[:group], refs[group:]
    b_buf, d_buf, l0_buf, l1_buf, y_buf, p_buf, i_buf, small, d_sem, l0_sem, l1_sem = refs
    rows = b_buf.shape[0]
    seg = rows // group
    size = rows // parts
    spot, _, _ = position(group)
    d_copies = chunked(diag.at[0], d_buf, d_sem, 2 * parts)
    l_copies = [
        chunked(tiles.at[0, 0], l0_buf, l0_sem, parts),
        chunked(tiles.at[0, 1], l1_buf, l1_sem, parts),
    ]
    b_copy = pltpu.make_async_copy(rhs.at[0], b_buf, small.at[0])
    i_copy = pltpu.make_async_copy(dest, i_buf, small.at[2])
    b_copy.start()
    i_copy.start()
    for copies in (d_copies, *l_copies):
        for copy in copies:
            copy.start()
    b_copy.wait()
    both = split_cols(b_buf[...])
    for c in range(2 * parts):
        at = pl.ds(c * (size // 2), size // 2)
        d_copies[c].wait()
        y_buf[at, :] = dot_terms(*split(d_buf[at, :]), both)
    y_copy = pltpu.make_async_copy(y_buf, sol.at[0], small.at[1])
    y_copy.start()
    i_copy.wait()
    base = 2 * seg
    extra = outs[0].shape[0] - base
    meta = tile_of(named(i_buf, 0), extra)
    for out in outs:
        out[pl.ds(base, extra), :] = meta
    both = split_cols(y_buf[...])
    for k, buf in enumerate((l0_buf, l1_buf)):
        for c in range(parts):
            at = pl.ds(c * size, size)
            l_copies[k][c].wait()
            p_buf[k, at, :] = dot_terms(*split(buf[at, :]), both)
        deal(p_buf.at[k], k, outs, spot, seg)
    y_copy.wait()


def vector_kernel(rhs, diag, weight, v_tile, share, b_buf, v_buf, w_buf, sem):
    rows = b_buf.shape[0]
    copies = [
        pltpu.make_async_copy(weight, w_buf, sem.at[0]),
        pltpu.make_async_copy(rhs.at[2], b_buf, sem.at[1]),
        pltpu.make_async_copy(diag.at[2], v_buf, sem.at[2]),
    ]
    for copy in copies:
        copy.start()
    for copy in copies:
        copy.wait()
    vector = left_product(w_buf[...], v_buf, rows)
    count = rows // LANES
    lines = [vector[:, r * LANES : (r + 1) * LANES] for r in range(count)]
    v_tile[...] = tile_of(lines, v_tile.shape[0])
    share[...] = left_product(v_tile[0:count, :], b_buf, rows)


def fold_kernel(k, rhs, diag, tiles, m_hi, m_lo, bias, d_buf, l_buf, d_sem, l_sem, b_sem):
    rows = d_buf.shape[0]
    parts = d_sem.shape[0]
    size = rows // parts
    d_copies = chunked(diag.at[1], d_buf, d_sem, parts)
    l_copies = chunked(tiles.at[1, k], l_buf, l_sem, parts)
    b_copy = pltpu.make_async_copy(rhs.at[1], bias, b_sem)
    for copy in (*d_copies, *l_copies, b_copy):
        copy.start()
    for copy in d_copies:
        copy.wait()
    both = split_cols(d_buf[...])
    for c in range(parts):
        at = pl.ds(c * size, size)
        l_copies[c].wait()
        hi, lo = split(dot_terms(*split(l_buf[at, :]), both))
        m_hi[at, :] = hi
        m_lo[at, :] = lo
    b_copy.wait()


def sum_kernel(group, mode, *refs):
    refs = list(refs)
    v_tile = refs.pop(0) if mode == "first" else None
    order = [*near_order(group), 0]
    got, refs = [refs[order.index(r)] for r in range(group)], refs[group:]
    near = None if mode == "first" else refs.pop(0)
    chips = group
    outs, (out, tiles) = refs[:chips], refs[chips:]
    seg = out.shape[1]
    base = 2 * seg
    spot, chip, _ = position(group)
    targets = []
    for r in range(group):
        rows = got[r][base : base + SUB, :]
        targets.append([rows[k, 0].astype(jnp.int32) for k in range(2)])
    out[...] = jnp.zeros_like(out)
    if near is None:
        for r in range(chips):
            outs[r][pl.ds(base, v_tile.shape[0]), :] = v_tile[...]
    else:
        for r in range(group):
            tiles[spot ^ r] = got[r][base : base + SUB, :]
        total = tiles[0, 2:3, :]
        for q in range(1, group):
            total = total + tiles[q, 2:3, :]
        near[...] = total
        outs[chips - 1][pl.ds(base, SUB), :] = jnp.broadcast_to(total, (SUB, LANES))
    for r in range(group):
        for k in range(2):
            out[targets[r][k]] += got[r][pl.ds(k * seg, seg), :]
    for r in range(chips):
        for j in range(2):
            outs[r][pl.ds(j * seg, seg), :] = out[2 * (chip ^ r) + j]


def pair_kernel(chips, mode, *refs):
    near = None if mode == "first" else refs[0]
    refs = refs if mode == "first" else refs[1:]
    got, refs = refs[:chips][::-1], refs[chips:]
    send, own, more = refs
    lanes = chips // 2
    seg = own.shape[1]
    _, chip, core = position(chips)
    mine, theirs = pl.multiple_of(core * seg, SUB), pl.multiple_of((1 - core) * seg, SUB)
    for r in range(lanes):
        q = lax.rem(chip, lanes) ^ r
        a, b = got[r], got[r + lanes]
        own[q] = a[pl.ds(mine, seg), :] + b[pl.ds(mine, seg), :]
        at = pl.ds(pl.multiple_of(q * seg, SUB), seg)
        send[at, :] = a[pl.ds(theirs, seg), :] + b[pl.ds(theirs, seg), :]
    if mode == "first":
        extra = more.shape[1]
        for r in range(chips):
            tile = got[r][2 * seg :, :]
            more[chip ^ r] = tile
            at = pl.ds(pl.multiple_of(lanes * seg + (chip ^ r) * extra, SUB), extra)
            send[at, :] = tile
    else:
        more[...] = near[...] + got[chips - 1][2 * seg : 2 * seg + 1, :]


def remainder(bias, own, other, core, rest):
    lanes, seg = own.shape[0], own.shape[1]
    for q in range(lanes):
        at = pl.ds(pl.multiple_of((2 * q + core) * seg, SUB), seg)
        rest[at, :] = bias[at, :] - own[q]
        at = pl.ds(pl.multiple_of((2 * q + 1 - core) * seg, SUB), seg)
        rest[at, :] = bias[at, :] - other[pl.ds(q * seg, seg), :]


def middle_kernel(group, parts, sol_in, own, other, bias, diag, tiles, m_hi, m_lo, share, kept,
                  dest, sol, *refs):
    outs, refs = refs[:group], refs[group:]
    rest, d_buf, l_buf, y_buf, p_buf, i_buf, small, d_sem, l_sem = refs
    rows = bias.shape[0]
    seg = rows // group
    size = rows // parts
    count = rows // LANES
    extra_v = kept.shape[1]
    offset = own.shape[0] * seg
    spot, _, core = position(group)
    i_copy = pltpu.make_async_copy(dest, i_buf, small.at[0])
    d_copies = chunked(diag.at[1], d_buf, d_sem, parts)
    l_copies = chunked(tiles.at[1, 0], l_buf, l_sem, parts)
    for copy in (i_copy, *d_copies, *l_copies):
        copy.start()
    remainder(bias, own, other, core, rest)
    both = split_cols(rest[...])
    p_buf[1] = dot_terms(m_hi[...], m_lo[...], both)
    deal(p_buf.at[1], 1, outs, spot, seg)
    i_copy.wait()
    vectors = []
    for k in range(2):
        target = i_buf[1, 0, k]
        here = kept[target // 2]
        at = pl.ds(pl.multiple_of(offset + (target // 2) * extra_v, SUB), extra_v)
        vectors.append(jnp.where(lax.rem(target, 2) == core, here, other[at, :]))
    part = share[...] - left_product(vectors[1][0:count, :], p_buf.at[1], rows)
    for c in range(parts):
        at = pl.ds(c * size, size)
        d_copies[c].wait()
        y_buf[at, :] = dot_terms(*split(d_buf[at, :]), both)
    y_copy = pltpu.make_async_copy(y_buf, sol.at[1], small.at[1])
    y_copy.start()
    both = split_cols(y_buf[...])
    for copy in l_copies:
        copy.wait()
    p_buf[0] = dot_terms(*split(l_buf[...]), both)
    deal(p_buf.at[0], 0, outs, spot, seg)
    part = part - left_product(vectors[0][0:count, :], p_buf.at[0], rows)
    base = 2 * seg
    extra = outs[0].shape[0] - base
    meta = tile_of([*named(i_buf, 1), part], extra)
    for out in outs:
        out[pl.ds(base, extra), :] = meta
    y_copy.wait()


def last_terms_kernel(parts, rhs, diag, d_hi, d_lo, bias, d_buf, d_sem, b_sem):
    rows = d_buf.shape[0]
    copies = chunked(diag.at[2], d_buf, d_sem, parts)
    b_copy = pltpu.make_async_copy(rhs.at[2], bias, b_sem)
    for copy in (*copies, b_copy):
        copy.start()
    size = rows // parts
    for c in range(parts):
        at = pl.ds(c * size, size)
        copies[c].wait()
        hi, lo = split(d_buf[at, :])
        d_hi[at, :] = hi
        d_lo[at, :] = lo
    b_copy.wait()


def last_kernel(group, parts, sol_in, own, other, bias, d_hi, d_lo, total, sol, seen,
                y_buf, rest, sem):
    rows = y_buf.shape[0]
    _, _, core = position(group)
    seen[...] = total[...]
    remainder(bias, own, other, core, rest)
    both = split_cols(rest[...])
    size = rows // parts
    outs = []
    for c in range(parts):
        at = pl.ds(c * size, size)
        y_buf[at, :] = dot_terms(d_hi[at, :], d_lo[at, :], both)
        outs.append(pltpu.make_async_copy(y_buf.at[at], sol.at[2, at], sem.at[c]))
        outs[c].start()
    for copy in outs:
        copy.wait()


def cost(flops, size):
    return pl.CostEstimate(flops=flops, bytes_accessed=size, transcendentals=0)


def limit(mib):
    return pltpu.CompilerParams(vmem_limit_bytes=mib << 20)


def stay(x):
    return pltpu.with_memory_space_constraint(x, pltpu.HBM)


def near_order(group):
    chips = (group - 2, *range(2, group - 2, 2))
    return [r + c for c in range(2) for r in chips] + [1]


def later(first, *others):
    tied = lax.optimization_barrier((tuple(first), tuple(others)))
    return list(tied[0]), tied[1]


def body(rhs, diag_inv, tiles, dest, obs_weight):
    count = lax.axis_size("rows")
    group = count // 2
    chips = count // 2
    levels, rows, width = rhs.shape
    seg = rows // group
    lines = rows // LANES
    extra = -(-lines // SUB) * SUB
    parts = 2
    f32 = jnp.float32
    def shift(x, bits):
        return lax.ppermute(x, "rows", [(i, i ^ bits) for i in range(count)])

    block = pltpu.VMEM((rows, width), f32)
    square = pltpu.VMEM((rows, rows), f32)
    sems = pltpu.SemaphoreType.DMA((parts,))
    term = jax.ShapeDtypeStruct((rows, rows), jnp.bfloat16)
    line = jax.ShapeDtypeStruct((1, width), f32)
    flat = jax.ShapeDtypeStruct((rows, width), f32)
    slot = jax.ShapeDtypeStruct((2 * seg + SUB, width), f32)
    mat_flops = 2 * rows * rows * width
    mat_bytes = 4 * rows * rows

    def exchange(pays):
        return [shift(pays[r], r) for r in near_order(group)] + [pays[0]]

    def spread(sums):
        return [shift(sums[r], 2 * r) for r in range(chips - 1, 0, -1)] + [sums[0]]

    def summed(got, v_tile):
        mode = "last" if v_tile is None else "first"
        tall = [2 * seg + (0 if v_tile is None else extra)] * chips
        if v_tile is None:
            tall[chips - 1] += SUB
        shapes = [jax.ShapeDtypeStruct((t, width), f32) for t in tall]
        given = list(got)
        if v_tile is None:
            shapes = [line, *shapes]
        else:
            given = [v_tile, *given]
        return pl.pallas_call(
            functools.partial(sum_kernel, group, mode),
            out_shape=tuple(shapes),
            in_specs=[VMEM] * len(given),
            out_specs=(VMEM,) * len(shapes),
            scratch_shapes=[
                pltpu.VMEM((count, seg, width), f32),
                pltpu.VMEM((group, SUB, width), f32),
            ],
            compiler_params=limit(6),
            cost_estimate=cost(2 * rows * width, 4 * 4 * rows * width),
            name="sum_parts",
        )(*given)

    def paired(got, near):
        mode = "first" if near is None else "last"
        lanes = chips // 2
        tall = lanes * seg + (chips * extra if near is None else 0)
        shapes = [jax.ShapeDtypeStruct((tall, width), f32)]
        shapes.append(jax.ShapeDtypeStruct((lanes, seg, width), f32))
        more = jax.ShapeDtypeStruct((chips, extra, width), f32)
        shapes.append(more if near is None else line)
        given = got if near is None else [near, *got]
        return pl.pallas_call(
            functools.partial(pair_kernel, chips, mode),
            out_shape=tuple(shapes),
            in_specs=[VMEM] * len(given),
            out_specs=(VMEM,) * len(shapes),
            compiler_params=limit(4),
            cost_estimate=cost(2 * rows * width, 4 * 3 * rows * width),
            name="pair_halves",
        )(*given)

    sol, *pays = pl.pallas_call(
        functools.partial(first_kernel, group, parts),
        out_shape=(pltpu.HBM(rhs.shape, f32), *[slot] * group),
        in_specs=[HBM, HBM, HBM, HBM],
        out_specs=(HBM, *[VMEM] * group),
        scratch_shapes=[
            block, square, square, square, block, pltpu.VMEM((2, rows, width), f32),
            pltpu.SMEM(dest.shape, jnp.int32),
            pltpu.SemaphoreType.DMA((3,)), pltpu.SemaphoreType.DMA((2 * parts,)), sems, sems,
        ],
        compiler_params=limit(24),
        cost_estimate=cost(3 * mat_flops, 3 * mat_bytes),
        name="level_first",
    )(stay(rhs), stay(diag_inv), stay(tiles), stay(dest))

    pays, (diag_later, rhs_later) = later(pays, diag_inv, rhs)
    got = exchange(pays)
    v_tile, share = pl.pallas_call(
        vector_kernel,
        out_shape=(jax.ShapeDtypeStruct((extra, width), f32), line),
        in_specs=[HBM, HBM, HBM],
        out_specs=(VMEM, VMEM),
        scratch_shapes=[
            block, square, pltpu.VMEM((lines, LANES), f32), pltpu.SemaphoreType.DMA((3,)),
        ],
        compiler_params=limit(8),
        cost_estimate=cost(4 * rows * rows, mat_bytes),
        name="vector",
    )(stay(rhs_later), stay(diag_later), stay(obs_weight.reshape(lines, LANES)))
    sums = summed(got, v_tile)

    sums, (diag_later, tiles_later, rhs_later) = later(sums, diag_inv, tiles, rhs)
    got = spread(sums)
    m_hi, m_lo, bias = pl.pallas_call(
        functools.partial(fold_kernel, 1),
        out_shape=(term, term, flat),
        in_specs=[HBM, HBM, HBM],
        out_specs=(VMEM, VMEM, VMEM),
        scratch_shapes=[square, square, sems, sems, pltpu.SemaphoreType.DMA],
        compiler_params=limit(32),
        cost_estimate=cost(3 * rows * mat_flops // width, 2 * mat_bytes),
        name="fold_levels",
    )(stay(rhs_later), stay(diag_later), stay(tiles_later))
    got, (m_hi, m_lo, bias) = later(got, m_hi, m_lo, bias)
    send, own, kept = paired(got, None)
    other = shift(send, 1)

    sol, *pays = pl.pallas_call(
        functools.partial(middle_kernel, group, parts),
        out_shape=(pltpu.HBM(rhs.shape, f32), *[slot] * group),
        in_specs=[HBM, VMEM, VMEM, VMEM, HBM, HBM, VMEM, VMEM, VMEM, VMEM, HBM],
        out_specs=(HBM, *[VMEM] * group),
        scratch_shapes=[
            block, square, square, block, pltpu.VMEM((2, rows, width), f32),
            pltpu.SMEM(dest.shape, jnp.int32), pltpu.SemaphoreType.DMA((2,)), sems, sems,
        ],
        input_output_aliases={0: 0},
        compiler_params=limit(24),
        cost_estimate=cost(3 * mat_flops, 2 * mat_bytes),
        name="level_middle",
    )(sol, own, other, bias, stay(diag_inv), stay(tiles), m_hi, m_lo, share, kept, stay(dest))

    pays, (diag_later,) = later(pays, diag_inv)
    got = exchange(pays)
    near, *sums = summed(got, None)
    sums, (diag_later, rhs_later) = later(sums, diag_later, rhs)
    got = spread(sums)
    d_hi, d_lo, bias = pl.pallas_call(
        functools.partial(last_terms_kernel, parts),
        out_shape=(term, term, flat),
        in_specs=[HBM, HBM],
        out_specs=(VMEM, VMEM, VMEM),
        scratch_shapes=[square, sems, pltpu.SemaphoreType.DMA],
        compiler_params=limit(12),
        cost_estimate=cost(rows * rows, 2 * mat_bytes),
        name="last_terms",
    )(stay(rhs_later), stay(diag_later))
    got, (d_hi, d_lo, bias) = later(got, d_hi, d_lo, bias)
    send, own, total = paired(got, near)
    other = shift(send, 1)

    sol, seen = pl.pallas_call(
        functools.partial(last_kernel, group, parts),
        out_shape=(pltpu.HBM(rhs.shape, f32), line),
        in_specs=[HBM] + [VMEM] * 6,
        out_specs=(HBM, VMEM),
        scratch_shapes=[block, block, sems],
        input_output_aliases={0: 0},
        compiler_params=limit(8),
        cost_estimate=cost(mat_flops, mat_bytes),
        name="level_last",
    )(sol, own, other, bias, d_hi, d_lo, total)
    return sol, seen.reshape(width)


def solution(mesh):
    in_specs = (
        P(None, "rows", "parts"),
        P(None, "rows", None),
        P(None, "rows", None, None),
        P(None, "rows", None),
        P("rows"),
    )
    out_specs = (P(None, "rows", "parts"), P("parts"))
    return jax.shard_map(body, mesh=mesh, in_specs=in_specs, out_specs=out_specs, check_vma=False)
```

```python
import functools

import jax
import jax.numpy as jnp
from jax import lax
from jax.experimental import pallas as pl
from jax.experimental.pallas import tpu as pltpu
from jax.sharding import PartitionSpec as P

LANES = 128
SUB = 8
HBM = pl.BlockSpec(memory_space=pltpu.HBM)
ANY = pl.BlockSpec(memory_space=pl.ANY)
VMEM = pl.BlockSpec(memory_space=pltpu.VMEM)
SMEM = pl.BlockSpec(memory_space=pltpu.SMEM)


def split(x):
    hi = x.astype(jnp.bfloat16)
    lo = (x - hi.astype(jnp.float32)).astype(jnp.bfloat16)
    return hi, lo


def split_cols(x):
    hi, lo = split(x)
    return jnp.concatenate([hi, lo], axis=1)


def dot_terms(hi, lo, both):
    width = both.shape[1] // 2
    wide = jnp.dot(hi, both, preferred_element_type=jnp.float32)
    narrow = jnp.dot(lo, both[:, :width], preferred_element_type=jnp.float32)
    return wide[:, :width] + (wide[:, width:] + narrow)


def left_product(vector, matrix, rows):
    columns = vector.T
    total = None
    for r in range(rows // LANES):
        block = matrix[r * LANES : (r + 1) * LANES, :]
        term = jnp.sum(columns[:, r : r + 1] * block, axis=0, keepdims=True)
        total = term if total is None else total + term
    return total


def chunked(ref, buf, sem, parts):
    size = buf.shape[0] // parts
    copies = []
    for c in range(parts):
        at = pl.ds(c * size, size)
        copies.append(pltpu.make_async_copy(ref.at[at], buf.at[at], sem.at[c]))
    return copies


def position(group):
    place = lax.axis_index("rows")
    return lax.rem(place, group), place // 2, lax.rem(place, 2)


def deal(product, k, outs, spot, seg):
    lanes = len(outs) // 2
    for r, out in enumerate(outs):
        there = spot ^ r
        first = (lax.rem(there, 2) * lanes + there // 2) * seg
        out[pl.ds(k * seg, seg), :] = product[pl.ds(pl.multiple_of(first, SUB), seg), :]


def tile_of(lines, extra):
    if extra > len(lines):
        lines = [*lines, jnp.zeros((extra - len(lines), LANES), jnp.float32)]
    return jnp.concatenate(lines, axis=0)


def named(dest, level):
    return [jnp.full((1, LANES), dest[level, 0, k].astype(jnp.float32)) for k in range(2)]


def first_kernel(group, parts, rhs, diag, tiles, dest, sol, *refs):
    outs, refs = refs[:group], refs[group:]
    b_buf, d_buf, l0_buf, l1_buf, y_buf, p_buf, i_buf, small, d_sem, l0_sem, l1_sem = refs
    rows = b_buf.shape[0]
    seg = rows // group
    size = rows // parts
    spot, _, _ = position(group)
    d_copies = chunked(diag.at[0], d_buf, d_sem, 2 * parts)
    l_copies = [
        chunked(tiles.at[0, 0], l0_buf, l0_sem, parts),
        chunked(tiles.at[0, 1], l1_buf, l1_sem, parts),
    ]
    b_copy = pltpu.make_async_copy(rhs.at[0], b_buf, small.at[0])
    i_copy = pltpu.make_async_copy(dest, i_buf, small.at[2])
    b_copy.start()
    i_copy.start()
    for copies in (d_copies, *l_copies):
        for copy in copies:
            copy.start()
    b_copy.wait()
    both = split_cols(b_buf[...])
    for c in range(2 * parts):
        at = pl.ds(c * (size // 2), size // 2)
        d_copies[c].wait()
        y_buf[at, :] = dot_terms(*split(d_buf[at, :]), both)
    y_copy = pltpu.make_async_copy(y_buf, sol.at[0], small.at[1])
    y_copy.start()
    i_copy.wait()
    base = 2 * seg
    extra = outs[0].shape[0] - base
    meta = tile_of(named(i_buf, 0), extra)
    for out in outs:
        out[pl.ds(base, extra), :] = meta
    both = split_cols(y_buf[...])
    for k, buf in enumerate((l0_buf, l1_buf)):
        for c in range(parts):
            at = pl.ds(c * size, size)
            l_copies[k][c].wait()
            p_buf[k, at, :] = dot_terms(*split(buf[at, :]), both)
        deal(p_buf.at[k], k, outs, spot, seg)
    y_copy.wait()


def vector_kernel(rhs, diag, weight, v_tile, share, b_buf, v_buf, w_buf, sem):
    rows = b_buf.shape[0]
    copies = [
        pltpu.make_async_copy(weight, w_buf, sem.at[0]),
        pltpu.make_async_copy(rhs.at[2], b_buf, sem.at[1]),
        pltpu.make_async_copy(diag.at[2], v_buf, sem.at[2]),
    ]
    for copy in copies:
        copy.start()
    for copy in copies:
        copy.wait()
    vector = left_product(w_buf[...], v_buf, rows)
    count = rows // LANES
    lines = [vector[:, r * LANES : (r + 1) * LANES] for r in range(count)]
    v_tile[...] = tile_of(lines, v_tile.shape[0])
    share[...] = left_product(v_tile[0:count, :], b_buf, rows)


def fold_kernel(rhs, diag, tiles, m_hi, m_lo, d_hi, d_lo, l_hi, l_lo, bias,
                d_buf, l_buf, d_sem, l_sem, b_sem):
    rows = d_buf.shape[0]
    parts = d_sem.shape[0]
    size = rows // parts
    d_copies = chunked(diag.at[1], d_buf, d_sem, parts)
    l_copies = [chunked(tiles.at[1, 1 - k], l_buf.at[k], l_sem.at[k], parts) for k in range(2)]
    b_copy = pltpu.make_async_copy(rhs.at[1], bias, b_sem)
    for copy in (*d_copies, *l_copies[0], *l_copies[1], b_copy):
        copy.start()
    for copy in d_copies:
        copy.wait()
    hi, lo = split(d_buf[...])
    d_hi[...] = hi
    d_lo[...] = lo
    both = jnp.concatenate([hi, lo], axis=1)
    for c in range(parts):
        at = pl.ds(c * size, size)
        l_copies[0][c].wait()
        hi, lo = split(dot_terms(*split(l_buf[0, at, :]), both))
        m_hi[at, :] = hi
        m_lo[at, :] = lo
    for copy in l_copies[1]:
        copy.wait()
    hi, lo = split(l_buf[1])
    l_hi[...] = hi
    l_lo[...] = lo
    b_copy.wait()


def sum_kernel(group, mode, *refs):
    refs = list(refs)
    v_tile = refs.pop(0) if mode == "first" else None
    order = [*near_order(group), 0]
    got, refs = [refs[order.index(r)] for r in range(group)], refs[group:]
    near = None if mode == "first" else refs.pop(0)
    chips = group
    outs, (out, tiles) = refs[:chips], refs[chips:]
    seg = out.shape[1]
    base = 2 * seg
    spot, chip, _ = position(group)
    targets = []
    for r in range(group):
        rows = got[r][base : base + SUB, :]
        targets.append([rows[k, 0].astype(jnp.int32) for k in range(2)])
    out[...] = jnp.zeros_like(out)
    if near is None:
        for r in range(chips):
            outs[r][pl.ds(base, v_tile.shape[0]), :] = v_tile[...]
    else:
        for r in range(group):
            tiles[spot ^ r] = got[r][base : base + SUB, :]
        total = tiles[0, 2:3, :]
        for q in range(1, group):
            total = total + tiles[q, 2:3, :]
        near[...] = total
        outs[chips - 1][pl.ds(base, SUB), :] = jnp.broadcast_to(total, (SUB, LANES))
    for r in range(group):
        for k in range(2):
            out[targets[r][k]] += got[r][pl.ds(k * seg, seg), :]
    for r in range(chips):
        for j in range(2):
            outs[r][pl.ds(j * seg, seg), :] = out[2 * (chip ^ r) + j]


def pair_kernel(chips, mode, *refs):
    near = None if mode == "first" else refs[0]
    refs = refs if mode == "first" else refs[1:]
    got, refs = refs[:chips][::-1], refs[chips:]
    send, own, more = refs
    lanes = chips // 2
    seg = own.shape[0] // lanes
    _, chip, core = position(chips)
    mine, theirs = pl.multiple_of(core * seg, SUB), pl.multiple_of((1 - core) * seg, SUB)
    for r in range(lanes):
        q = lax.rem(chip, lanes) ^ r
        a, b = got[r], got[r + lanes]
        at = pl.ds(pl.multiple_of(q * seg, SUB), seg)
        own[at, :] = a[pl.ds(mine, seg), :] + b[pl.ds(mine, seg), :]
        send[at, :] = a[pl.ds(theirs, seg), :] + b[pl.ds(theirs, seg), :]
    if mode == "first":
        extra = more.shape[1]
        for r in range(chips):
            tile = got[r][2 * seg :, :]
            more[chip ^ r] = tile
            at = pl.ds(pl.multiple_of(lanes * seg + (chip ^ r) * extra, SUB), extra)
            send[at, :] = tile
    else:
        more[...] = near[...] + got[chips - 1][2 * seg : 2 * seg + 1, :]


def own_part(group, which, own, bias, *refs):
    core = position(group)[2]
    depth = bias.shape[0] // 2
    at = pl.ds(pl.multiple_of((core if which == 0 else 1 - core) * depth, depth), depth)
    both = split_cols(bias[at, :] - own[0:depth, :])
    return [dot_terms(refs[j][:, at], refs[j + 1][:, at], both) for j in range(0, len(refs), 2)]


def early_kernel(group, *refs):
    count = (len(refs) - 2) // 3
    outs = refs[-count:]
    for out, value in zip(outs, own_part(group, 0, *refs[:-count])):
        out[...] = value


def middle_kernel(group, sol_in, other, bias, m_hi, m_lo, d_hi, d_lo, m_part, d_part, l_hi, l_lo,
                  share, kept, dest, sol, *refs):
    outs, refs = refs[:group], refs[group:]
    y_buf, p_buf, i_buf, small = refs
    rows = bias.shape[0]
    seg = rows // group
    count = rows // LANES
    extra_v = kept.shape[1]
    offset = rows // 2
    spot, _, core = position(group)
    i_copy = pltpu.make_async_copy(dest, i_buf, small.at[0])
    i_copy.start()
    product, solved = own_part(group, 1, other, bias, m_hi, m_lo, d_hi, d_lo)
    solved = solved + d_part[...]
    y_buf[...] = solved
    both = split_cols(solved)
    p_buf[1] = product + m_part[...]
    deal(p_buf.at[1], 1, outs, spot, seg)
    p_buf[0] = dot_terms(l_hi[...], l_lo[...], both)
    deal(p_buf.at[0], 0, outs, spot, seg)
    i_copy.wait()
    y_copy = pltpu.make_async_copy(y_buf, sol.at[1], small.at[1])
    y_copy.start()
    part = share[...]
    for k in range(2):
        target = i_buf[1, 0, k]
        here = kept[target // 2]
        at = pl.ds(pl.multiple_of(offset + (target // 2) * extra_v, SUB), extra_v)
        vector = jnp.where(lax.rem(target, 2) == core, here, other[at, :])
        part = part - left_product(vector[0:count, :], p_buf.at[k], rows)
    base = 2 * seg
    extra = outs[0].shape[0] - base
    meta = tile_of([*named(i_buf, 1), part], extra)
    for out in outs:
        out[pl.ds(base, extra), :] = meta
    y_copy.wait()


def last_terms_kernel(parts, rhs, diag, d_hi, d_lo, bias, d_buf, d_sem, b_sem):
    rows = d_buf.shape[0]
    copies = chunked(diag.at[2], d_buf, d_sem, parts)
    b_copy = pltpu.make_async_copy(rhs.at[2], bias, b_sem)
    for copy in (*copies, b_copy):
        copy.start()
    size = rows // parts
    for c in range(parts):
        at = pl.ds(c * size, size)
        copies[c].wait()
        hi, lo = split(d_buf[at, :])
        d_hi[at, :] = hi
        d_lo[at, :] = lo
    b_copy.wait()


def last_kernel(group, sol_in, other, bias, d_hi, d_lo, part, total, sol, seen, y_buf, sem):
    total_copy = pltpu.make_async_copy(total, seen, sem.at[1])
    total_copy.start()
    (value,) = own_part(group, 1, other, bias, d_hi, d_lo)
    y_buf[...] = value + part[...]
    copy = pltpu.make_async_copy(y_buf, sol.at[2], sem.at[0])
    copy.start()
    total_copy.wait()
    copy.wait()


def cost(flops, size):
    return pl.CostEstimate(flops=flops, bytes_accessed=size, transcendentals=0)


def limit(mib):
    return pltpu.CompilerParams(vmem_limit_bytes=mib << 20)


def stay(x):
    return pltpu.with_memory_space_constraint(x, pltpu.HBM)


def near_order(group):
    chips = (group - 2, *range(2, group - 2, 2))
    return [r + c for c in range(2) for r in chips] + [1]


def later(first, *others):
    tied = lax.optimization_barrier((tuple(first), tuple(others)))
    return list(tied[0]), tied[1]


def body(rhs, diag_inv, tiles, dest, obs_weight):
    count = lax.axis_size("rows")
    group = count // 2
    chips = count // 2
    levels, rows, width = rhs.shape
    seg = rows // group
    lines = rows // LANES
    extra = -(-lines // SUB) * SUB
    parts = 2
    f32 = jnp.float32
    def shift(x, bits):
        return lax.ppermute(x, "rows", [(i, i ^ bits) for i in range(count)])

    block = pltpu.VMEM((rows, width), f32)
    square = pltpu.VMEM((rows, rows), f32)
    sems = pltpu.SemaphoreType.DMA((parts,))
    term = jax.ShapeDtypeStruct((rows, rows), jnp.bfloat16)
    line = jax.ShapeDtypeStruct((1, width), f32)
    flat = jax.ShapeDtypeStruct((rows, width), f32)
    slot = jax.ShapeDtypeStruct((2 * seg + SUB, width), f32)
    mat_flops = 2 * rows * rows * width
    mat_bytes = 4 * rows * rows

    def exchange(pays):
        return [shift(pays[r], r) for r in near_order(group)] + [pays[0]]

    def spread(sums):
        return [shift(sums[r], 2 * r) for r in range(chips - 1, 0, -1)] + [sums[0]]

    def summed(got, v_tile):
        mode = "last" if v_tile is None else "first"
        tall = [2 * seg + (0 if v_tile is None else extra)] * chips
        if v_tile is None:
            tall[chips - 1] += SUB
        shapes = [jax.ShapeDtypeStruct((t, width), f32) for t in tall]
        given = list(got)
        if v_tile is None:
            shapes = [line, *shapes]
        else:
            given = [v_tile, *given]
        return pl.pallas_call(
            functools.partial(sum_kernel, group, mode),
            out_shape=tuple(shapes),
            in_specs=[VMEM] * len(given),
            out_specs=(VMEM,) * len(shapes),
            scratch_shapes=[
                pltpu.VMEM((count, seg, width), f32),
                pltpu.VMEM((group, SUB, width), f32),
            ],
            compiler_params=limit(6),
            cost_estimate=cost(2 * rows * width, 4 * 4 * rows * width),
            name="sum_parts",
        )(*given)

    def paired(got, near):
        mode = "first" if near is None else "last"
        lanes = chips // 2
        tall = lanes * seg + (chips * extra if near is None else 0)
        shapes = [jax.ShapeDtypeStruct((tall, width), f32)]
        shapes.append(jax.ShapeDtypeStruct((lanes * seg, width), f32))
        more = jax.ShapeDtypeStruct((chips, extra, width), f32)
        shapes.append(more if near is None else line)
        given = got if near is None else [near, *got]
        return pl.pallas_call(
            functools.partial(pair_kernel, chips, mode),
            out_shape=tuple(shapes),
            in_specs=[VMEM] * len(given),
            out_specs=(VMEM,) * len(shapes),
            compiler_params=limit(4),
            cost_estimate=cost(2 * rows * width, 4 * 3 * rows * width),
            name="pair_halves",
        )(*given)

    def early(own, bias, *terms):
        return pl.pallas_call(
            functools.partial(early_kernel, group),
            out_shape=(flat,) * (len(terms) // 2),
            in_specs=[VMEM] * (2 + len(terms)),
            out_specs=(VMEM,) * (len(terms) // 2),
            compiler_params=limit(8),
            cost_estimate=cost(len(terms) * mat_flops, len(terms) * mat_bytes // 4),
            name="own_columns",
        )(own, bias, *terms)

    sol, *pays = pl.pallas_call(
        functools.partial(first_kernel, group, parts),
        out_shape=(pltpu.HBM(rhs.shape, f32), *[slot] * group),
        in_specs=[HBM, HBM, HBM, HBM],
        out_specs=(HBM, *[VMEM] * group),
        scratch_shapes=[
            block, square, square, square, block, pltpu.VMEM((2, rows, width), f32),
            pltpu.SMEM(dest.shape, jnp.int32),
            pltpu.SemaphoreType.DMA((3,)), pltpu.SemaphoreType.DMA((2 * parts,)), sems, sems,
        ],
        compiler_params=limit(24),
        cost_estimate=cost(3 * mat_flops, 3 * mat_bytes),
        name="level_first",
    )(stay(rhs), stay(diag_inv), stay(tiles), stay(dest))

    pays, (diag_later, rhs_later) = later(pays, diag_inv, rhs)
    got = exchange(pays)
    v_tile, share = pl.pallas_call(
        vector_kernel,
        out_shape=(jax.ShapeDtypeStruct((extra, width), f32), line),
        in_specs=[HBM, HBM, HBM],
        out_specs=(VMEM, VMEM),
        scratch_shapes=[
            block, square, pltpu.VMEM((lines, LANES), f32), pltpu.SemaphoreType.DMA((3,)),
        ],
        compiler_params=limit(8),
        cost_estimate=cost(4 * rows * rows, mat_bytes),
        name="vector",
    )(stay(rhs_later), stay(diag_later), stay(obs_weight.reshape(lines, LANES)))
    sums = summed(got, v_tile)

    sums, (diag_later, tiles_later, rhs_later) = later(sums, diag_inv, tiles, rhs)
    got = spread(sums)
    *terms, bias = pl.pallas_call(
        fold_kernel,
        out_shape=(*[term] * 6, flat),
        in_specs=[HBM, HBM, HBM],
        out_specs=(VMEM,) * 7,
        scratch_shapes=[
            square, pltpu.VMEM((2, rows, rows), f32), sems,
            pltpu.SemaphoreType.DMA((2, parts)), pltpu.SemaphoreType.DMA,
        ],
        compiler_params=limit(32),
        cost_estimate=cost(3 * rows * mat_flops // width, 3 * mat_bytes),
        name="fold_levels",
    )(stay(rhs_later), stay(diag_later), stay(tiles_later))
    m_hi, m_lo, d_hi, d_lo, l_hi, l_lo = terms
    got, (m_hi, m_lo, d_hi, d_lo, l_hi, l_lo, bias) = later(got, *terms, bias)
    send, own, kept = paired(got, None)
    other = shift(send, 1)
    m_part, d_part = early(own, bias, m_hi, m_lo, d_hi, d_lo)

    sol, *pays = pl.pallas_call(
        functools.partial(middle_kernel, group),
        out_shape=(pltpu.HBM(rhs.shape, f32), *[slot] * group),
        in_specs=[HBM] + [VMEM] * 12 + [HBM],
        out_specs=(HBM, *[VMEM] * group),
        scratch_shapes=[
            block, pltpu.VMEM((2, rows, width), f32),
            pltpu.SMEM(dest.shape, jnp.int32), pltpu.SemaphoreType.DMA((2,)),
        ],
        input_output_aliases={0: 0},
        compiler_params=limit(16),
        cost_estimate=cost(3 * mat_flops, 2 * mat_bytes),
        name="level_middle",
    )(
        sol, other, bias, m_hi, m_lo, d_hi, d_lo, m_part, d_part, l_hi, l_lo,
        share, kept, stay(dest),
    )

    pays, (diag_later,) = later(pays, diag_inv)
    got = exchange(pays)
    near, *sums = summed(got, None)
    sums, (diag_later, rhs_later) = later(sums, diag_later, rhs)
    got = spread(sums)
    d_hi, d_lo, bias = pl.pallas_call(
        functools.partial(last_terms_kernel, parts),
        out_shape=(term, term, flat),
        in_specs=[HBM, HBM],
        out_specs=(VMEM, VMEM, VMEM),
        scratch_shapes=[square, sems, pltpu.SemaphoreType.DMA],
        compiler_params=limit(12),
        cost_estimate=cost(rows * rows, 2 * mat_bytes),
        name="last_terms",
    )(stay(rhs_later), stay(diag_later))
    got, (d_hi, d_lo, bias) = later(got, d_hi, d_lo, bias)
    send, own, total = paired(got, near)
    other = shift(send, 1)
    (d_part,) = early(own, bias, d_hi, d_lo)

    sol, seen = pl.pallas_call(
        functools.partial(last_kernel, group),
        out_shape=(pltpu.HBM(rhs.shape, f32), pltpu.HBM((1, width), f32)),
        in_specs=[HBM] + [VMEM] * 6,
        out_specs=(HBM, HBM),
        scratch_shapes=[block, pltpu.SemaphoreType.DMA((2,))],
        input_output_aliases={0: 0},
        compiler_params=limit(8),
        cost_estimate=cost(mat_flops, mat_bytes),
        name="level_last",
    )(sol, other, bias, d_hi, d_lo, d_part, total)
    return sol, seen.reshape(width)


def solution(mesh):
    in_specs = (
        P(None, "rows", "parts"),
        P(None, "rows", None),
        P(None, "rows", None, None),
        P(None, "rows", None),
        P("rows"),
    )
    out_specs = (P(None, "rows", "parts"), P("parts"))
    return jax.shard_map(body, mesh=mesh, in_specs=in_specs, out_specs=out_specs, check_vma=False)
```

```python
import functools

import jax
import jax.numpy as jnp
from jax import lax
from jax.experimental import pallas as pl
from jax.experimental.pallas import tpu as pltpu
from jax.sharding import PartitionSpec as P

LANES = 128
SUB = 8
HBM = pl.BlockSpec(memory_space=pltpu.HBM)
ANY = pl.BlockSpec(memory_space=pl.ANY)
VMEM = pl.BlockSpec(memory_space=pltpu.VMEM)
SMEM = pl.BlockSpec(memory_space=pltpu.SMEM)


def split(x):
    hi = x.astype(jnp.bfloat16)
    lo = (x - hi.astype(jnp.float32)).astype(jnp.bfloat16)
    return hi, lo


def split_cols(x):
    hi, lo = split(x)
    return jnp.concatenate([hi, lo], axis=1)


def dot_terms(hi, lo, both):
    width = both.shape[1] // 2
    wide = jnp.dot(hi, both, preferred_element_type=jnp.float32)
    narrow = jnp.dot(lo, both[:, :width], preferred_element_type=jnp.float32)
    return wide[:, :width] + (wide[:, width:] + narrow)


def left_product(vector, matrix, rows):
    columns = vector.T
    total = None
    for r in range(rows // LANES):
        block = matrix[r * LANES : (r + 1) * LANES, :]
        term = jnp.sum(columns[:, r : r + 1] * block, axis=0, keepdims=True)
        total = term if total is None else total + term
    return total


def chunked(ref, buf, sem, parts):
    size = buf.shape[0] // parts
    copies = []
    for c in range(parts):
        at = pl.ds(c * size, size)
        copies.append(pltpu.make_async_copy(ref.at[at], buf.at[at], sem.at[c]))
    return copies


def position(group):
    place = lax.axis_index("rows")
    return lax.rem(place, group), place // 2, lax.rem(place, 2)


def deal(product, k, outs, spot, seg):
    lanes = len(outs) // 2
    for r, out in enumerate(outs):
        there = spot ^ r
        first = (lax.rem(there, 2) * lanes + there // 2) * seg
        out[pl.ds(k * seg, seg), :] = product[pl.ds(pl.multiple_of(first, SUB), seg), :]


def tile_of(lines, extra):
    if extra > len(lines):
        lines = [*lines, jnp.zeros((extra - len(lines), LANES), jnp.float32)]
    return jnp.concatenate(lines, axis=0)


def named(dest, level):
    return [jnp.full((1, LANES), dest[level, 0, k].astype(jnp.float32)) for k in range(2)]


def first_kernel(group, parts, rhs, diag, tiles, dest, y_buf, *refs):
    outs, refs = refs[:group], refs[group:]
    b_buf, d_buf, l0_buf, l1_buf, p_buf, i_buf, small, d_sem, l0_sem, l1_sem = refs
    rows = b_buf.shape[0]
    seg = rows // group
    size = rows // parts
    spot, _, _ = position(group)
    d_copies = chunked(diag.at[0], d_buf, d_sem, 2 * parts)
    l_copies = [
        chunked(tiles.at[0, 0], l0_buf, l0_sem, parts),
        chunked(tiles.at[0, 1], l1_buf, l1_sem, parts),
    ]
    b_copy = pltpu.make_async_copy(rhs.at[0], b_buf, small.at[0])
    i_copy = pltpu.make_async_copy(dest, i_buf, small.at[1])
    b_copy.start()
    i_copy.start()
    for copies in (d_copies, *l_copies):
        for copy in copies:
            copy.start()
    b_copy.wait()
    both = split_cols(b_buf[...])
    for c in range(2 * parts):
        at = pl.ds(c * (size // 2), size // 2)
        d_copies[c].wait()
        y_buf[at, :] = dot_terms(*split(d_buf[at, :]), both)
    i_copy.wait()
    base = 2 * seg
    extra = outs[0].shape[0] - base
    meta = tile_of(named(i_buf, 0), extra)
    for out in outs:
        out[pl.ds(base, extra), :] = meta
    both = split_cols(y_buf[...])
    for k, buf in enumerate((l0_buf, l1_buf)):
        for c in range(parts):
            at = pl.ds(c * size, size)
            l_copies[k][c].wait()
            p_buf[k, at, :] = dot_terms(*split(buf[at, :]), both)
        deal(p_buf.at[k], k, outs, spot, seg)


def vector_kernel(rhs, diag, weight, solved, sol, v_tile, share, b_buf, v_buf, w_buf, sem):
    rows = b_buf.shape[0]
    copies = [
        pltpu.make_async_copy(weight, w_buf, sem.at[0]),
        pltpu.make_async_copy(rhs.at[2], b_buf, sem.at[1]),
        pltpu.make_async_copy(diag.at[2], v_buf, sem.at[2]),
        pltpu.make_async_copy(solved, sol.at[0], sem.at[3]),
    ]
    for copy in copies:
        copy.start()
    for copy in copies:
        copy.wait()
    vector = left_product(w_buf[...], v_buf, rows)
    count = rows // LANES
    lines = [vector[:, r * LANES : (r + 1) * LANES] for r in range(count)]
    v_tile[...] = tile_of(lines, v_tile.shape[0])
    share[...] = left_product(v_tile[0:count, :], b_buf, rows)


def fold_kernel(rhs, diag, tiles, m_hi, m_lo, d_hi, d_lo, l_hi, l_lo, bias,
                d_buf, l_buf, d_sem, l_sem, b_sem):
    rows = d_buf.shape[0]
    parts = d_sem.shape[0]
    size = rows // parts
    d_copies = chunked(diag.at[1], d_buf, d_sem, parts)
    l_copies = [chunked(tiles.at[1, 1 - k], l_buf.at[k], l_sem.at[k], parts) for k in range(2)]
    b_copy = pltpu.make_async_copy(rhs.at[1], bias, b_sem)
    for copy in (*d_copies, *l_copies[0], *l_copies[1], b_copy):
        copy.start()
    for copy in d_copies:
        copy.wait()
    hi, lo = split(d_buf[...])
    d_hi[...] = hi
    d_lo[...] = lo
    both = jnp.concatenate([hi, lo], axis=1)
    for c in range(parts):
        at = pl.ds(c * size, size)
        l_copies[0][c].wait()
        hi, lo = split(dot_terms(*split(l_buf[0, at, :]), both))
        m_hi[at, :] = hi
        m_lo[at, :] = lo
    for copy in l_copies[1]:
        copy.wait()
    hi, lo = split(l_buf[1])
    l_hi[...] = hi
    l_lo[...] = lo
    b_copy.wait()


def sum_kernel(group, mode, *refs):
    refs = list(refs)
    v_tile = refs.pop(0) if mode == "first" else None
    order = [*near_order(group), 0]
    got, refs = [refs[order.index(r)] for r in range(group)], refs[group:]
    near = None if mode == "first" else refs.pop(0)
    chips = group
    outs, (out, tiles) = refs[:chips], refs[chips:]
    seg = out.shape[1]
    base = 2 * seg
    spot, chip, _ = position(group)
    targets = []
    for r in range(group):
        rows = got[r][base : base + SUB, :]
        targets.append([rows[k, 0].astype(jnp.int32) for k in range(2)])
    out[...] = jnp.zeros_like(out)
    if near is None:
        for r in range(chips):
            outs[r][pl.ds(base, v_tile.shape[0]), :] = v_tile[...]
    else:
        for r in range(group):
            tiles[spot ^ r] = got[r][base : base + SUB, :]
        total = tiles[0, 2:3, :]
        for q in range(1, group):
            total = total + tiles[q, 2:3, :]
        near[...] = total
        outs[chips - 1][pl.ds(base, SUB), :] = jnp.broadcast_to(total, (SUB, LANES))
    for r in range(group):
        for k in range(2):
            out[targets[r][k]] += got[r][pl.ds(k * seg, seg), :]
    for r in range(chips):
        for j in range(2):
            outs[r][pl.ds(j * seg, seg), :] = out[2 * (chip ^ r) + j]


def pair_kernel(chips, mode, *refs):
    near = None if mode == "first" else refs[0]
    refs = refs if mode == "first" else refs[1:]
    got, refs = refs[:chips][::-1], refs[chips:]
    send, own, more = refs
    lanes = chips // 2
    seg = own.shape[0] // lanes
    _, chip, core = position(chips)
    mine, theirs = pl.multiple_of(core * seg, SUB), pl.multiple_of((1 - core) * seg, SUB)
    for r in range(lanes):
        q = lax.rem(chip, lanes) ^ r
        a, b = got[r], got[r + lanes]
        at = pl.ds(pl.multiple_of(q * seg, SUB), seg)
        own[at, :] = a[pl.ds(mine, seg), :] + b[pl.ds(mine, seg), :]
        send[at, :] = a[pl.ds(theirs, seg), :] + b[pl.ds(theirs, seg), :]
    if mode == "first":
        extra = more.shape[1]
        for r in range(chips):
            tile = got[r][2 * seg :, :]
            more[chip ^ r] = tile
            at = pl.ds(pl.multiple_of(lanes * seg + (chip ^ r) * extra, SUB), extra)
            send[at, :] = tile
    else:
        more[...] = near[...] + got[chips - 1][2 * seg : 2 * seg + 1, :]


def own_part(group, which, own, bias, *refs):
    core = position(group)[2]
    depth = bias.shape[0] // 2
    at = pl.ds(pl.multiple_of((core if which == 0 else 1 - core) * depth, depth), depth)
    both = split_cols(bias[at, :] - own[0:depth, :])
    return [dot_terms(refs[j][:, at], refs[j + 1][:, at], both) for j in range(0, len(refs), 2)]


def early_kernel(group, *refs):
    count = (len(refs) - 2) // 3
    outs = refs[-count:]
    for out, value in zip(outs, own_part(group, 0, *refs[:-count])):
        out[...] = value


def middle_kernel(group, other, bias, m_hi, m_lo, d_hi, d_lo, m_part, d_part, l_hi, l_lo,
                  share, kept, dest, solved, *refs):
    outs, (p_buf,) = refs[:group], refs[group:]
    rows = bias.shape[0]
    seg = rows // group
    count = rows // LANES
    extra_v = kept.shape[1]
    offset = rows // 2
    spot, _, core = position(group)
    names = dest[1]
    targets = [names[0, k] for k in range(2)]
    product, value = own_part(group, 1, other, bias, m_hi, m_lo, d_hi, d_lo)
    value = value + d_part[...]
    solved[...] = value
    both = split_cols(value)
    p_buf[1] = product + m_part[...]
    p_buf[0] = dot_terms(l_hi[...], l_lo[...], both)
    part = share[...]
    for k in (1, 0):
        deal(p_buf.at[k], k, outs, spot, seg)
        here = kept[targets[k] // 2]
        at = pl.ds(pl.multiple_of(offset + (targets[k] // 2) * extra_v, SUB), extra_v)
        vector = jnp.where(lax.rem(targets[k], 2) == core, here, other[at, :])
        part = part - left_product(vector[0:count, :], p_buf.at[k], rows)
    base = 2 * seg
    extra = outs[0].shape[0] - base
    lines = [jnp.full((1, LANES), target.astype(jnp.float32)) for target in targets]
    meta = tile_of([*lines, part], extra)
    for out in outs:
        out[pl.ds(base, extra), :] = meta


def last_terms_kernel(parts, sol_in, solved, rhs, diag, sol, d_hi, d_lo, bias,
                      d_buf, d_sem, b_sem):
    rows = d_buf.shape[0]
    copies = chunked(diag.at[2], d_buf, d_sem, parts)
    b_copy = pltpu.make_async_copy(rhs.at[2], bias, b_sem.at[0])
    y_copy = pltpu.make_async_copy(solved, sol.at[1], b_sem.at[1])
    for copy in (*copies, b_copy, y_copy):
        copy.start()
    size = rows // parts
    for c in range(parts):
        at = pl.ds(c * size, size)
        copies[c].wait()
        hi, lo = split(d_buf[at, :])
        d_hi[at, :] = hi
        d_lo[at, :] = lo
    b_copy.wait()
    y_copy.wait()


def last_kernel(group, sol_in, other, bias, d_hi, d_lo, part, total, sol, seen, y_buf, sem):
    total_copy = pltpu.make_async_copy(total, seen, sem.at[1])
    total_copy.start()
    (value,) = own_part(group, 1, other, bias, d_hi, d_lo)
    y_buf[...] = value + part[...]
    copy = pltpu.make_async_copy(y_buf, sol.at[2], sem.at[0])
    copy.start()
    total_copy.wait()
    copy.wait()


def cost(flops, size):
    return pl.CostEstimate(flops=flops, bytes_accessed=size, transcendentals=0)


def limit(mib):
    return pltpu.CompilerParams(vmem_limit_bytes=mib << 20)


def stay(x):
    return pltpu.with_memory_space_constraint(x, pltpu.HBM)


def near_order(group):
    chips = (group - 2, *range(2, group - 2, 2))
    return [r + c for c in range(2) for r in chips] + [1]


def later(first, *others):
    tied = lax.optimization_barrier((tuple(first), tuple(others)))
    return list(tied[0]), tied[1]


def body(rhs, diag_inv, tiles, dest, obs_weight):
    count = lax.axis_size("rows")
    group = count // 2
    chips = count // 2
    levels, rows, width = rhs.shape
    seg = rows // group
    lines = rows // LANES
    extra = -(-lines // SUB) * SUB
    parts = 2
    f32 = jnp.float32
    def shift(x, bits):
        return lax.ppermute(x, "rows", [(i, i ^ bits) for i in range(count)])

    block = pltpu.VMEM((rows, width), f32)
    square = pltpu.VMEM((rows, rows), f32)
    sems = pltpu.SemaphoreType.DMA((parts,))
    term = jax.ShapeDtypeStruct((rows, rows), jnp.bfloat16)
    line = jax.ShapeDtypeStruct((1, width), f32)
    flat = jax.ShapeDtypeStruct((rows, width), f32)
    slot = jax.ShapeDtypeStruct((2 * seg + SUB, width), f32)
    mat_flops = 2 * rows * rows * width
    mat_bytes = 4 * rows * rows

    def exchange(pays):
        return [shift(pays[r], r) for r in near_order(group)] + [pays[0]]

    def spread(sums):
        return [shift(sums[r], 2 * r) for r in range(chips - 1, 0, -1)] + [sums[0]]

    def summed(got, v_tile):
        mode = "last" if v_tile is None else "first"
        tall = [2 * seg + (0 if v_tile is None else extra)] * chips
        if v_tile is None:
            tall[chips - 1] += SUB
        shapes = [jax.ShapeDtypeStruct((t, width), f32) for t in tall]
        given = list(got)
        if v_tile is None:
            shapes = [line, *shapes]
        else:
            given = [v_tile, *given]
        return pl.pallas_call(
            functools.partial(sum_kernel, group, mode),
            out_shape=tuple(shapes),
            in_specs=[VMEM] * len(given),
            out_specs=(VMEM,) * len(shapes),
            scratch_shapes=[
                pltpu.VMEM((count, seg, width), f32),
                pltpu.VMEM((group, SUB, width), f32),
            ],
            compiler_params=limit(6),
            cost_estimate=cost(2 * rows * width, 4 * 4 * rows * width),
            name="sum_parts",
        )(*given)

    def paired(got, near):
        mode = "first" if near is None else "last"
        lanes = chips // 2
        tall = lanes * seg + (chips * extra if near is None else 0)
        shapes = [jax.ShapeDtypeStruct((tall, width), f32)]
        shapes.append(jax.ShapeDtypeStruct((lanes * seg, width), f32))
        more = jax.ShapeDtypeStruct((chips, extra, width), f32)
        shapes.append(more if near is None else line)
        given = got if near is None else [near, *got]
        return pl.pallas_call(
            functools.partial(pair_kernel, chips, mode),
            out_shape=tuple(shapes),
            in_specs=[VMEM] * len(given),
            out_specs=(VMEM,) * len(shapes),
            compiler_params=limit(4),
            cost_estimate=cost(2 * rows * width, 4 * 3 * rows * width),
            name="pair_halves",
        )(*given)

    def early(own, bias, *terms):
        return pl.pallas_call(
            functools.partial(early_kernel, group),
            out_shape=(flat,) * (len(terms) // 2),
            in_specs=[VMEM] * (2 + len(terms)),
            out_specs=(VMEM,) * (len(terms) // 2),
            compiler_params=limit(8),
            cost_estimate=cost(len(terms) * mat_flops, len(terms) * mat_bytes // 4),
            name="own_columns",
        )(own, bias, *terms)

    solved, *pays = pl.pallas_call(
        functools.partial(first_kernel, group, parts),
        out_shape=(flat, *[slot] * group),
        in_specs=[HBM, HBM, HBM, HBM],
        out_specs=(VMEM, *[VMEM] * group),
        scratch_shapes=[
            block, square, square, square, pltpu.VMEM((2, rows, width), f32),
            pltpu.SMEM(dest.shape, jnp.int32),
            pltpu.SemaphoreType.DMA((2,)), pltpu.SemaphoreType.DMA((2 * parts,)), sems, sems,
        ],
        compiler_params=limit(24),
        cost_estimate=cost(3 * mat_flops, 3 * mat_bytes),
        name="level_first",
    )(stay(rhs), stay(diag_inv), stay(tiles), stay(dest))

    pays, (diag_later, rhs_later) = later(pays, diag_inv, rhs)
    got = exchange(pays)
    sol, v_tile, share = pl.pallas_call(
        vector_kernel,
        out_shape=(
            pltpu.HBM(rhs.shape, f32), jax.ShapeDtypeStruct((extra, width), f32), line,
        ),
        in_specs=[HBM, HBM, HBM, VMEM],
        out_specs=(HBM, VMEM, VMEM),
        scratch_shapes=[
            block, square, pltpu.VMEM((lines, LANES), f32), pltpu.SemaphoreType.DMA((4,)),
        ],
        compiler_params=limit(8),
        cost_estimate=cost(4 * rows * rows, mat_bytes),
        name="vector",
    )(stay(rhs_later), stay(diag_later), stay(obs_weight.reshape(lines, LANES)), solved)
    sums = summed(got, v_tile)

    sums, (diag_later, tiles_later, rhs_later) = later(sums, diag_inv, tiles, rhs)
    got = spread(sums)
    *terms, bias = pl.pallas_call(
        fold_kernel,
        out_shape=(*[term] * 6, flat),
        in_specs=[HBM, HBM, HBM],
        out_specs=(VMEM,) * 7,
        scratch_shapes=[
            square, pltpu.VMEM((2, rows, rows), f32), sems,
            pltpu.SemaphoreType.DMA((2, parts)), pltpu.SemaphoreType.DMA,
        ],
        compiler_params=limit(32),
        cost_estimate=cost(3 * rows * mat_flops // width, 3 * mat_bytes),
        name="fold_levels",
    )(stay(rhs_later), stay(diag_later), stay(tiles_later))
    m_hi, m_lo, d_hi, d_lo, l_hi, l_lo = terms
    got, (m_hi, m_lo, d_hi, d_lo, l_hi, l_lo, bias) = later(got, *terms, bias)
    send, own, kept = paired(got, None)
    other = shift(send, 1)
    m_part, d_part = early(own, bias, m_hi, m_lo, d_hi, d_lo)

    solved, *pays = pl.pallas_call(
        functools.partial(middle_kernel, group),
        out_shape=(flat, *[slot] * group),
        in_specs=[VMEM] * 13,
        out_specs=(VMEM,) * (1 + group),
        scratch_shapes=[pltpu.VMEM((2, rows, width), f32)],
        compiler_params=limit(16),
        cost_estimate=cost(3 * mat_flops, 2 * mat_bytes),
        name="level_middle",
    )(
        other, bias, m_hi, m_lo, d_hi, d_lo, m_part, d_part, l_hi, l_lo, share, kept, dest,
    )

    pays, (diag_later,) = later(pays, diag_inv)
    got = exchange(pays)
    near, *sums = summed(got, None)
    sums, (diag_later, rhs_later) = later(sums, diag_later, rhs)
    got = spread(sums)
    sol, d_hi, d_lo, bias = pl.pallas_call(
        functools.partial(last_terms_kernel, parts),
        out_shape=(pltpu.HBM(rhs.shape, f32), term, term, flat),
        in_specs=[HBM, VMEM, HBM, HBM],
        out_specs=(HBM, VMEM, VMEM, VMEM),
        scratch_shapes=[square, sems, pltpu.SemaphoreType.DMA((2,))],
        input_output_aliases={0: 0},
        compiler_params=limit(12),
        cost_estimate=cost(rows * rows, 2 * mat_bytes),
        name="last_terms",
    )(sol, solved, stay(rhs_later), stay(diag_later))
    got, (d_hi, d_lo, bias) = later(got, d_hi, d_lo, bias)
    send, own, total = paired(got, near)
    other = shift(send, 1)
    (d_part,) = early(own, bias, d_hi, d_lo)

    sol, seen = pl.pallas_call(
        functools.partial(last_kernel, group),
        out_shape=(pltpu.HBM(rhs.shape, f32), pltpu.HBM((1, width), f32)),
        in_specs=[HBM] + [VMEM] * 6,
        out_specs=(HBM, HBM),
        scratch_shapes=[block, pltpu.SemaphoreType.DMA((2,))],
        input_output_aliases={0: 0},
        compiler_params=limit(8),
        cost_estimate=cost(mat_flops, mat_bytes),
        name="level_last",
    )(sol, other, bias, d_hi, d_lo, d_part, total)
    return sol, seen.reshape(width)


def solution(mesh):
    in_specs = (
        P(None, "rows", "parts"),
        P(None, "rows", None),
        P(None, "rows", None, None),
        P(None, "rows", None),
        P("rows"),
    )
    out_specs = (P(None, "rows", "parts"), P("parts"))
    return jax.shard_map(body, mesh=mesh, in_specs=in_specs, out_specs=out_specs, check_vma=False)
```

```python
import functools

import jax
import jax.numpy as jnp
from jax import lax
from jax.experimental import pallas as pl
from jax.experimental.pallas import tpu as pltpu
from jax.sharding import PartitionSpec as P

LANES = 128
SUB = 8
CUTS = (4, 1, 1)
HBM = pl.BlockSpec(memory_space=pltpu.HBM)
ANY = pl.BlockSpec(memory_space=pl.ANY)
VMEM = pl.BlockSpec(memory_space=pltpu.VMEM)
SMEM = pl.BlockSpec(memory_space=pltpu.SMEM)


def split(x):
    hi = x.astype(jnp.bfloat16)
    lo = (x - hi.astype(jnp.float32)).astype(jnp.bfloat16)
    return hi, lo


def split_cols(x):
    hi, lo = split(x)
    return jnp.concatenate([hi, lo], axis=1)


def dot_terms(hi, lo, both):
    width = both.shape[1] // 2
    wide = jnp.dot(hi, both, preferred_element_type=jnp.float32)
    narrow = jnp.dot(lo, both[:, :width], preferred_element_type=jnp.float32)
    return wide[:, :width] + (wide[:, width:] + narrow)


def left_product(vector, matrix, rows):
    columns = vector.T
    total = None
    for r in range(rows // LANES):
        block = matrix[r * LANES : (r + 1) * LANES, :]
        term = jnp.sum(columns[:, r : r + 1] * block, axis=0, keepdims=True)
        total = term if total is None else total + term
    return total


def chunked(ref, buf, sem, parts):
    size = buf.shape[0] // parts
    copies = []
    for c in range(parts):
        at = pl.ds(c * size, size)
        copies.append(pltpu.make_async_copy(ref.at[at], buf.at[at], sem.at[c]))
    return copies


def position(group):
    place = lax.axis_index("rows")
    return lax.rem(place, group), place // 2, lax.rem(place, 2)


def deal(product, k, outs, spot, seg):
    lanes = len(outs) // 2
    for r, out in enumerate(outs):
        there = spot ^ r
        first = (lax.rem(there, 2) * lanes + there // 2) * seg
        out[pl.ds(k * seg, seg), :] = product[pl.ds(pl.multiple_of(first, SUB), seg), :]


def tile_of(lines, extra):
    if extra > len(lines):
        lines = [*lines, jnp.zeros((extra - len(lines), LANES), jnp.float32)]
    return jnp.concatenate(lines, axis=0)


def named(dest, level):
    return [jnp.full((1, LANES), dest[level, 0, k].astype(jnp.float32)) for k in range(2)]


def first_kernel(group, cuts, rhs, diag, tiles, dest, solved, *refs):
    outs, refs = refs[:group], refs[group:]
    b_buf, d_buf, l_buf, p_buf, i_buf, small, d_sem, l0_sem, l1_sem = refs
    rows = b_buf.shape[0]
    seg = rows // group
    spot, _, _ = position(group)
    d_copies = chunked(diag.at[0], d_buf, d_sem, cuts[0])
    l_copies = [
        chunked(tiles.at[0, 0], l_buf.at[0], l0_sem, cuts[1]),
        chunked(tiles.at[0, 1], l_buf.at[1], l1_sem, cuts[2]),
    ]
    b_copy = pltpu.make_async_copy(rhs.at[0], b_buf, small.at[0])
    i_copy = pltpu.make_async_copy(dest, i_buf, small.at[1])
    b_copy.start()
    for copies in (d_copies, *l_copies):
        for copy in copies:
            copy.start()
    i_copy.start()
    b_copy.wait()
    both = split_cols(b_buf[...])
    size = rows // cuts[0]
    for c in range(cuts[0]):
        at = pl.ds(c * size, size)
        d_copies[c].wait()
        solved[at, :] = dot_terms(*split(d_buf[at, :]), both)
    i_copy.wait()
    base = 2 * seg
    extra = outs[0].shape[0] - base
    meta = tile_of(named(i_buf, 0), extra)
    for out in outs:
        out[pl.ds(base, extra), :] = meta
    both = split_cols(solved[...])
    for k in range(2):
        size = rows // cuts[1 + k]
        for c in range(cuts[1 + k]):
            at = pl.ds(c * size, size)
            l_copies[k][c].wait()
            p_buf[k, at, :] = dot_terms(*split(l_buf[k, at, :]), both)
        deal(p_buf.at[k], k, outs, spot, seg)


def vector_kernel(rhs, diag, weight, solved, sol, v_tile, share, b_buf, v_buf, w_buf, sem):
    rows = b_buf.shape[0]
    copies = [
        pltpu.make_async_copy(weight, w_buf, sem.at[0]),
        pltpu.make_async_copy(rhs.at[2], b_buf, sem.at[1]),
        pltpu.make_async_copy(diag.at[2], v_buf, sem.at[2]),
        pltpu.make_async_copy(solved, sol.at[0], sem.at[3]),
    ]
    for copy in copies:
        copy.start()
    for copy in copies:
        copy.wait()
    vector = left_product(w_buf[...], v_buf, rows)
    count = rows // LANES
    lines = [vector[:, r * LANES : (r + 1) * LANES] for r in range(count)]
    v_tile[...] = tile_of(lines, v_tile.shape[0])
    share[...] = left_product(v_tile[0:count, :], b_buf, rows)


def fold_kernel(rhs, diag, tiles, m_hi, m_lo, d_hi, d_lo, l_hi, l_lo, bias,
                d_buf, l_buf, d_sem, l_sem, b_sem):
    rows = d_buf.shape[0]
    parts = d_sem.shape[0]
    size = rows // parts
    d_copies = chunked(diag.at[1], d_buf, d_sem, parts)
    l_copies = [chunked(tiles.at[1, 1 - k], l_buf.at[k], l_sem.at[k], parts) for k in range(2)]
    b_copy = pltpu.make_async_copy(rhs.at[1], bias, b_sem)
    for copy in (*d_copies, *l_copies[0], *l_copies[1], b_copy):
        copy.start()
    for copy in d_copies:
        copy.wait()
    hi, lo = split(d_buf[...])
    d_hi[...] = hi
    d_lo[...] = lo
    both = jnp.concatenate([hi, lo], axis=1)
    for c in range(parts):
        at = pl.ds(c * size, size)
        l_copies[0][c].wait()
        hi, lo = split(dot_terms(*split(l_buf[0, at, :]), both))
        m_hi[at, :] = hi
        m_lo[at, :] = lo
    for copy in l_copies[1]:
        copy.wait()
    hi, lo = split(l_buf[1])
    l_hi[...] = hi
    l_lo[...] = lo
    b_copy.wait()


def sum_kernel(group, mode, *refs):
    refs = list(refs)
    v_tile = refs.pop(0) if mode == "first" else None
    order = [*near_order(group), 0]
    got, refs = [refs[order.index(r)] for r in range(group)], refs[group:]
    near = None if mode == "first" else refs.pop(0)
    chips = group
    outs, (out, tiles) = refs[:chips], refs[chips:]
    seg = out.shape[1]
    base = 2 * seg
    spot, chip, _ = position(group)
    targets = []
    for r in range(group):
        rows = got[r][base : base + SUB, :]
        targets.append([rows[k, 0].astype(jnp.int32) for k in range(2)])
    out[...] = jnp.zeros_like(out)
    if near is None:
        for r in range(chips):
            outs[r][pl.ds(base, v_tile.shape[0]), :] = v_tile[...]
    else:
        for r in range(group):
            tiles[spot ^ r] = got[r][base : base + SUB, :]
        total = tiles[0, 2:3, :]
        for q in range(1, group):
            total = total + tiles[q, 2:3, :]
        near[...] = total
        outs[chips - 1][pl.ds(base, SUB), :] = jnp.broadcast_to(total, (SUB, LANES))
    for r in range(group):
        for k in range(2):
            out[targets[r][k]] += got[r][pl.ds(k * seg, seg), :]
    for r in range(chips):
        for j in range(2):
            outs[r][pl.ds(j * seg, seg), :] = out[2 * (chip ^ r) + j]


def pair_kernel(chips, mode, *refs):
    near = None if mode == "first" else refs[0]
    refs = refs if mode == "first" else refs[1:]
    got, refs = refs[:chips][::-1], refs[chips:]
    send, own, more = refs
    lanes = chips // 2
    seg = own.shape[0] // lanes
    _, chip, core = position(chips)
    mine, theirs = pl.multiple_of(core * seg, SUB), pl.multiple_of((1 - core) * seg, SUB)
    for r in range(lanes):
        q = lax.rem(chip, lanes) ^ r
        a, b = got[r], got[r + lanes]
        at = pl.ds(pl.multiple_of(q * seg, SUB), seg)
        own[at, :] = a[pl.ds(mine, seg), :] + b[pl.ds(mine, seg), :]
        send[at, :] = a[pl.ds(theirs, seg), :] + b[pl.ds(theirs, seg), :]
    if mode == "first":
        extra = more.shape[1]
        for r in range(chips):
            tile = got[r][2 * seg :, :]
            more[chip ^ r] = tile
            at = pl.ds(pl.multiple_of(lanes * seg + (chip ^ r) * extra, SUB), extra)
            send[at, :] = tile
    else:
        more[...] = near[...] + got[chips - 1][2 * seg : 2 * seg + 1, :]


def own_part(group, which, own, bias, *refs):
    core = position(group)[2]
    depth = bias.shape[0] // 2
    at = pl.ds(pl.multiple_of((core if which == 0 else 1 - core) * depth, depth), depth)
    both = split_cols(bias[at, :] - own[0:depth, :])
    return [dot_terms(refs[j][:, at], refs[j + 1][:, at], both) for j in range(0, len(refs), 2)]


def early_kernel(group, *refs):
    count = (len(refs) - 2) // 3
    outs = refs[-count:]
    for out, value in zip(outs, own_part(group, 0, *refs[:-count])):
        out[...] = value


def middle_kernel(group, other, bias, m_hi, m_lo, d_hi, d_lo, m_part, d_part, l_hi, l_lo,
                  share, kept, dest, solved, *refs):
    outs, (p_buf,) = refs[:group], refs[group:]
    rows = bias.shape[0]
    seg = rows // group
    count = rows // LANES
    extra_v = kept.shape[1]
    offset = rows // 2
    spot, _, core = position(group)
    names = dest[1]
    targets = [names[0, k] for k in range(2)]
    product, value = own_part(group, 1, other, bias, m_hi, m_lo, d_hi, d_lo)
    value = value + d_part[...]
    solved[...] = value
    both = split_cols(value)
    p_buf[1] = product + m_part[...]
    p_buf[0] = dot_terms(l_hi[...], l_lo[...], both)
    part = share[...]
    for k in (1, 0):
        deal(p_buf.at[k], k, outs, spot, seg)
        here = kept[targets[k] // 2]
        at = pl.ds(pl.multiple_of(offset + (targets[k] // 2) * extra_v, SUB), extra_v)
        vector = jnp.where(lax.rem(targets[k], 2) == core, here, other[at, :])
        part = part - left_product(vector[0:count, :], p_buf.at[k], rows)
    base = 2 * seg
    extra = outs[0].shape[0] - base
    lines = [jnp.full((1, LANES), target.astype(jnp.float32)) for target in targets]
    meta = tile_of([*lines, part], extra)
    for out in outs:
        out[pl.ds(base, extra), :] = meta


def last_terms_kernel(parts, sol_in, solved, rhs, diag, sol, d_hi, d_lo, bias,
                      d_buf, d_sem, b_sem):
    rows = d_buf.shape[0]
    copies = chunked(diag.at[2], d_buf, d_sem, parts)
    b_copy = pltpu.make_async_copy(rhs.at[2], bias, b_sem.at[0])
    y_copy = pltpu.make_async_copy(solved, sol.at[1], b_sem.at[1])
    for copy in (*copies, b_copy, y_copy):
        copy.start()
    size = rows // parts
    for c in range(parts):
        at = pl.ds(c * size, size)
        copies[c].wait()
        hi, lo = split(d_buf[at, :])
        d_hi[at, :] = hi
        d_lo[at, :] = lo
    b_copy.wait()
    y_copy.wait()


def last_kernel(group, sol_in, other, bias, d_hi, d_lo, part, total, sol, seen, y_buf, sem):
    total_copy = pltpu.make_async_copy(total, seen, sem.at[1])
    total_copy.start()
    (value,) = own_part(group, 1, other, bias, d_hi, d_lo)
    y_buf[...] = value + part[...]
    copy = pltpu.make_async_copy(y_buf, sol.at[2], sem.at[0])
    copy.start()
    total_copy.wait()
    copy.wait()


def cost(flops, size):
    return pl.CostEstimate(flops=flops, bytes_accessed=size, transcendentals=0)


def limit(mib):
    return pltpu.CompilerParams(vmem_limit_bytes=mib << 20)


def stay(x):
    return pltpu.with_memory_space_constraint(x, pltpu.HBM)


def near_order(group):
    chips = (group - 2, *range(2, group - 2, 2))
    return [r + c for c in range(2) for r in chips] + [1]


def later(first, *others):
    tied = lax.optimization_barrier((tuple(first), tuple(others)))
    return list(tied[0]), tied[1]


def body(rhs, diag_inv, tiles, dest, obs_weight):
    count = lax.axis_size("rows")
    group = count // 2
    chips = count // 2
    levels, rows, width = rhs.shape
    seg = rows // group
    lines = rows // LANES
    extra = -(-lines // SUB) * SUB
    parts = 2
    f32 = jnp.float32
    def shift(x, bits):
        return lax.ppermute(x, "rows", [(i, i ^ bits) for i in range(count)])

    block = pltpu.VMEM((rows, width), f32)
    square = pltpu.VMEM((rows, rows), f32)
    sems = pltpu.SemaphoreType.DMA((parts,))
    term = jax.ShapeDtypeStruct((rows, rows), jnp.bfloat16)
    line = jax.ShapeDtypeStruct((1, width), f32)
    flat = jax.ShapeDtypeStruct((rows, width), f32)
    slot = jax.ShapeDtypeStruct((2 * seg + SUB, width), f32)
    mat_flops = 2 * rows * rows * width
    mat_bytes = 4 * rows * rows

    def exchange(pays):
        return [shift(pays[r], r) for r in near_order(group)] + [pays[0]]

    def spread(sums):
        return [shift(sums[r], 2 * r) for r in range(chips - 1, 0, -1)] + [sums[0]]

    def summed(got, v_tile):
        mode = "last" if v_tile is None else "first"
        tall = [2 * seg + (0 if v_tile is None else extra)] * chips
        if v_tile is None:
            tall[chips - 1] += SUB
        shapes = [jax.ShapeDtypeStruct((t, width), f32) for t in tall]
        given = list(got)
        if v_tile is None:
            shapes = [line, *shapes]
        else:
            given = [v_tile, *given]
        return pl.pallas_call(
            functools.partial(sum_kernel, group, mode),
            out_shape=tuple(shapes),
            in_specs=[VMEM] * len(given),
            out_specs=(VMEM,) * len(shapes),
            scratch_shapes=[
                pltpu.VMEM((count, seg, width), f32),
                pltpu.VMEM((group, SUB, width), f32),
            ],
            compiler_params=limit(6),
            cost_estimate=cost(2 * rows * width, 4 * 4 * rows * width),
            name="sum_parts",
        )(*given)

    def paired(got, near):
        mode = "first" if near is None else "last"
        lanes = chips // 2
        tall = lanes * seg + (chips * extra if near is None else 0)
        shapes = [jax.ShapeDtypeStruct((tall, width), f32)]
        shapes.append(jax.ShapeDtypeStruct((lanes * seg, width), f32))
        more = jax.ShapeDtypeStruct((chips, extra, width), f32)
        shapes.append(more if near is None else line)
        given = got if near is None else [near, *got]
        return pl.pallas_call(
            functools.partial(pair_kernel, chips, mode),
            out_shape=tuple(shapes),
            in_specs=[VMEM] * len(given),
            out_specs=(VMEM,) * len(shapes),
            compiler_params=limit(4),
            cost_estimate=cost(2 * rows * width, 4 * 3 * rows * width),
            name="pair_halves",
        )(*given)

    def early(own, bias, *terms):
        return pl.pallas_call(
            functools.partial(early_kernel, group),
            out_shape=(flat,) * (len(terms) // 2),
            in_specs=[VMEM] * (2 + len(terms)),
            out_specs=(VMEM,) * (len(terms) // 2),
            compiler_params=limit(8),
            cost_estimate=cost(len(terms) * mat_flops, len(terms) * mat_bytes // 4),
            name="own_columns",
        )(own, bias, *terms)

    cuts = CUTS
    solved, *pays = pl.pallas_call(
        functools.partial(first_kernel, group, cuts),
        out_shape=(flat, *[slot] * group),
        in_specs=[HBM, HBM, HBM, HBM],
        out_specs=(VMEM,) * (1 + group),
        scratch_shapes=[
            block, square, pltpu.VMEM((2, rows, rows), f32), pltpu.VMEM((2, rows, width), f32),
            pltpu.SMEM(dest.shape, jnp.int32), pltpu.SemaphoreType.DMA((2,)),
            *[pltpu.SemaphoreType.DMA((cut,)) for cut in cuts],
        ],
        compiler_params=limit(24),
        cost_estimate=cost(3 * mat_flops, 3 * mat_bytes),
        name="level_first",
    )(stay(rhs), stay(diag_inv), stay(tiles), stay(dest))

    pays, (diag_later, rhs_later) = later(pays, diag_inv, rhs)
    got = exchange(pays)
    sol, v_tile, share = pl.pallas_call(
        vector_kernel,
        out_shape=(
            pltpu.HBM(rhs.shape, f32), jax.ShapeDtypeStruct((extra, width), f32), line,
        ),
        in_specs=[HBM, HBM, HBM, VMEM],
        out_specs=(HBM, VMEM, VMEM),
        scratch_shapes=[
            block, square, pltpu.VMEM((lines, LANES), f32), pltpu.SemaphoreType.DMA((4,)),
        ],
        compiler_params=limit(8),
        cost_estimate=cost(4 * rows * rows, mat_bytes),
        name="vector",
    )(stay(rhs_later), stay(diag_later), stay(obs_weight.reshape(lines, LANES)), solved)
    sums = summed(got, v_tile)

    sums, (diag_later, tiles_later, rhs_later) = later(sums, diag_inv, tiles, rhs)
    got = spread(sums)
    *terms, bias = pl.pallas_call(
        fold_kernel,
        out_shape=(*[term] * 6, flat),
        in_specs=[HBM, HBM, HBM],
        out_specs=(VMEM,) * 7,
        scratch_shapes=[
            square, pltpu.VMEM((2, rows, rows), f32), sems,
            pltpu.SemaphoreType.DMA((2, parts)), pltpu.SemaphoreType.DMA,
        ],
        compiler_params=limit(32),
        cost_estimate=cost(3 * rows * mat_flops // width, 3 * mat_bytes),
        name="fold_levels",
    )(stay(rhs_later), stay(diag_later), stay(tiles_later))
    m_hi, m_lo, d_hi, d_lo, l_hi, l_lo = terms
    got, (m_hi, m_lo, d_hi, d_lo, l_hi, l_lo, bias) = later(got, *terms, bias)
    send, own, kept = paired(got, None)
    other = shift(send, 1)
    m_part, d_part = early(own, bias, m_hi, m_lo, d_hi, d_lo)

    solved, *pays = pl.pallas_call(
        functools.partial(middle_kernel, group),
        out_shape=(flat, *[slot] * group),
        in_specs=[VMEM] * 13,
        out_specs=(VMEM,) * (1 + group),
        scratch_shapes=[pltpu.VMEM((2, rows, width), f32)],
        compiler_params=limit(16),
        cost_estimate=cost(3 * mat_flops, 2 * mat_bytes),
        name="level_middle",
    )(
        other, bias, m_hi, m_lo, d_hi, d_lo, m_part, d_part, l_hi, l_lo, share, kept, dest,
    )

    pays, (diag_later,) = later(pays, diag_inv)
    got = exchange(pays)
    near, *sums = summed(got, None)
    sums, (diag_later, rhs_later) = later(sums, diag_later, rhs)
    got = spread(sums)
    sol, d_hi, d_lo, bias = pl.pallas_call(
        functools.partial(last_terms_kernel, parts),
        out_shape=(pltpu.HBM(rhs.shape, f32), term, term, flat),
        in_specs=[HBM, VMEM, HBM, HBM],
        out_specs=(HBM, VMEM, VMEM, VMEM),
        scratch_shapes=[square, sems, pltpu.SemaphoreType.DMA((2,))],
        input_output_aliases={0: 0},
        compiler_params=limit(12),
        cost_estimate=cost(rows * rows, 2 * mat_bytes),
        name="last_terms",
    )(sol, solved, stay(rhs_later), stay(diag_later))
    got, (d_hi, d_lo, bias) = later(got, d_hi, d_lo, bias)
    send, own, total = paired(got, near)
    other = shift(send, 1)
    (d_part,) = early(own, bias, d_hi, d_lo)

    sol, seen = pl.pallas_call(
        functools.partial(last_kernel, group),
        out_shape=(pltpu.HBM(rhs.shape, f32), pltpu.HBM((1, width), f32)),
        in_specs=[HBM] + [VMEM] * 6,
        out_specs=(HBM, HBM),
        scratch_shapes=[block, pltpu.SemaphoreType.DMA((2,))],
        input_output_aliases={0: 0},
        compiler_params=limit(8),
        cost_estimate=cost(mat_flops, mat_bytes),
        name="level_last",
    )(sol, other, bias, d_hi, d_lo, d_part, total)
    return sol, seen.reshape(width)


def solution(mesh):
    in_specs = (
        P(None, "rows", "parts"),
        P(None, "rows", None),
        P(None, "rows", None, None),
        P(None, "rows", None),
        P("rows"),
    )
    out_specs = (P(None, "rows", "parts"), P("parts"))
    return jax.shard_map(body, mesh=mesh, in_specs=in_specs, out_specs=out_specs, check_vma=False)
```

```python
import functools

import jax
import jax.numpy as jnp
from jax import lax
from jax.experimental import pallas as pl
from jax.experimental.pallas import tpu as pltpu
from jax.sharding import PartitionSpec as P

LANES = 128
SUB = 8
CUTS = (4, 1, 1)
HBM = pl.BlockSpec(memory_space=pltpu.HBM)
ANY = pl.BlockSpec(memory_space=pl.ANY)
VMEM = pl.BlockSpec(memory_space=pltpu.VMEM)
SMEM = pl.BlockSpec(memory_space=pltpu.SMEM)


def split(x):
    hi = x.astype(jnp.bfloat16)
    lo = (x - hi.astype(jnp.float32)).astype(jnp.bfloat16)
    return hi, lo


def split_cols(x):
    hi, lo = split(x)
    return jnp.concatenate([hi, lo], axis=1)


def dot_terms(hi, lo, both):
    width = both.shape[1] // 2
    wide = jnp.dot(hi, both, preferred_element_type=jnp.float32)
    narrow = jnp.dot(lo, both[:, :width], preferred_element_type=jnp.float32)
    return wide[:, :width] + (wide[:, width:] + narrow)


def left_product(vector, matrix, rows):
    columns = vector.T
    total = None
    for r in range(rows // LANES):
        block = matrix[r * LANES : (r + 1) * LANES, :]
        term = jnp.sum(columns[:, r : r + 1] * block, axis=0, keepdims=True)
        total = term if total is None else total + term
    return total


def chunked(ref, buf, sem, parts):
    size = buf.shape[0] // parts
    copies = []
    for c in range(parts):
        at = pl.ds(c * size, size)
        copies.append(pltpu.make_async_copy(ref.at[at], buf.at[at], sem.at[c]))
    return copies


def position(group):
    place = lax.axis_index("rows")
    return lax.rem(place, group), place // 2, lax.rem(place, 2)


def deal(product, k, outs, spot, seg):
    lanes = len(outs) // 2
    for r, out in enumerate(outs):
        there = spot ^ r
        first = (lax.rem(there, 2) * lanes + there // 2) * seg
        out[pl.ds(k * seg, seg), :] = product[pl.ds(pl.multiple_of(first, SUB), seg), :]


def tile_of(lines, extra):
    if extra > len(lines):
        lines = [*lines, jnp.zeros((extra - len(lines), LANES), jnp.float32)]
    return jnp.concatenate(lines, axis=0)


def named(dest, level):
    return [jnp.full((1, LANES), dest[level, 0, k].astype(jnp.float32)) for k in range(2)]


def first_kernel(group, cuts, rhs, diag, tiles, dest, solved, *refs):
    outs, refs = refs[:group], refs[group:]
    b_buf, d_buf, l_buf, p_buf, i_buf, small, d_sem, l0_sem, l1_sem = refs
    rows = b_buf.shape[0]
    seg = rows // group
    spot, _, _ = position(group)
    d_copies = chunked(diag.at[0], d_buf, d_sem, cuts[0])
    l_copies = [
        chunked(tiles.at[0, 0], l_buf.at[0], l0_sem, cuts[1]),
        chunked(tiles.at[0, 1], l_buf.at[1], l1_sem, cuts[2]),
    ]
    b_copy = pltpu.make_async_copy(rhs.at[0], b_buf, small.at[0])
    i_copy = pltpu.make_async_copy(dest, i_buf, small.at[1])
    b_copy.start()
    for copies in (d_copies, *l_copies):
        for copy in copies:
            copy.start()
    i_copy.start()
    b_copy.wait()
    both = split_cols(b_buf[...])
    size = rows // cuts[0]
    for c in range(cuts[0]):
        at = pl.ds(c * size, size)
        d_copies[c].wait()
        solved[at, :] = dot_terms(*split(d_buf[at, :]), both)
    i_copy.wait()
    base = 2 * seg
    extra = outs[0].shape[0] - base
    meta = tile_of(named(i_buf, 0), extra)
    for out in outs:
        out[pl.ds(base, extra), :] = meta
    both = split_cols(solved[...])
    for k in range(2):
        size = rows // cuts[1 + k]
        for c in range(cuts[1 + k]):
            at = pl.ds(c * size, size)
            l_copies[k][c].wait()
            p_buf[k, at, :] = dot_terms(*split(l_buf[k, at, :]), both)
        deal(p_buf.at[k], k, outs, spot, seg)


def vector_kernel(rhs, diag, weight, solved, sol, v_tile, share, b_buf, v_buf, w_buf, sem):
    rows = b_buf.shape[0]
    copies = [
        pltpu.make_async_copy(weight, w_buf, sem.at[0]),
        pltpu.make_async_copy(rhs.at[2], b_buf, sem.at[1]),
        pltpu.make_async_copy(diag.at[2], v_buf, sem.at[2]),
        pltpu.make_async_copy(solved, sol.at[0], sem.at[3]),
    ]
    for copy in copies:
        copy.start()
    for copy in copies:
        copy.wait()
    vector = left_product(w_buf[...], v_buf, rows)
    count = rows // LANES
    lines = [vector[:, r * LANES : (r + 1) * LANES] for r in range(count)]
    v_tile[...] = tile_of(lines, v_tile.shape[0])
    share[...] = left_product(v_tile[0:count, :], b_buf, rows)


def fold_kernel(rhs, diag, tiles, m_hi, m_lo, d_hi, d_lo, l_hi, l_lo, bias,
                d_buf, l_buf, d_sem, l_sem, b_sem):
    rows = d_buf.shape[0]
    parts = d_sem.shape[0]
    size = rows // parts
    d_copies = chunked(diag.at[1], d_buf, d_sem, parts)
    l_copies = [chunked(tiles.at[1, 1 - k], l_buf.at[k], l_sem.at[k], parts) for k in range(2)]
    b_copy = pltpu.make_async_copy(rhs.at[1], bias, b_sem)
    for copy in (*d_copies, *l_copies[0], *l_copies[1], b_copy):
        copy.start()
    for copy in d_copies:
        copy.wait()
    hi, lo = split(d_buf[...])
    d_hi[...] = hi
    d_lo[...] = lo
    both = jnp.concatenate([hi, lo], axis=1)
    for c in range(parts):
        at = pl.ds(c * size, size)
        l_copies[0][c].wait()
        hi, lo = split(dot_terms(*split(l_buf[0, at, :]), both))
        m_hi[at, :] = hi
        m_lo[at, :] = lo
    for copy in l_copies[1]:
        copy.wait()
    hi, lo = split(l_buf[1])
    l_hi[...] = hi
    l_lo[...] = lo
    b_copy.wait()


def sum_kernel(group, mode, *refs):
    refs = list(refs)
    v_tile = refs.pop(0) if mode == "first" else None
    order = [*near_order(group), 0]
    got, refs = [refs[order.index(r)] for r in range(group)], refs[group:]
    near = None if mode == "first" else refs.pop(0)
    chips = group
    outs, (out, tiles) = refs[:chips], refs[chips:]
    seg = out.shape[1]
    base = 2 * seg
    spot, chip, _ = position(group)
    targets = []
    for r in range(group):
        rows = got[r][base : base + SUB, :]
        targets.append([rows[k, 0].astype(jnp.int32) for k in range(2)])
    out[...] = jnp.zeros_like(out)
    if near is None:
        for r in range(chips):
            outs[r][pl.ds(base, v_tile.shape[0]), :] = v_tile[...]
    else:
        for r in range(group):
            tiles[spot ^ r] = got[r][base : base + SUB, :]
        total = tiles[0, 2:3, :]
        for q in range(1, group):
            total = total + tiles[q, 2:3, :]
        near[...] = total
        outs[chips - 1][pl.ds(base, SUB), :] = jnp.broadcast_to(total, (SUB, LANES))
    for r in range(group):
        for k in range(2):
            out[targets[r][k]] += got[r][pl.ds(k * seg, seg), :]
    for r in range(chips):
        for j in range(2):
            outs[r][pl.ds(j * seg, seg), :] = out[2 * (chip ^ r) + j]


def pair_kernel(chips, mode, *refs):
    near = None if mode == "first" else refs[0]
    refs = refs if mode == "first" else refs[1:]
    got, refs = refs[:chips][::-1], refs[chips:]
    send, own, more = refs
    lanes = chips // 2
    seg = own.shape[0] // lanes
    _, chip, core = position(chips)
    mine, theirs = pl.multiple_of(core * seg, SUB), pl.multiple_of((1 - core) * seg, SUB)
    for r in range(lanes):
        q = lax.rem(chip, lanes) ^ r
        a, b = got[r], got[r + lanes]
        at = pl.ds(pl.multiple_of(q * seg, SUB), seg)
        own[at, :] = a[pl.ds(mine, seg), :] + b[pl.ds(mine, seg), :]
        send[at, :] = a[pl.ds(theirs, seg), :] + b[pl.ds(theirs, seg), :]
    if mode == "first":
        extra = more.shape[1]
        for r in range(chips):
            tile = got[r][2 * seg :, :]
            more[chip ^ r] = tile
            at = pl.ds(pl.multiple_of(lanes * seg + (chip ^ r) * extra, SUB), extra)
            send[at, :] = tile
    else:
        more[...] = near[...] + got[chips - 1][2 * seg : 2 * seg + 1, :]


def own_part(group, which, own, bias, *refs):
    core = position(group)[2]
    depth = bias.shape[0] // 2
    at = pl.ds(pl.multiple_of((core if which == 0 else 1 - core) * depth, depth), depth)
    both = split_cols(bias[at, :] - own[0:depth, :])
    return [dot_terms(refs[j][:, at], refs[j + 1][:, at], both) for j in range(0, len(refs), 2)]


def early_kernel(group, *refs):
    count = (len(refs) - 2) // 3
    outs = refs[-count:]
    for out, value in zip(outs, own_part(group, 0, *refs[:-count])):
        out[...] = value


def middle_kernel(group, other, bias, m_hi, m_lo, d_hi, d_lo, m_part, d_part, l_hi, l_lo,
                  share, kept, dest, solved, *refs):
    outs, (p_buf,) = refs[:group], refs[group:]
    rows = bias.shape[0]
    seg = rows // group
    count = rows // LANES
    extra_v = kept.shape[1]
    offset = rows // 2
    spot, _, core = position(group)
    names = dest[1]
    targets = [names[0, k] for k in range(2)]
    product, value = own_part(group, 1, other, bias, m_hi, m_lo, d_hi, d_lo)
    value = value + d_part[...]
    solved[...] = value
    both = split_cols(value)
    p_buf[1] = product + m_part[...]
    p_buf[0] = dot_terms(l_hi[...], l_lo[...], both)
    part = share[...]
    for k in (1, 0):
        deal(p_buf.at[k], k, outs, spot, seg)
        here = kept[targets[k] // 2]
        at = pl.ds(pl.multiple_of(offset + (targets[k] // 2) * extra_v, SUB), extra_v)
        vector = jnp.where(lax.rem(targets[k], 2) == core, here, other[at, :])
        part = part - left_product(vector[0:count, :], p_buf.at[k], rows)
    base = 2 * seg
    extra = outs[0].shape[0] - base
    lines = [jnp.full((1, LANES), target.astype(jnp.float32)) for target in targets]
    meta = tile_of([*lines, part], extra)
    for out in outs:
        out[pl.ds(base, extra), :] = meta


def last_terms_kernel(parts, sol_in, solved, rhs, diag, sol, d_hi, d_lo, bias,
                      d_buf, d_sem, b_sem):
    rows = d_buf.shape[0]
    copies = chunked(diag.at[2], d_buf, d_sem, parts)
    b_copy = pltpu.make_async_copy(rhs.at[2], bias, b_sem.at[0])
    y_copy = pltpu.make_async_copy(solved, sol.at[1], b_sem.at[1])
    for copy in (*copies, b_copy, y_copy):
        copy.start()
    size = rows // parts
    for c in range(parts):
        at = pl.ds(c * size, size)
        copies[c].wait()
        hi, lo = split(d_buf[at, :])
        d_hi[at, :] = hi
        d_lo[at, :] = lo
    b_copy.wait()
    y_copy.wait()


def last_kernel(group, sol_in, other, bias, d_hi, d_lo, part, total, sol, seen, y_buf, sem):
    total_copy = pltpu.make_async_copy(total, seen, sem.at[2])
    total_copy.start()
    half = y_buf.shape[0] // 2
    copies = []
    for c in range(2):
        at = pl.ds(c * half, half)
        (value,) = own_part(group, 1, other, bias, d_hi.at[at], d_lo.at[at])
        y_buf[at, :] = value + part[at, :]
        copies.append(pltpu.make_async_copy(y_buf.at[at], sol.at[2, at], sem.at[c]))
        copies[c].start()
    total_copy.wait()
    for copy in copies:
        copy.wait()


def cost(flops, size):
    return pl.CostEstimate(flops=flops, bytes_accessed=size, transcendentals=0)


def limit(mib):
    return pltpu.CompilerParams(vmem_limit_bytes=mib << 20)


def stay(x):
    return pltpu.with_memory_space_constraint(x, pltpu.HBM)


def near_order(group):
    chips = (group - 2, *range(2, group - 2, 2))
    return [r + c for c in range(2) for r in chips] + [1]


def later(first, *others):
    tied = lax.optimization_barrier((tuple(first), tuple(others)))
    return list(tied[0]), tied[1]


def body(rhs, diag_inv, tiles, dest, obs_weight):
    count = lax.axis_size("rows")
    group = count // 2
    chips = count // 2
    levels, rows, width = rhs.shape
    seg = rows // group
    lines = rows // LANES
    extra = -(-lines // SUB) * SUB
    parts = 2
    f32 = jnp.float32
    def shift(x, bits):
        return lax.ppermute(x, "rows", [(i, i ^ bits) for i in range(count)])

    block = pltpu.VMEM((rows, width), f32)
    square = pltpu.VMEM((rows, rows), f32)
    sems = pltpu.SemaphoreType.DMA((parts,))
    term = jax.ShapeDtypeStruct((rows, rows), jnp.bfloat16)
    line = jax.ShapeDtypeStruct((1, width), f32)
    flat = jax.ShapeDtypeStruct((rows, width), f32)
    slot = jax.ShapeDtypeStruct((2 * seg + SUB, width), f32)
    mat_flops = 2 * rows * rows * width
    mat_bytes = 4 * rows * rows

    def exchange(pays):
        return [shift(pays[r], r) for r in near_order(group)] + [pays[0]]

    def spread(sums):
        return [shift(sums[r], 2 * r) for r in range(chips - 1, 0, -1)] + [sums[0]]

    def summed(got, v_tile):
        mode = "last" if v_tile is None else "first"
        tall = [2 * seg + (0 if v_tile is None else extra)] * chips
        if v_tile is None:
            tall[chips - 1] += SUB
        shapes = [jax.ShapeDtypeStruct((t, width), f32) for t in tall]
        given = list(got)
        if v_tile is None:
            shapes = [line, *shapes]
        else:
            given = [v_tile, *given]
        return pl.pallas_call(
            functools.partial(sum_kernel, group, mode),
            out_shape=tuple(shapes),
            in_specs=[VMEM] * len(given),
            out_specs=(VMEM,) * len(shapes),
            scratch_shapes=[
                pltpu.VMEM((count, seg, width), f32),
                pltpu.VMEM((group, SUB, width), f32),
            ],
            compiler_params=limit(6),
            cost_estimate=cost(2 * rows * width, 4 * 4 * rows * width),
            name="sum_parts",
        )(*given)

    def paired(got, near):
        mode = "first" if near is None else "last"
        lanes = chips // 2
        tall = lanes * seg + (chips * extra if near is None else 0)
        shapes = [jax.ShapeDtypeStruct((tall, width), f32)]
        shapes.append(jax.ShapeDtypeStruct((lanes * seg, width), f32))
        more = jax.ShapeDtypeStruct((chips, extra, width), f32)
        shapes.append(more if near is None else line)
        given = got if near is None else [near, *got]
        return pl.pallas_call(
            functools.partial(pair_kernel, chips, mode),
            out_shape=tuple(shapes),
            in_specs=[VMEM] * len(given),
            out_specs=(VMEM,) * len(shapes),
            compiler_params=limit(4),
            cost_estimate=cost(2 * rows * width, 4 * 3 * rows * width),
            name="pair_halves",
        )(*given)

    def early(own, bias, *terms):
        return pl.pallas_call(
            functools.partial(early_kernel, group),
            out_shape=(flat,) * (len(terms) // 2),
            in_specs=[VMEM] * (2 + len(terms)),
            out_specs=(VMEM,) * (len(terms) // 2),
            compiler_params=limit(8),
            cost_estimate=cost(len(terms) * mat_flops, len(terms) * mat_bytes // 4),
            name="own_columns",
        )(own, bias, *terms)

    cuts = CUTS
    solved, *pays = pl.pallas_call(
        functools.partial(first_kernel, group, cuts),
        out_shape=(flat, *[slot] * group),
        in_specs=[HBM, HBM, HBM, HBM],
        out_specs=(VMEM,) * (1 + group),
        scratch_shapes=[
            block, square, pltpu.VMEM((2, rows, rows), f32), pltpu.VMEM((2, rows, width), f32),
            pltpu.SMEM(dest.shape, jnp.int32), pltpu.SemaphoreType.DMA((2,)),
            *[pltpu.SemaphoreType.DMA((cut,)) for cut in cuts],
        ],
        compiler_params=limit(24),
        cost_estimate=cost(3 * mat_flops, 3 * mat_bytes),
        name="level_first",
    )(stay(rhs), stay(diag_inv), stay(tiles), stay(dest))

    pays, (diag_later, rhs_later) = later(pays, diag_inv, rhs)
    got = exchange(pays)
    sol, v_tile, share = pl.pallas_call(
        vector_kernel,
        out_shape=(
            pltpu.HBM(rhs.shape, f32), jax.ShapeDtypeStruct((extra, width), f32), line,
        ),
        in_specs=[HBM, HBM, HBM, VMEM],
        out_specs=(HBM, VMEM, VMEM),
        scratch_shapes=[
            block, square, pltpu.VMEM((lines, LANES), f32), pltpu.SemaphoreType.DMA((4,)),
        ],
        compiler_params=limit(8),
        cost_estimate=cost(4 * rows * rows, mat_bytes),
        name="vector",
    )(stay(rhs_later), stay(diag_later), stay(obs_weight.reshape(lines, LANES)), solved)
    sums = summed(got, v_tile)

    sums, (diag_later, tiles_later, rhs_later) = later(sums, diag_inv, tiles, rhs)
    got = spread(sums)
    *terms, bias = pl.pallas_call(
        fold_kernel,
        out_shape=(*[term] * 6, flat),
        in_specs=[HBM, HBM, HBM],
        out_specs=(VMEM,) * 7,
        scratch_shapes=[
            square, pltpu.VMEM((2, rows, rows), f32), sems,
            pltpu.SemaphoreType.DMA((2, parts)), pltpu.SemaphoreType.DMA,
        ],
        compiler_params=limit(32),
        cost_estimate=cost(3 * rows * mat_flops // width, 3 * mat_bytes),
        name="fold_levels",
    )(stay(rhs_later), stay(diag_later), stay(tiles_later))
    m_hi, m_lo, d_hi, d_lo, l_hi, l_lo = terms
    got, (m_hi, m_lo, d_hi, d_lo, l_hi, l_lo, bias) = later(got, *terms, bias)
    send, own, kept = paired(got, None)
    other = shift(send, 1)
    m_part, d_part = early(own, bias, m_hi, m_lo, d_hi, d_lo)

    solved, *pays = pl.pallas_call(
        functools.partial(middle_kernel, group),
        out_shape=(flat, *[slot] * group),
        in_specs=[VMEM] * 13,
        out_specs=(VMEM,) * (1 + group),
        scratch_shapes=[pltpu.VMEM((2, rows, width), f32)],
        compiler_params=limit(16),
        cost_estimate=cost(3 * mat_flops, 2 * mat_bytes),
        name="level_middle",
    )(
        other, bias, m_hi, m_lo, d_hi, d_lo, m_part, d_part, l_hi, l_lo, share, kept, dest,
    )

    pays, (diag_later,) = later(pays, diag_inv)
    got = exchange(pays)
    near, *sums = summed(got, None)
    sums, (diag_later, rhs_later) = later(sums, diag_later, rhs)
    got = spread(sums)
    sol, d_hi, d_lo, bias = pl.pallas_call(
        functools.partial(last_terms_kernel, parts),
        out_shape=(pltpu.HBM(rhs.shape, f32), term, term, flat),
        in_specs=[HBM, VMEM, HBM, HBM],
        out_specs=(HBM, VMEM, VMEM, VMEM),
        scratch_shapes=[square, sems, pltpu.SemaphoreType.DMA((2,))],
        input_output_aliases={0: 0},
        compiler_params=limit(12),
        cost_estimate=cost(rows * rows, 2 * mat_bytes),
        name="last_terms",
    )(sol, solved, stay(rhs_later), stay(diag_later))
    got, (d_hi, d_lo, bias) = later(got, d_hi, d_lo, bias)
    send, own, total = paired(got, near)
    other = shift(send, 1)
    (d_part,) = early(own, bias, d_hi, d_lo)

    sol, seen = pl.pallas_call(
        functools.partial(last_kernel, group),
        out_shape=(pltpu.HBM(rhs.shape, f32), pltpu.HBM((1, width), f32)),
        in_specs=[HBM] + [VMEM] * 6,
        out_specs=(HBM, HBM),
        scratch_shapes=[block, pltpu.SemaphoreType.DMA((3,))],
        input_output_aliases={0: 0},
        compiler_params=limit(8),
        cost_estimate=cost(mat_flops, mat_bytes),
        name="level_last",
    )(sol, other, bias, d_hi, d_lo, d_part, total)
    return sol, seen.reshape(width)


def solution(mesh):
    in_specs = (
        P(None, "rows", "parts"),
        P(None, "rows", None),
        P(None, "rows", None, None),
        P(None, "rows", None),
        P("rows"),
    )
    out_specs = (P(None, "rows", "parts"), P("parts"))
    return jax.shard_map(body, mesh=mesh, in_specs=in_specs, out_specs=out_specs, check_vma=False)
```

```python
import functools

import jax
import jax.numpy as jnp
from jax import lax
from jax.experimental import pallas as pl
from jax.experimental.pallas import tpu as pltpu
from jax.sharding import PartitionSpec as P

LANES = 128
SUB = 8
CUTS = (4, 1, 1)
HBM = pl.BlockSpec(memory_space=pltpu.HBM)
ANY = pl.BlockSpec(memory_space=pl.ANY)
VMEM = pl.BlockSpec(memory_space=pltpu.VMEM)
SMEM = pl.BlockSpec(memory_space=pltpu.SMEM)


def split(x):
    hi = x.astype(jnp.bfloat16)
    lo = (x - hi.astype(jnp.float32)).astype(jnp.bfloat16)
    return hi, lo


def split_cols(x):
    hi, lo = split(x)
    return jnp.concatenate([hi, lo], axis=1)


def dot_terms(hi, lo, both):
    width = both.shape[1] // 2
    wide = jnp.dot(hi, both, preferred_element_type=jnp.float32)
    narrow = jnp.dot(lo, both[:, :width], preferred_element_type=jnp.float32)
    return wide[:, :width] + (wide[:, width:] + narrow)


def left_product(vector, matrix, rows):
    columns = vector.T
    total = None
    for r in range(rows // LANES):
        block = matrix[r * LANES : (r + 1) * LANES, :]
        term = jnp.sum(columns[:, r : r + 1] * block, axis=0, keepdims=True)
        total = term if total is None else total + term
    return total


def chunked(ref, buf, sem, parts):
    size = buf.shape[0] // parts
    copies = []
    for c in range(parts):
        at = pl.ds(c * size, size)
        copies.append(pltpu.make_async_copy(ref.at[at], buf.at[at], sem.at[c]))
    return copies


def position(group):
    place = lax.axis_index("rows")
    return lax.rem(place, group), place // 2, lax.rem(place, 2)


def deal(product, k, outs, spot, seg):
    lanes = len(outs) // 2
    for r, out in enumerate(outs):
        there = spot ^ r
        first = (lax.rem(there, 2) * lanes + there // 2) * seg
        out[pl.ds(k * seg, seg), :] = product[pl.ds(pl.multiple_of(first, SUB), seg), :]


def tile_of(lines, extra):
    if extra > len(lines):
        lines = [*lines, jnp.zeros((extra - len(lines), LANES), jnp.float32)]
    return jnp.concatenate(lines, axis=0)


def named(dest, level):
    return [jnp.full((1, LANES), dest[level, 0, k].astype(jnp.float32)) for k in range(2)]


def first_kernel(group, cuts, rhs, diag, tiles, dest, solved, *refs):
    outs, refs = refs[:group], refs[group:]
    b_buf, d_buf, l_buf, p_buf, i_buf, small, d_sem, l0_sem, l1_sem = refs
    rows = b_buf.shape[0]
    seg = rows // group
    spot, _, _ = position(group)
    d_copies = chunked(diag.at[0], d_buf, d_sem, cuts[0])
    l_copies = [
        chunked(tiles.at[0, 0], l_buf.at[0], l0_sem, cuts[1]),
        chunked(tiles.at[0, 1], l_buf.at[1], l1_sem, cuts[2]),
    ]
    b_copy = pltpu.make_async_copy(rhs.at[0], b_buf, small.at[0])
    i_copy = pltpu.make_async_copy(dest, i_buf, small.at[1])
    b_copy.start()
    for copies in (d_copies, *l_copies):
        for copy in copies:
            copy.start()
    i_copy.start()
    b_copy.wait()
    both = split_cols(b_buf[...])
    size = rows // cuts[0]
    for c in range(cuts[0]):
        at = pl.ds(c * size, size)
        d_copies[c].wait()
        solved[at, :] = dot_terms(*split(d_buf[at, :]), both)
    i_copy.wait()
    base = 2 * seg
    extra = outs[0].shape[0] - base
    meta = tile_of(named(i_buf, 0), extra)
    for out in outs:
        out[pl.ds(base, extra), :] = meta
    both = split_cols(solved[...])
    for k in range(2):
        size = rows // cuts[1 + k]
        for c in range(cuts[1 + k]):
            at = pl.ds(c * size, size)
            l_copies[k][c].wait()
            p_buf[k, at, :] = dot_terms(*split(l_buf[k, at, :]), both)
        deal(p_buf.at[k], k, outs, spot, seg)


def vector_kernel(rhs, diag, weight, solved, sol, v_tile, share, b_buf, v_buf, w_buf, sem):
    rows = b_buf.shape[0]
    copies = [
        pltpu.make_async_copy(weight, w_buf, sem.at[0]),
        pltpu.make_async_copy(rhs.at[2], b_buf, sem.at[1]),
        pltpu.make_async_copy(diag.at[2], v_buf, sem.at[2]),
        pltpu.make_async_copy(solved, sol.at[0], sem.at[3]),
    ]
    for copy in copies:
        copy.start()
    for copy in copies:
        copy.wait()
    vector = left_product(w_buf[...], v_buf, rows)
    count = rows // LANES
    lines = [vector[:, r * LANES : (r + 1) * LANES] for r in range(count)]
    v_tile[...] = tile_of(lines, v_tile.shape[0])
    share[...] = left_product(v_tile[0:count, :], b_buf, rows)


def fold_kernel(rhs, diag, tiles, m_hi, m_lo, d_hi, d_lo, l_hi, l_lo, bias,
                d_buf, l_buf, d_sem, l_sem, b_sem):
    rows = d_buf.shape[0]
    parts = d_sem.shape[0]
    size = rows // parts
    d_copies = chunked(diag.at[1], d_buf, d_sem, parts)
    l_copies = [chunked(tiles.at[1, 1 - k], l_buf.at[k], l_sem.at[k], parts) for k in range(2)]
    b_copy = pltpu.make_async_copy(rhs.at[1], bias, b_sem)
    for copy in (*d_copies, *l_copies[0], *l_copies[1], b_copy):
        copy.start()
    for copy in d_copies:
        copy.wait()
    hi, lo = split(d_buf[...])
    d_hi[...] = hi
    d_lo[...] = lo
    both = jnp.concatenate([hi, lo], axis=1)
    for c in range(parts):
        at = pl.ds(c * size, size)
        l_copies[0][c].wait()
        hi, lo = split(dot_terms(*split(l_buf[0, at, :]), both))
        m_hi[at, :] = hi
        m_lo[at, :] = lo
    for copy in l_copies[1]:
        copy.wait()
    hi, lo = split(l_buf[1])
    l_hi[...] = hi
    l_lo[...] = lo
    b_copy.wait()


def sum_kernel(group, mode, *refs):
    refs = list(refs)
    v_tile = refs.pop(0) if mode == "first" else None
    order = [*near_order(group), 0]
    got, refs = [refs[order.index(r)] for r in range(group)], refs[group:]
    near = None if mode == "first" else refs.pop(0)
    chips = group
    outs, (out, tiles) = refs[:chips], refs[chips:]
    seg = out.shape[1]
    base = 2 * seg
    spot, chip, _ = position(group)
    targets = []
    for r in range(group):
        rows = got[r][base : base + SUB, :]
        targets.append([rows[k, 0].astype(jnp.int32) for k in range(2)])
    out[...] = jnp.zeros_like(out)
    if near is None:
        for r in range(chips):
            outs[r][pl.ds(base, v_tile.shape[0]), :] = v_tile[...]
    else:
        for r in range(group):
            tiles[spot ^ r] = got[r][base : base + SUB, :]
        total = tiles[0, 2:3, :]
        for q in range(1, group):
            total = total + tiles[q, 2:3, :]
        near[...] = total
        outs[chips - 2][pl.ds(base, SUB), :] = jnp.broadcast_to(total, (SUB, LANES))
    for r in range(group):
        for k in range(2):
            out[targets[r][k]] += got[r][pl.ds(k * seg, seg), :]
    for r in range(chips):
        for j in range(2):
            outs[r][pl.ds(j * seg, seg), :] = out[2 * (chip ^ r) + j]


def pair_kernel(chips, mode, *refs):
    near = None if mode == "first" else refs[0]
    refs = refs if mode == "first" else refs[1:]
    order = [*far_order(chips), 0]
    got, refs = [refs[order.index(r)] for r in range(chips)], refs[chips:]
    send, own, more = refs
    lanes = chips // 2
    seg = own.shape[0] // lanes
    _, chip, core = position(chips)
    mine, theirs = pl.multiple_of(core * seg, SUB), pl.multiple_of((1 - core) * seg, SUB)
    for r in range(lanes):
        q = lax.rem(chip, lanes) ^ r
        a, b = got[r], got[r + lanes]
        at = pl.ds(pl.multiple_of(q * seg, SUB), seg)
        own[at, :] = a[pl.ds(mine, seg), :] + b[pl.ds(mine, seg), :]
        send[at, :] = a[pl.ds(theirs, seg), :] + b[pl.ds(theirs, seg), :]
    if mode == "first":
        extra = more.shape[1]
        for r in range(chips):
            tile = got[r][2 * seg :, :]
            more[chip ^ r] = tile
            at = pl.ds(pl.multiple_of(lanes * seg + (chip ^ r) * extra, SUB), extra)
            send[at, :] = tile
    else:
        more[...] = near[...] + got[chips - 2][2 * seg : 2 * seg + 1, :]


def own_part(group, which, own, bias, *refs):
    core = position(group)[2]
    depth = bias.shape[0] // 2
    at = pl.ds(pl.multiple_of((core if which == 0 else 1 - core) * depth, depth), depth)
    both = split_cols(bias[at, :] - own[0:depth, :])
    return [dot_terms(refs[j][:, at], refs[j + 1][:, at], both) for j in range(0, len(refs), 2)]


def early_kernel(group, *refs):
    count = (len(refs) - 2) // 3
    outs = refs[-count:]
    for out, value in zip(outs, own_part(group, 0, *refs[:-count])):
        out[...] = value


def middle_kernel(group, other, bias, m_hi, m_lo, d_hi, d_lo, m_part, d_part, l_hi, l_lo,
                  share, kept, dest, solved, *refs):
    outs, (p_buf,) = refs[:group], refs[group:]
    rows = bias.shape[0]
    seg = rows // group
    count = rows // LANES
    extra_v = kept.shape[1]
    offset = rows // 2
    spot, _, core = position(group)
    names = dest[1]
    targets = [names[0, k] for k in range(2)]
    product, value = own_part(group, 1, other, bias, m_hi, m_lo, d_hi, d_lo)
    value = value + d_part[...]
    solved[...] = value
    both = split_cols(value)
    p_buf[1] = product + m_part[...]
    p_buf[0] = dot_terms(l_hi[...], l_lo[...], both)
    part = share[...]
    for k in (1, 0):
        deal(p_buf.at[k], k, outs, spot, seg)
        here = kept[targets[k] // 2]
        at = pl.ds(pl.multiple_of(offset + (targets[k] // 2) * extra_v, SUB), extra_v)
        vector = jnp.where(lax.rem(targets[k], 2) == core, here, other[at, :])
        part = part - left_product(vector[0:count, :], p_buf.at[k], rows)
    base = 2 * seg
    extra = outs[0].shape[0] - base
    lines = [jnp.full((1, LANES), target.astype(jnp.float32)) for target in targets]
    meta = tile_of([*lines, part], extra)
    for out in outs:
        out[pl.ds(base, extra), :] = meta


def last_terms_kernel(parts, sol_in, solved, rhs, diag, sol, d_hi, d_lo, bias,
                      d_buf, d_sem, b_sem):
    rows = d_buf.shape[0]
    copies = chunked(diag.at[2], d_buf, d_sem, parts)
    b_copy = pltpu.make_async_copy(rhs.at[2], bias, b_sem.at[0])
    y_copy = pltpu.make_async_copy(solved, sol.at[1], b_sem.at[1])
    for copy in (*copies, b_copy, y_copy):
        copy.start()
    size = rows // parts
    for c in range(parts):
        at = pl.ds(c * size, size)
        copies[c].wait()
        hi, lo = split(d_buf[at, :])
        d_hi[at, :] = hi
        d_lo[at, :] = lo
    b_copy.wait()
    y_copy.wait()


def last_kernel(group, sol_in, other, bias, d_hi, d_lo, part, total, sol, seen, y_buf, sem):
    total_copy = pltpu.make_async_copy(total, seen, sem.at[2])
    total_copy.start()
    half = y_buf.shape[0] // 2
    copies = []
    for c in range(2):
        at = pl.ds(c * half, half)
        (value,) = own_part(group, 1, other, bias, d_hi.at[at], d_lo.at[at])
        y_buf[at, :] = value + part[at, :]
        copies.append(pltpu.make_async_copy(y_buf.at[at], sol.at[2, at], sem.at[c]))
        copies[c].start()
    total_copy.wait()
    for copy in copies:
        copy.wait()


def cost(flops, size):
    return pl.CostEstimate(flops=flops, bytes_accessed=size, transcendentals=0)


def limit(mib):
    return pltpu.CompilerParams(vmem_limit_bytes=mib << 20)


def stay(x):
    return pltpu.with_memory_space_constraint(x, pltpu.HBM)


def near_order(group):
    chips = (group - 2, *range(2, group - 2, 2))
    return [r + c for c in range(2) for r in chips] + [1]


def far_order(chips):
    return [chips - 2, chips - 1, *range(chips - 3, 0, -1)]


def later(first, *others):
    tied = lax.optimization_barrier((tuple(first), tuple(others)))
    return list(tied[0]), tied[1]


def body(rhs, diag_inv, tiles, dest, obs_weight):
    count = lax.axis_size("rows")
    group = count // 2
    chips = count // 2
    levels, rows, width = rhs.shape
    seg = rows // group
    lines = rows // LANES
    extra = -(-lines // SUB) * SUB
    parts = 2
    f32 = jnp.float32
    def shift(x, bits):
        return lax.ppermute(x, "rows", [(i, i ^ bits) for i in range(count)])

    block = pltpu.VMEM((rows, width), f32)
    square = pltpu.VMEM((rows, rows), f32)
    sems = pltpu.SemaphoreType.DMA((parts,))
    term = jax.ShapeDtypeStruct((rows, rows), jnp.bfloat16)
    line = jax.ShapeDtypeStruct((1, width), f32)
    flat = jax.ShapeDtypeStruct((rows, width), f32)
    slot = jax.ShapeDtypeStruct((2 * seg + SUB, width), f32)
    mat_flops = 2 * rows * rows * width
    mat_bytes = 4 * rows * rows

    def exchange(pays):
        return [shift(pays[r], r) for r in near_order(group)] + [pays[0]]

    def spread(sums):
        return [shift(sums[r], 2 * r) for r in far_order(chips)] + [sums[0]]

    def summed(got, v_tile):
        mode = "last" if v_tile is None else "first"
        tall = [2 * seg + (0 if v_tile is None else extra)] * chips
        if v_tile is None:
            tall[chips - 2] += SUB
        shapes = [jax.ShapeDtypeStruct((t, width), f32) for t in tall]
        given = list(got)
        if v_tile is None:
            shapes = [line, *shapes]
        else:
            given = [v_tile, *given]
        return pl.pallas_call(
            functools.partial(sum_kernel, group, mode),
            out_shape=tuple(shapes),
            in_specs=[VMEM] * len(given),
            out_specs=(VMEM,) * len(shapes),
            scratch_shapes=[
                pltpu.VMEM((count, seg, width), f32),
                pltpu.VMEM((group, SUB, width), f32),
            ],
            compiler_params=limit(6),
            cost_estimate=cost(2 * rows * width, 4 * 4 * rows * width),
            name="sum_parts",
        )(*given)

    def paired(got, near):
        mode = "first" if near is None else "last"
        lanes = chips // 2
        tall = lanes * seg + (chips * extra if near is None else 0)
        shapes = [jax.ShapeDtypeStruct((tall, width), f32)]
        shapes.append(jax.ShapeDtypeStruct((lanes * seg, width), f32))
        more = jax.ShapeDtypeStruct((chips, extra, width), f32)
        shapes.append(more if near is None else line)
        given = got if near is None else [near, *got]
        return pl.pallas_call(
            functools.partial(pair_kernel, chips, mode),
            out_shape=tuple(shapes),
            in_specs=[VMEM] * len(given),
            out_specs=(VMEM,) * len(shapes),
            compiler_params=limit(4),
            cost_estimate=cost(2 * rows * width, 4 * 3 * rows * width),
            name="pair_halves",
        )(*given)

    def early(own, bias, *terms):
        return pl.pallas_call(
            functools.partial(early_kernel, group),
            out_shape=(flat,) * (len(terms) // 2),
            in_specs=[VMEM] * (2 + len(terms)),
            out_specs=(VMEM,) * (len(terms) // 2),
            compiler_params=limit(8),
            cost_estimate=cost(len(terms) * mat_flops, len(terms) * mat_bytes // 4),
            name="own_columns",
        )(own, bias, *terms)

    cuts = CUTS
    solved, *pays = pl.pallas_call(
        functools.partial(first_kernel, group, cuts),
        out_shape=(flat, *[slot] * group),
        in_specs=[HBM, HBM, HBM, HBM],
        out_specs=(VMEM,) * (1 + group),
        scratch_shapes=[
            block, square, pltpu.VMEM((2, rows, rows), f32), pltpu.VMEM((2, rows, width), f32),
            pltpu.SMEM(dest.shape, jnp.int32), pltpu.SemaphoreType.DMA((2,)),
            *[pltpu.SemaphoreType.DMA((cut,)) for cut in cuts],
        ],
        compiler_params=limit(24),
        cost_estimate=cost(3 * mat_flops, 3 * mat_bytes),
        name="level_first",
    )(stay(rhs), stay(diag_inv), stay(tiles), stay(dest))

    pays, (diag_later, rhs_later) = later(pays, diag_inv, rhs)
    got = exchange(pays)
    sol, v_tile, share = pl.pallas_call(
        vector_kernel,
        out_shape=(
            pltpu.HBM(rhs.shape, f32), jax.ShapeDtypeStruct((extra, width), f32), line,
        ),
        in_specs=[HBM, HBM, HBM, VMEM],
        out_specs=(HBM, VMEM, VMEM),
        scratch_shapes=[
            block, square, pltpu.VMEM((lines, LANES), f32), pltpu.SemaphoreType.DMA((4,)),
        ],
        compiler_params=limit(8),
        cost_estimate=cost(4 * rows * rows, mat_bytes),
        name="vector",
    )(stay(rhs_later), stay(diag_later), stay(obs_weight.reshape(lines, LANES)), solved)
    sums = summed(got, v_tile)

    sums, (diag_later, tiles_later, rhs_later) = later(sums, diag_inv, tiles, rhs)
    got = spread(sums)
    *terms, bias = pl.pallas_call(
        fold_kernel,
        out_shape=(*[term] * 6, flat),
        in_specs=[HBM, HBM, HBM],
        out_specs=(VMEM,) * 7,
        scratch_shapes=[
            square, pltpu.VMEM((2, rows, rows), f32), sems,
            pltpu.SemaphoreType.DMA((2, parts)), pltpu.SemaphoreType.DMA,
        ],
        compiler_params=limit(32),
        cost_estimate=cost(3 * rows * mat_flops // width, 3 * mat_bytes),
        name="fold_levels",
    )(stay(rhs_later), stay(diag_later), stay(tiles_later))
    m_hi, m_lo, d_hi, d_lo, l_hi, l_lo = terms
    got, (m_hi, m_lo, d_hi, d_lo, l_hi, l_lo, bias) = later(got, *terms, bias)
    send, own, kept = paired(got, None)
    other = shift(send, 1)
    m_part, d_part = early(own, bias, m_hi, m_lo, d_hi, d_lo)

    solved, *pays = pl.pallas_call(
        functools.partial(middle_kernel, group),
        out_shape=(flat, *[slot] * group),
        in_specs=[VMEM] * 13,
        out_specs=(VMEM,) * (1 + group),
        scratch_shapes=[pltpu.VMEM((2, rows, width), f32)],
        compiler_params=limit(16),
        cost_estimate=cost(3 * mat_flops, 2 * mat_bytes),
        name="level_middle",
    )(
        other, bias, m_hi, m_lo, d_hi, d_lo, m_part, d_part, l_hi, l_lo, share, kept, dest,
    )

    pays, (diag_later,) = later(pays, diag_inv)
    got = exchange(pays)
    near, *sums = summed(got, None)
    sums, (diag_later, rhs_later) = later(sums, diag_later, rhs)
    got = spread(sums)
    sol, d_hi, d_lo, bias = pl.pallas_call(
        functools.partial(last_terms_kernel, parts),
        out_shape=(pltpu.HBM(rhs.shape, f32), term, term, flat),
        in_specs=[HBM, VMEM, HBM, HBM],
        out_specs=(HBM, VMEM, VMEM, VMEM),
        scratch_shapes=[square, sems, pltpu.SemaphoreType.DMA((2,))],
        input_output_aliases={0: 0},
        compiler_params=limit(12),
        cost_estimate=cost(rows * rows, 2 * mat_bytes),
        name="last_terms",
    )(sol, solved, stay(rhs_later), stay(diag_later))
    got, (d_hi, d_lo, bias) = later(got, d_hi, d_lo, bias)
    send, own, total = paired(got, near)
    other = shift(send, 1)
    (d_part,) = early(own, bias, d_hi, d_lo)

    sol, seen = pl.pallas_call(
        functools.partial(last_kernel, group),
        out_shape=(pltpu.HBM(rhs.shape, f32), pltpu.HBM((1, width), f32)),
        in_specs=[HBM] + [VMEM] * 6,
        out_specs=(HBM, HBM),
        scratch_shapes=[block, pltpu.SemaphoreType.DMA((3,))],
        input_output_aliases={0: 0},
        compiler_params=limit(8),
        cost_estimate=cost(mat_flops, mat_bytes),
        name="level_last",
    )(sol, other, bias, d_hi, d_lo, d_part, total)
    return sol, seen.reshape(width)


def solution(mesh):
    in_specs = (
        P(None, "rows", "parts"),
        P(None, "rows", None),
        P(None, "rows", None, None),
        P(None, "rows", None),
        P("rows"),
    )
    out_specs = (P(None, "rows", "parts"), P("parts"))
    return jax.shard_map(body, mesh=mesh, in_specs=in_specs, out_specs=out_specs, check_vma=False)
```

```python
import functools

import jax
import jax.numpy as jnp
from jax import lax
from jax.experimental import pallas as pl
from jax.experimental.pallas import tpu as pltpu
from jax.sharding import PartitionSpec as P

LANES = 128
SUB = 8
CUTS = (4, 1, 1)
HBM = pl.BlockSpec(memory_space=pltpu.HBM)
ANY = pl.BlockSpec(memory_space=pl.ANY)
VMEM = pl.BlockSpec(memory_space=pltpu.VMEM)
SMEM = pl.BlockSpec(memory_space=pltpu.SMEM)


def split(x):
    hi = x.astype(jnp.bfloat16)
    lo = (x - hi.astype(jnp.float32)).astype(jnp.bfloat16)
    return hi, lo


def split_cols(x):
    hi, lo = split(x)
    return jnp.concatenate([hi, lo], axis=1)


def dot_terms(hi, lo, both):
    width = both.shape[1] // 2
    wide = jnp.dot(hi, both, preferred_element_type=jnp.float32)
    narrow = jnp.dot(lo, both[:, :width], preferred_element_type=jnp.float32)
    return wide[:, :width] + (wide[:, width:] + narrow)


def left_product(vector, matrix, rows):
    columns = vector.T
    total = None
    for r in range(rows // LANES):
        block = matrix[r * LANES : (r + 1) * LANES, :]
        term = jnp.sum(columns[:, r : r + 1] * block, axis=0, keepdims=True)
        total = term if total is None else total + term
    return total


def chunked(ref, buf, sem, parts):
    size = buf.shape[0] // parts
    copies = []
    for c in range(parts):
        at = pl.ds(c * size, size)
        copies.append(pltpu.make_async_copy(ref.at[at], buf.at[at], sem.at[c]))
    return copies


def position(group):
    place = lax.axis_index("rows")
    return lax.rem(place, group), place // 2, lax.rem(place, 2)


def deal(product, k, outs, spot, seg):
    lanes = len(outs) // 2
    for r, out in enumerate(outs):
        there = spot ^ r
        first = (lax.rem(there, 2) * lanes + there // 2) * seg
        out[pl.ds(k * seg, seg), :] = product[pl.ds(pl.multiple_of(first, SUB), seg), :]


def tile_of(lines, extra):
    if extra > len(lines):
        lines = [*lines, jnp.zeros((extra - len(lines), LANES), jnp.float32)]
    return jnp.concatenate(lines, axis=0)


def named(dest, level):
    return [jnp.full((1, LANES), dest[level, 0, k].astype(jnp.float32)) for k in range(2)]


def first_kernel(group, cuts, rhs, diag, tiles, dest, solved, *refs):
    outs, refs = refs[:group], refs[group:]
    b_buf, d_buf, l_buf, p_buf, i_buf, small, d_sem, l0_sem, l1_sem = refs
    rows = b_buf.shape[0]
    seg = rows // group
    spot, _, _ = position(group)
    d_copies = chunked(diag.at[0], d_buf, d_sem, cuts[0])
    l_copies = [
        chunked(tiles.at[0, 0], l_buf.at[0], l0_sem, cuts[1]),
        chunked(tiles.at[0, 1], l_buf.at[1], l1_sem, cuts[2]),
    ]
    b_copy = pltpu.make_async_copy(rhs.at[0], b_buf, small.at[0])
    i_copy = pltpu.make_async_copy(dest, i_buf, small.at[1])
    b_copy.start()
    for copies in (d_copies, *l_copies):
        for copy in copies:
            copy.start()
    i_copy.start()
    b_copy.wait()
    both = split_cols(b_buf[...])
    size = rows // cuts[0]
    for c in range(cuts[0]):
        at = pl.ds(c * size, size)
        d_copies[c].wait()
        solved[at, :] = dot_terms(*split(d_buf[at, :]), both)
    i_copy.wait()
    base = 2 * seg
    extra = outs[0].shape[0] - base
    meta = tile_of(named(i_buf, 0), extra)
    for out in outs:
        out[pl.ds(base, extra), :] = meta
    both = split_cols(solved[...])
    for k in range(2):
        size = rows // cuts[1 + k]
        for c in range(cuts[1 + k]):
            at = pl.ds(c * size, size)
            l_copies[k][c].wait()
            p_buf[k, at, :] = dot_terms(*split(l_buf[k, at, :]), both)
        deal(p_buf.at[k], k, outs, spot, seg)


def vector_kernel(rhs, diag, weight, solved, sol, v_tile, share, b_buf, v_buf, w_buf, sem):
    rows = b_buf.shape[0]
    copies = [
        pltpu.make_async_copy(weight, w_buf, sem.at[0]),
        pltpu.make_async_copy(rhs.at[2], b_buf, sem.at[1]),
        pltpu.make_async_copy(diag.at[2], v_buf, sem.at[2]),
        pltpu.make_async_copy(solved, sol.at[0], sem.at[3]),
    ]
    for copy in copies:
        copy.start()
    for copy in copies:
        copy.wait()
    vector = left_product(w_buf[...], v_buf, rows)
    count = rows // LANES
    lines = [vector[:, r * LANES : (r + 1) * LANES] for r in range(count)]
    v_tile[...] = tile_of(lines, v_tile.shape[0])
    share[...] = left_product(v_tile[0:count, :], b_buf, rows)


def fold_kernel(rhs, diag, tiles, m_hi, m_lo, d_hi, d_lo, l_hi, l_lo, bias,
                d_buf, l_buf, d_sem, l_sem, b_sem):
    rows = d_buf.shape[0]
    parts = d_sem.shape[0]
    size = rows // parts
    d_copies = chunked(diag.at[1], d_buf, d_sem, parts)
    l_copies = [chunked(tiles.at[1, 1 - k], l_buf.at[k], l_sem.at[k], parts) for k in range(2)]
    b_copy = pltpu.make_async_copy(rhs.at[1], bias, b_sem)
    for copy in (*d_copies, *l_copies[0], *l_copies[1], b_copy):
        copy.start()
    for copy in d_copies:
        copy.wait()
    hi, lo = split(d_buf[...])
    d_hi[...] = hi
    d_lo[...] = lo
    both = jnp.concatenate([hi, lo], axis=1)
    for c in range(parts):
        at = pl.ds(c * size, size)
        l_copies[0][c].wait()
        hi, lo = split(dot_terms(*split(l_buf[0, at, :]), both))
        m_hi[at, :] = hi
        m_lo[at, :] = lo
    for copy in l_copies[1]:
        copy.wait()
    hi, lo = split(l_buf[1])
    l_hi[...] = hi
    l_lo[...] = lo
    b_copy.wait()


def sum_kernel(group, mode, *refs):
    refs = list(refs)
    v_tile = refs.pop(0) if mode == "first" else None
    order = [*near_order(group), 0]
    got, refs = [refs[order.index(r)] for r in range(group)], refs[group:]
    near = None if mode == "first" else refs.pop(0)
    chips = group
    outs, (out, tiles) = refs[:chips], refs[chips:]
    seg = out.shape[1]
    base = 2 * seg
    spot, chip, _ = position(group)
    targets = []
    for r in range(group):
        rows = got[r][base : base + SUB, :]
        targets.append([rows[k, 0].astype(jnp.int32) for k in range(2)])
    out[...] = jnp.zeros_like(out)
    if near is None:
        for r in range(chips):
            outs[r][pl.ds(base, v_tile.shape[0]), :] = v_tile[...]
    else:
        for r in range(group):
            tiles[spot ^ r] = got[r][base : base + SUB, :]
        total = tiles[0, 2:3, :]
        for q in range(1, group):
            total = total + tiles[q, 2:3, :]
        near[...] = total
        outs[chips - 2][pl.ds(base, SUB), :] = jnp.broadcast_to(total, (SUB, LANES))
    for r in range(group):
        for k in range(2):
            out[targets[r][k]] += got[r][pl.ds(k * seg, seg), :]
    for r in range(chips):
        for j in range(2):
            outs[r][pl.ds(j * seg, seg), :] = out[2 * (chip ^ r) + j]


def pair_kernel(chips, mode, *refs):
    near = None if mode == "first" else refs[0]
    refs = refs if mode == "first" else refs[1:]
    order = [*far_order(chips), 0]
    got, refs = [refs[order.index(r)] for r in range(chips)], refs[chips:]
    send, own, more = refs
    lanes = chips // 2
    seg = own.shape[0] // lanes
    _, chip, core = position(chips)
    mine, theirs = pl.multiple_of(core * seg, SUB), pl.multiple_of((1 - core) * seg, SUB)
    for r in range(lanes):
        q = lax.rem(chip, lanes) ^ r
        a, b = got[r], got[r + lanes]
        at = pl.ds(pl.multiple_of(q * seg, SUB), seg)
        own[at, :] = a[pl.ds(mine, seg), :] + b[pl.ds(mine, seg), :]
        send[at, :] = a[pl.ds(theirs, seg), :] + b[pl.ds(theirs, seg), :]
    if mode == "first":
        extra = more.shape[1]
        for r in range(chips):
            tile = got[r][2 * seg :, :]
            more[chip ^ r] = tile
            at = pl.ds(pl.multiple_of(lanes * seg + (chip ^ r) * extra, SUB), extra)
            send[at, :] = tile
    else:
        more[...] = near[...] + got[chips - 2][2 * seg : 2 * seg + 1, :]


def own_part(group, which, own, bias, *refs):
    core = position(group)[2]
    depth = bias.shape[0] // 2
    at = pl.ds(pl.multiple_of((core if which == 0 else 1 - core) * depth, depth), depth)
    both = split_cols(bias[at, :] - own[0:depth, :])
    return [dot_terms(refs[j][:, at], refs[j + 1][:, at], both) for j in range(0, len(refs), 2)]


def early_kernel(group, *refs):
    count = (len(refs) - 2) // 3
    outs = refs[-count:]
    for out, value in zip(outs, own_part(group, 0, *refs[:-count])):
        out[...] = value


def middle_kernel(group, other, bias, m_hi, m_lo, d_hi, d_lo, m_part, d_part, l_hi, l_lo,
                  share, kept, dest, solved, *refs):
    outs, (p_buf,) = refs[:group], refs[group:]
    rows = bias.shape[0]
    seg = rows // group
    count = rows // LANES
    extra_v = kept.shape[1]
    offset = rows // 2
    spot, _, core = position(group)
    names = dest[1]
    targets = [names[0, k] for k in range(2)]
    product, value = own_part(group, 1, other, bias, m_hi, m_lo, d_hi, d_lo)
    value = value + d_part[...]
    solved[...] = value
    both = split_cols(value)
    p_buf[1] = product + m_part[...]
    p_buf[0] = dot_terms(l_hi[...], l_lo[...], both)
    part = share[...]
    for k in (1, 0):
        deal(p_buf.at[k], k, outs, spot, seg)
        here = kept[targets[k] // 2]
        at = pl.ds(pl.multiple_of(offset + (targets[k] // 2) * extra_v, SUB), extra_v)
        vector = jnp.where(lax.rem(targets[k], 2) == core, here, other[at, :])
        part = part - left_product(vector[0:count, :], p_buf.at[k], rows)
    base = 2 * seg
    extra = outs[0].shape[0] - base
    lines = [jnp.full((1, LANES), target.astype(jnp.float32)) for target in targets]
    meta = tile_of([*lines, part], extra)
    for out in outs:
        out[pl.ds(base, extra), :] = meta


def last_terms_kernel(parts, sol_in, solved, rhs, diag, sol, d_hi, d_lo, bias,
                      d_buf, d_sem, b_sem):
    rows = d_buf.shape[0]
    copies = chunked(diag.at[2], d_buf, d_sem, parts)
    b_copy = pltpu.make_async_copy(rhs.at[2], bias, b_sem.at[0])
    y_copy = pltpu.make_async_copy(solved, sol.at[1], b_sem.at[1])
    for copy in (*copies, b_copy, y_copy):
        copy.start()
    size = rows // parts
    for c in range(parts):
        at = pl.ds(c * size, size)
        copies[c].wait()
        hi, lo = split(d_buf[at, :])
        d_hi[at, :] = hi
        d_lo[at, :] = lo
    b_copy.wait()
    y_copy.wait()


def last_kernel(group, sol_in, other, bias, d_hi, d_lo, part, total, sol, seen, y_buf, sem):
    total_copy = pltpu.make_async_copy(total, seen, sem.at[2])
    total_copy.start()
    half = y_buf.shape[0] // 2
    copies = []
    for c in range(2):
        at = pl.ds(c * half, half)
        (value,) = own_part(group, 1, other, bias, d_hi.at[at], d_lo.at[at])
        y_buf[at, :] = value + part[at, :]
        copies.append(pltpu.make_async_copy(y_buf.at[at], sol.at[2, at], sem.at[c]))
        copies[c].start()
    total_copy.wait()
    for copy in copies:
        copy.wait()


def cost(flops, size):
    return pl.CostEstimate(flops=flops, bytes_accessed=size, transcendentals=0)


def limit(mib):
    return pltpu.CompilerParams(vmem_limit_bytes=mib << 20)


def stay(x):
    return pltpu.with_memory_space_constraint(x, pltpu.HBM)


def near_order(group):
    chips = (group - 2, *range(2, group - 2, 2))
    return [r + c for c in range(2) for r in chips] + [1]


def far_order(chips):
    return [chips - 2, chips - 1, *range(chips - 3, chips // 2 - 1, -1), *range(1, chips // 2)]


def later(first, *others):
    tied = lax.optimization_barrier((tuple(first), tuple(others)))
    return list(tied[0]), tied[1]


def body(rhs, diag_inv, tiles, dest, obs_weight):
    count = lax.axis_size("rows")
    group = count // 2
    chips = count // 2
    levels, rows, width = rhs.shape
    seg = rows // group
    lines = rows // LANES
    extra = -(-lines // SUB) * SUB
    parts = 2
    f32 = jnp.float32
    def shift(x, bits):
        return lax.ppermute(x, "rows", [(i, i ^ bits) for i in range(count)])

    block = pltpu.VMEM((rows, width), f32)
    square = pltpu.VMEM((rows, rows), f32)
    sems = pltpu.SemaphoreType.DMA((parts,))
    term = jax.ShapeDtypeStruct((rows, rows), jnp.bfloat16)
    line = jax.ShapeDtypeStruct((1, width), f32)
    flat = jax.ShapeDtypeStruct((rows, width), f32)
    slot = jax.ShapeDtypeStruct((2 * seg + SUB, width), f32)
    mat_flops = 2 * rows * rows * width
    mat_bytes = 4 * rows * rows

    def exchange(pays):
        return [shift(pays[r], r) for r in near_order(group)] + [pays[0]]

    def spread(sums):
        return [shift(sums[r], 2 * r) for r in far_order(chips)] + [sums[0]]

    def summed(got, v_tile):
        mode = "last" if v_tile is None else "first"
        tall = [2 * seg + (0 if v_tile is None else extra)] * chips
        if v_tile is None:
            tall[chips - 2] += SUB
        shapes = [jax.ShapeDtypeStruct((t, width), f32) for t in tall]
        given = list(got)
        if v_tile is None:
            shapes = [line, *shapes]
        else:
            given = [v_tile, *given]
        return pl.pallas_call(
            functools.partial(sum_kernel, group, mode),
            out_shape=tuple(shapes),
            in_specs=[VMEM] * len(given),
            out_specs=(VMEM,) * len(shapes),
            scratch_shapes=[
                pltpu.VMEM((count, seg, width), f32),
                pltpu.VMEM((group, SUB, width), f32),
            ],
            compiler_params=limit(6),
            cost_estimate=cost(2 * rows * width, 4 * 4 * rows * width),
            name="sum_parts",
        )(*given)

    def paired(got, near):
        mode = "first" if near is None else "last"
        lanes = chips // 2
        tall = lanes * seg + (chips * extra if near is None else 0)
        shapes = [jax.ShapeDtypeStruct((tall, width), f32)]
        shapes.append(jax.ShapeDtypeStruct((lanes * seg, width), f32))
        more = jax.ShapeDtypeStruct((chips, extra, width), f32)
        shapes.append(more if near is None else line)
        given = got if near is None else [near, *got]
        return pl.pallas_call(
            functools.partial(pair_kernel, chips, mode),
            out_shape=tuple(shapes),
            in_specs=[VMEM] * len(given),
            out_specs=(VMEM,) * len(shapes),
            compiler_params=limit(4),
            cost_estimate=cost(2 * rows * width, 4 * 3 * rows * width),
            name="pair_halves",
        )(*given)

    def early(own, bias, *terms):
        return pl.pallas_call(
            functools.partial(early_kernel, group),
            out_shape=(flat,) * (len(terms) // 2),
            in_specs=[VMEM] * (2 + len(terms)),
            out_specs=(VMEM,) * (len(terms) // 2),
            compiler_params=limit(8),
            cost_estimate=cost(len(terms) * mat_flops, len(terms) * mat_bytes // 4),
            name="own_columns",
        )(own, bias, *terms)

    cuts = CUTS
    solved, *pays = pl.pallas_call(
        functools.partial(first_kernel, group, cuts),
        out_shape=(flat, *[slot] * group),
        in_specs=[HBM, HBM, HBM, HBM],
        out_specs=(VMEM,) * (1 + group),
        scratch_shapes=[
            block, square, pltpu.VMEM((2, rows, rows), f32), pltpu.VMEM((2, rows, width), f32),
            pltpu.SMEM(dest.shape, jnp.int32), pltpu.SemaphoreType.DMA((2,)),
            *[pltpu.SemaphoreType.DMA((cut,)) for cut in cuts],
        ],
        compiler_params=limit(24),
        cost_estimate=cost(3 * mat_flops, 3 * mat_bytes),
        name="level_first",
    )(stay(rhs), stay(diag_inv), stay(tiles), stay(dest))

    pays, (diag_later, rhs_later) = later(pays, diag_inv, rhs)
    got = exchange(pays)
    sol, v_tile, share = pl.pallas_call(
        vector_kernel,
        out_shape=(
            pltpu.HBM(rhs.shape, f32), jax.ShapeDtypeStruct((extra, width), f32), line,
        ),
        in_specs=[HBM, HBM, HBM, VMEM],
        out_specs=(HBM, VMEM, VMEM),
        scratch_shapes=[
            block, square, pltpu.VMEM((lines, LANES), f32), pltpu.SemaphoreType.DMA((4,)),
        ],
        compiler_params=limit(8),
        cost_estimate=cost(4 * rows * rows, mat_bytes),
        name="vector",
    )(stay(rhs_later), stay(diag_later), stay(obs_weight.reshape(lines, LANES)), solved)
    sums = summed(got, v_tile)

    sums, (diag_later, tiles_later, rhs_later) = later(sums, diag_inv, tiles, rhs)
    got = spread(sums)
    *terms, bias = pl.pallas_call(
        fold_kernel,
        out_shape=(*[term] * 6, flat),
        in_specs=[HBM, HBM, HBM],
        out_specs=(VMEM,) * 7,
        scratch_shapes=[
            square, pltpu.VMEM((2, rows, rows), f32), sems,
            pltpu.SemaphoreType.DMA((2, parts)), pltpu.SemaphoreType.DMA,
        ],
        compiler_params=limit(32),
        cost_estimate=cost(3 * rows * mat_flops // width, 3 * mat_bytes),
        name="fold_levels",
    )(stay(rhs_later), stay(diag_later), stay(tiles_later))
    m_hi, m_lo, d_hi, d_lo, l_hi, l_lo = terms
    got, (m_hi, m_lo, d_hi, d_lo, l_hi, l_lo, bias) = later(got, *terms, bias)
    send, own, kept = paired(got, None)
    other = shift(send, 1)
    m_part, d_part = early(own, bias, m_hi, m_lo, d_hi, d_lo)

    solved, *pays = pl.pallas_call(
        functools.partial(middle_kernel, group),
        out_shape=(flat, *[slot] * group),
        in_specs=[VMEM] * 13,
        out_specs=(VMEM,) * (1 + group),
        scratch_shapes=[pltpu.VMEM((2, rows, width), f32)],
        compiler_params=limit(16),
        cost_estimate=cost(3 * mat_flops, 2 * mat_bytes),
        name="level_middle",
    )(
        other, bias, m_hi, m_lo, d_hi, d_lo, m_part, d_part, l_hi, l_lo, share, kept, dest,
    )

    pays, (diag_later,) = later(pays, diag_inv)
    got = exchange(pays)
    near, *sums = summed(got, None)
    sums, (diag_later, rhs_later) = later(sums, diag_later, rhs)
    got = spread(sums)
    sol, d_hi, d_lo, bias = pl.pallas_call(
        functools.partial(last_terms_kernel, parts),
        out_shape=(pltpu.HBM(rhs.shape, f32), term, term, flat),
        in_specs=[HBM, VMEM, HBM, HBM],
        out_specs=(HBM, VMEM, VMEM, VMEM),
        scratch_shapes=[square, sems, pltpu.SemaphoreType.DMA((2,))],
        input_output_aliases={0: 0},
        compiler_params=limit(12),
        cost_estimate=cost(rows * rows, 2 * mat_bytes),
        name="last_terms",
    )(sol, solved, stay(rhs_later), stay(diag_later))
    got, (d_hi, d_lo, bias) = later(got, d_hi, d_lo, bias)
    send, own, total = paired(got, near)
    other = shift(send, 1)
    (d_part,) = early(own, bias, d_hi, d_lo)

    sol, seen = pl.pallas_call(
        functools.partial(last_kernel, group),
        out_shape=(pltpu.HBM(rhs.shape, f32), pltpu.HBM((1, width), f32)),
        in_specs=[HBM] + [VMEM] * 6,
        out_specs=(HBM, HBM),
        scratch_shapes=[block, pltpu.SemaphoreType.DMA((3,))],
        input_output_aliases={0: 0},
        compiler_params=limit(8),
        cost_estimate=cost(mat_flops, mat_bytes),
        name="level_last",
    )(sol, other, bias, d_hi, d_lo, d_part, total)
    return sol, seen.reshape(width)


def solution(mesh):
    in_specs = (
        P(None, "rows", "parts"),
        P(None, "rows", None),
        P(None, "rows", None, None),
        P(None, "rows", None),
        P("rows"),
    )
    out_specs = (P(None, "rows", "parts"), P("parts"))
    return jax.shard_map(body, mesh=mesh, in_specs=in_specs, out_specs=out_specs, check_vma=False)
```

```python
import functools

import jax
import jax.numpy as jnp
from jax import lax
from jax.experimental import pallas as pl
from jax.experimental.pallas import tpu as pltpu
from jax.sharding import PartitionSpec as P

LANES = 128
SUB = 8
CUTS = (4, 1, 1)
HBM = pl.BlockSpec(memory_space=pltpu.HBM)
ANY = pl.BlockSpec(memory_space=pl.ANY)
VMEM = pl.BlockSpec(memory_space=pltpu.VMEM)
SMEM = pl.BlockSpec(memory_space=pltpu.SMEM)


def split(x):
    hi = x.astype(jnp.bfloat16)
    lo = (x - hi.astype(jnp.float32)).astype(jnp.bfloat16)
    return hi, lo


def split_cols(x):
    hi, lo = split(x)
    return jnp.concatenate([hi, lo], axis=1)


def dot_terms(hi, lo, both):
    width = both.shape[1] // 2
    wide = jnp.dot(hi, both, preferred_element_type=jnp.float32)
    narrow = jnp.dot(lo, both[:, :width], preferred_element_type=jnp.float32)
    return wide[:, :width] + (wide[:, width:] + narrow)


def left_product(vector, matrix, rows):
    columns = vector.T
    total = None
    for r in range(rows // LANES):
        block = matrix[r * LANES : (r + 1) * LANES, :]
        term = jnp.sum(columns[:, r : r + 1] * block, axis=0, keepdims=True)
        total = term if total is None else total + term
    return total


def chunked(ref, buf, sem, parts):
    size = buf.shape[0] // parts
    copies = []
    for c in range(parts):
        at = pl.ds(c * size, size)
        copies.append(pltpu.make_async_copy(ref.at[at], buf.at[at], sem.at[c]))
    return copies


def position(group):
    place = lax.axis_index("rows")
    return lax.rem(place, group), place // 2, lax.rem(place, 2)


def deal(product, k, outs, spot, seg):
    lanes = len(outs) // 2
    for r, out in enumerate(outs):
        there = spot ^ r
        first = (lax.rem(there, 2) * lanes + there // 2) * seg
        out[pl.ds(k * seg, seg), :] = product[pl.ds(pl.multiple_of(first, SUB), seg), :]


def tile_of(lines, extra):
    if extra > len(lines):
        lines = [*lines, jnp.zeros((extra - len(lines), LANES), jnp.float32)]
    return jnp.concatenate(lines, axis=0)


def named(dest, level):
    return [jnp.full((1, LANES), dest[level, 0, k].astype(jnp.float32)) for k in range(2)]


def first_kernel(group, cuts, rhs, diag, tiles, dest, solved, *refs):
    outs, refs = refs[:group], refs[group:]
    b_buf, d_buf, l_buf, p_buf, i_buf, small, d_sem, l0_sem, l1_sem = refs
    rows = b_buf.shape[0]
    seg = rows // group
    spot, _, _ = position(group)
    d_copies = chunked(diag.at[0], d_buf, d_sem, cuts[0])
    l_copies = [
        chunked(tiles.at[0, 0], l_buf.at[0], l0_sem, cuts[1]),
        chunked(tiles.at[0, 1], l_buf.at[1], l1_sem, cuts[2]),
    ]
    b_copy = pltpu.make_async_copy(rhs.at[0], b_buf, small.at[0])
    i_copy = pltpu.make_async_copy(dest, i_buf, small.at[1])
    b_copy.start()
    for copies in (d_copies, *l_copies):
        for copy in copies:
            copy.start()
    i_copy.start()
    b_copy.wait()
    both = split_cols(b_buf[...])
    size = rows // cuts[0]
    for c in range(cuts[0]):
        at = pl.ds(c * size, size)
        d_copies[c].wait()
        solved[at, :] = dot_terms(*split(d_buf[at, :]), both)
    i_copy.wait()
    base = 2 * seg
    extra = outs[0].shape[0] - base
    meta = tile_of(named(i_buf, 0), extra)
    for out in outs:
        out[pl.ds(base, extra), :] = meta
    both = split_cols(solved[...])
    for k in range(2):
        size = rows // cuts[1 + k]
        for c in range(cuts[1 + k]):
            at = pl.ds(c * size, size)
            l_copies[k][c].wait()
            p_buf[k, at, :] = dot_terms(*split(l_buf[k, at, :]), both)
        deal(p_buf.at[k], k, outs, spot, seg)


def vector_kernel(rhs, diag, weight, solved, sol, v_tile, share, b_buf, v_buf, w_buf, sem):
    rows = b_buf.shape[0]
    copies = [
        pltpu.make_async_copy(weight, w_buf, sem.at[0]),
        pltpu.make_async_copy(rhs.at[2], b_buf, sem.at[1]),
        pltpu.make_async_copy(diag.at[2], v_buf, sem.at[2]),
        pltpu.make_async_copy(solved, sol.at[0], sem.at[3]),
    ]
    for copy in copies:
        copy.start()
    for copy in copies:
        copy.wait()
    vector = left_product(w_buf[...], v_buf, rows)
    count = rows // LANES
    lines = [vector[:, r * LANES : (r + 1) * LANES] for r in range(count)]
    v_tile[...] = tile_of(lines, v_tile.shape[0])
    share[...] = left_product(v_tile[0:count, :], b_buf, rows)


def fold_kernel(rhs, diag, tiles, m_hi, m_lo, d_hi, d_lo, l_hi, l_lo, bias,
                d_buf, l_buf, d_sem, l_sem, b_sem):
    rows = d_buf.shape[0]
    parts = d_sem.shape[0]
    size = rows // parts
    d_copies = chunked(diag.at[1], d_buf, d_sem, parts)
    l_copies = [chunked(tiles.at[1, 1 - k], l_buf.at[k], l_sem.at[k], parts) for k in range(2)]
    b_copy = pltpu.make_async_copy(rhs.at[1], bias, b_sem)
    for copy in (*d_copies, *l_copies[0], *l_copies[1], b_copy):
        copy.start()
    for copy in d_copies:
        copy.wait()
    hi, lo = split(d_buf[...])
    d_hi[...] = hi
    d_lo[...] = lo
    both = jnp.concatenate([hi, lo], axis=1)
    for c in range(parts):
        at = pl.ds(c * size, size)
        l_copies[0][c].wait()
        hi, lo = split(dot_terms(*split(l_buf[0, at, :]), both))
        m_hi[at, :] = hi
        m_lo[at, :] = lo
    for copy in l_copies[1]:
        copy.wait()
    hi, lo = split(l_buf[1])
    l_hi[...] = hi
    l_lo[...] = lo
    b_copy.wait()


def sum_kernel(group, mode, *refs):
    refs = list(refs)
    v_tile = refs.pop(0) if mode == "first" else None
    order = [*near_order(group), 0]
    got, refs = [refs[order.index(r)] for r in range(group)], refs[group:]
    near = None if mode == "first" else refs.pop(0)
    chips = group
    outs, (out, tiles) = refs[:chips], refs[chips:]
    seg = out.shape[1]
    base = 2 * seg
    spot, chip, _ = position(group)
    targets = []
    for r in range(group):
        rows = got[r][base : base + SUB, :]
        targets.append([rows[k, 0].astype(jnp.int32) for k in range(2)])
    out[...] = jnp.zeros_like(out)
    if near is None:
        for r in range(chips):
            outs[r][pl.ds(base, v_tile.shape[0]), :] = v_tile[...]
    else:
        for r in range(group):
            tiles[spot ^ r] = got[r][base : base + SUB, :]
        total = tiles[0, 2:3, :]
        for q in range(1, group):
            total = total + tiles[q, 2:3, :]
        near[...] = total
        outs[chips - 2][pl.ds(base, SUB), :] = jnp.broadcast_to(total, (SUB, LANES))
    for r in range(group):
        for k in range(2):
            out[targets[r][k]] += got[r][pl.ds(k * seg, seg), :]
    for r in range(chips):
        for j in range(2):
            outs[r][pl.ds(j * seg, seg), :] = out[2 * (chip ^ r) + j]


def pair_kernel(chips, mode, *refs):
    near = None if mode == "first" else refs[0]
    refs = refs if mode == "first" else refs[1:]
    order = [*far_order(chips), 0]
    got, refs = [refs[order.index(r)] for r in range(chips)], refs[chips:]
    send, own, more = refs
    lanes = chips // 2
    seg = own.shape[0] // lanes
    _, chip, core = position(chips)
    mine, theirs = pl.multiple_of(core * seg, SUB), pl.multiple_of((1 - core) * seg, SUB)
    for r in range(lanes):
        q = lax.rem(chip, lanes) ^ r
        a, b = got[r], got[r + lanes]
        at = pl.ds(pl.multiple_of(q * seg, SUB), seg)
        own[at, :] = a[pl.ds(mine, seg), :] + b[pl.ds(mine, seg), :]
        send[at, :] = a[pl.ds(theirs, seg), :] + b[pl.ds(theirs, seg), :]
    if mode == "first":
        extra = more.shape[1]
        for r in range(chips):
            tile = got[r][2 * seg :, :]
            more[chip ^ r] = tile
            at = pl.ds(pl.multiple_of(lanes * seg + (chip ^ r) * extra, SUB), extra)
            send[at, :] = tile
    else:
        more[...] = near[...] + got[chips - 2][2 * seg : 2 * seg + 1, :]


def own_part(group, which, own, bias, *refs):
    core = position(group)[2]
    depth = bias.shape[0] // 2
    at = pl.ds(pl.multiple_of((core if which == 0 else 1 - core) * depth, depth), depth)
    both = split_cols(bias[at, :] - own[0:depth, :])
    return [dot_terms(refs[j][:, at], refs[j + 1][:, at], both) for j in range(0, len(refs), 2)]


def early_kernel(group, *refs):
    count = (len(refs) - 2) // 3
    outs = refs[-count:]
    for out, value in zip(outs, own_part(group, 0, *refs[:-count])):
        out[...] = value


def middle_kernel(group, other, bias, m_hi, m_lo, d_hi, d_lo, m_part, d_part, l_hi, l_lo,
                  share, kept, dest, solved, *refs):
    outs, (p_buf,) = refs[:group], refs[group:]
    rows = bias.shape[0]
    seg = rows // group
    count = rows // LANES
    extra_v = kept.shape[1]
    offset = rows // 2
    spot, _, core = position(group)
    names = dest[1]
    targets = [names[0, k] for k in range(2)]
    product, value = own_part(group, 1, other, bias, m_hi, m_lo, d_hi, d_lo)
    value = value + d_part[...]
    solved[...] = value
    both = split_cols(value)
    p_buf[1] = product + m_part[...]
    p_buf[0] = dot_terms(l_hi[...], l_lo[...], both)
    part = share[...]
    for k in (1, 0):
        deal(p_buf.at[k], k, outs, spot, seg)
        here = kept[targets[k] // 2]
        at = pl.ds(pl.multiple_of(offset + (targets[k] // 2) * extra_v, SUB), extra_v)
        vector = jnp.where(lax.rem(targets[k], 2) == core, here, other[at, :])
        part = part - left_product(vector[0:count, :], p_buf.at[k], rows)
    base = 2 * seg
    extra = outs[0].shape[0] - base
    lines = [jnp.full((1, LANES), target.astype(jnp.float32)) for target in targets]
    meta = tile_of([*lines, part], extra)
    for out in outs:
        out[pl.ds(base, extra), :] = meta


def last_terms_kernel(parts, sol_in, solved, rhs, diag, sol, d_hi, d_lo, bias,
                      d_buf, d_sem, b_sem):
    rows = d_buf.shape[0]
    copies = chunked(diag.at[2], d_buf, d_sem, parts)
    b_copy = pltpu.make_async_copy(rhs.at[2], bias, b_sem.at[0])
    y_copy = pltpu.make_async_copy(solved, sol.at[1], b_sem.at[1])
    for copy in (*copies, b_copy, y_copy):
        copy.start()
    size = rows // parts
    for c in range(parts):
        at = pl.ds(c * size, size)
        copies[c].wait()
        hi, lo = split(d_buf[at, :])
        d_hi[at, :] = hi
        d_lo[at, :] = lo
    b_copy.wait()
    y_copy.wait()


def last_kernel(group, sol_in, other, bias, d_hi, d_lo, part, total, sol, seen, y_buf, sem):
    total_copy = pltpu.make_async_copy(total, seen, sem.at[2])
    total_copy.start()
    half = y_buf.shape[0] // 2
    copies = []
    for c in range(2):
        at = pl.ds(c * half, half)
        (value,) = own_part(group, 1, other, bias, d_hi.at[at], d_lo.at[at])
        y_buf[at, :] = value + part[at, :]
        copies.append(pltpu.make_async_copy(y_buf.at[at], sol.at[2, at], sem.at[c]))
        copies[c].start()
    total_copy.wait()
    for copy in copies:
        copy.wait()


def cost(flops, size):
    return pl.CostEstimate(flops=flops, bytes_accessed=size, transcendentals=0)


def limit(mib):
    return pltpu.CompilerParams(vmem_limit_bytes=mib << 20)


def stay(x):
    return pltpu.with_memory_space_constraint(x, pltpu.HBM)


def near_order(group):
    chips = (group - 2, *range(2, group - 2, 2))
    return [r + c for c in range(2) for r in chips] + [1]


def far_order(chips):
    return [chips - 2, chips - 1, *range(chips - 3, 0, -1)]


def later(first, *others):
    tied = lax.optimization_barrier((tuple(first), tuple(others)))
    return list(tied[0]), tied[1]


def body(rhs, diag_inv, tiles, dest, obs_weight):
    count = lax.axis_size("rows")
    group = count // 2
    chips = count // 2
    levels, rows, width = rhs.shape
    seg = rows // group
    lines = rows // LANES
    extra = -(-lines // SUB) * SUB
    parts = 1
    f32 = jnp.float32
    def shift(x, bits):
        return lax.ppermute(x, "rows", [(i, i ^ bits) for i in range(count)])

    block = pltpu.VMEM((rows, width), f32)
    square = pltpu.VMEM((rows, rows), f32)
    sems = pltpu.SemaphoreType.DMA((parts,))
    term = jax.ShapeDtypeStruct((rows, rows), jnp.bfloat16)
    line = jax.ShapeDtypeStruct((1, width), f32)
    flat = jax.ShapeDtypeStruct((rows, width), f32)
    slot = jax.ShapeDtypeStruct((2 * seg + SUB, width), f32)
    mat_flops = 2 * rows * rows * width
    mat_bytes = 4 * rows * rows

    def exchange(pays):
        return [shift(pays[r], r) for r in near_order(group)] + [pays[0]]

    def spread(sums):
        return [shift(sums[r], 2 * r) for r in far_order(chips)] + [sums[0]]

    def summed(got, v_tile):
        mode = "last" if v_tile is None else "first"
        tall = [2 * seg + (0 if v_tile is None else extra)] * chips
        if v_tile is None:
            tall[chips - 2] += SUB
        shapes = [jax.ShapeDtypeStruct((t, width), f32) for t in tall]
        given = list(got)
        if v_tile is None:
            shapes = [line, *shapes]
        else:
            given = [v_tile, *given]
        return pl.pallas_call(
            functools.partial(sum_kernel, group, mode),
            out_shape=tuple(shapes),
            in_specs=[VMEM] * len(given),
            out_specs=(VMEM,) * len(shapes),
            scratch_shapes=[
                pltpu.VMEM((count, seg, width), f32),
                pltpu.VMEM((group, SUB, width), f32),
            ],
            compiler_params=limit(6),
            cost_estimate=cost(2 * rows * width, 4 * 4 * rows * width),
            name="sum_parts",
        )(*given)

    def paired(got, near):
        mode = "first" if near is None else "last"
        lanes = chips // 2
        tall = lanes * seg + (chips * extra if near is None else 0)
        shapes = [jax.ShapeDtypeStruct((tall, width), f32)]
        shapes.append(jax.ShapeDtypeStruct((lanes * seg, width), f32))
        more = jax.ShapeDtypeStruct((chips, extra, width), f32)
        shapes.append(more if near is None else line)
        given = got if near is None else [near, *got]
        return pl.pallas_call(
            functools.partial(pair_kernel, chips, mode),
            out_shape=tuple(shapes),
            in_specs=[VMEM] * len(given),
            out_specs=(VMEM,) * len(shapes),
            compiler_params=limit(4),
            cost_estimate=cost(2 * rows * width, 4 * 3 * rows * width),
            name="pair_halves",
        )(*given)

    def early(own, bias, *terms):
        return pl.pallas_call(
            functools.partial(early_kernel, group),
            out_shape=(flat,) * (len(terms) // 2),
            in_specs=[VMEM] * (2 + len(terms)),
            out_specs=(VMEM,) * (len(terms) // 2),
            compiler_params=limit(8),
            cost_estimate=cost(len(terms) * mat_flops, len(terms) * mat_bytes // 4),
            name="own_columns",
        )(own, bias, *terms)

    cuts = CUTS
    solved, *pays = pl.pallas_call(
        functools.partial(first_kernel, group, cuts),
        out_shape=(flat, *[slot] * group),
        in_specs=[HBM, HBM, HBM, HBM],
        out_specs=(VMEM,) * (1 + group),
        scratch_shapes=[
            block, square, pltpu.VMEM((2, rows, rows), f32), pltpu.VMEM((2, rows, width), f32),
            pltpu.SMEM(dest.shape, jnp.int32), pltpu.SemaphoreType.DMA((2,)),
            *[pltpu.SemaphoreType.DMA((cut,)) for cut in cuts],
        ],
        compiler_params=limit(24),
        cost_estimate=cost(3 * mat_flops, 3 * mat_bytes),
        name="level_first",
    )(stay(rhs), stay(diag_inv), stay(tiles), stay(dest))

    pays, (diag_later, rhs_later) = later(pays, diag_inv, rhs)
    got = exchange(pays)
    sol, v_tile, share = pl.pallas_call(
        vector_kernel,
        out_shape=(
            pltpu.HBM(rhs.shape, f32), jax.ShapeDtypeStruct((extra, width), f32), line,
        ),
        in_specs=[HBM, HBM, HBM, VMEM],
        out_specs=(HBM, VMEM, VMEM),
        scratch_shapes=[
            block, square, pltpu.VMEM((lines, LANES), f32), pltpu.SemaphoreType.DMA((4,)),
        ],
        compiler_params=limit(8),
        cost_estimate=cost(4 * rows * rows, mat_bytes),
        name="vector",
    )(stay(rhs_later), stay(diag_later), stay(obs_weight.reshape(lines, LANES)), solved)
    sums = summed(got, v_tile)

    sums, (diag_later, tiles_later, rhs_later) = later(sums, diag_inv, tiles, rhs)
    got = spread(sums)
    *terms, bias = pl.pallas_call(
        fold_kernel,
        out_shape=(*[term] * 6, flat),
        in_specs=[HBM, HBM, HBM],
        out_specs=(VMEM,) * 7,
        scratch_shapes=[
            square, pltpu.VMEM((2, rows, rows), f32), sems,
            pltpu.SemaphoreType.DMA((2, parts)), pltpu.SemaphoreType.DMA,
        ],
        compiler_params=limit(32),
        cost_estimate=cost(3 * rows * mat_flops // width, 3 * mat_bytes),
        name="fold_levels",
    )(stay(rhs_later), stay(diag_later), stay(tiles_later))
    m_hi, m_lo, d_hi, d_lo, l_hi, l_lo = terms
    got, (m_hi, m_lo, d_hi, d_lo, l_hi, l_lo, bias) = later(got, *terms, bias)
    send, own, kept = paired(got, None)
    other = shift(send, 1)
    m_part, d_part = early(own, bias, m_hi, m_lo, d_hi, d_lo)

    solved, *pays = pl.pallas_call(
        functools.partial(middle_kernel, group),
        out_shape=(flat, *[slot] * group),
        in_specs=[VMEM] * 13,
        out_specs=(VMEM,) * (1 + group),
        scratch_shapes=[pltpu.VMEM((2, rows, width), f32)],
        compiler_params=limit(16),
        cost_estimate=cost(3 * mat_flops, 2 * mat_bytes),
        name="level_middle",
    )(
        other, bias, m_hi, m_lo, d_hi, d_lo, m_part, d_part, l_hi, l_lo, share, kept, dest,
    )

    pays, (diag_later,) = later(pays, diag_inv)
    got = exchange(pays)
    near, *sums = summed(got, None)
    sums, (diag_later, rhs_later) = later(sums, diag_later, rhs)
    got = spread(sums)
    sol, d_hi, d_lo, bias = pl.pallas_call(
        functools.partial(last_terms_kernel, parts),
        out_shape=(pltpu.HBM(rhs.shape, f32), term, term, flat),
        in_specs=[HBM, VMEM, HBM, HBM],
        out_specs=(HBM, VMEM, VMEM, VMEM),
        scratch_shapes=[square, sems, pltpu.SemaphoreType.DMA((2,))],
        input_output_aliases={0: 0},
        compiler_params=limit(12),
        cost_estimate=cost(rows * rows, 2 * mat_bytes),
        name="last_terms",
    )(sol, solved, stay(rhs_later), stay(diag_later))
    got, (d_hi, d_lo, bias) = later(got, d_hi, d_lo, bias)
    send, own, total = paired(got, near)
    other = shift(send, 1)
    (d_part,) = early(own, bias, d_hi, d_lo)

    sol, seen = pl.pallas_call(
        functools.partial(last_kernel, group),
        out_shape=(pltpu.HBM(rhs.shape, f32), pltpu.HBM((1, width), f32)),
        in_specs=[HBM] + [VMEM] * 6,
        out_specs=(HBM, HBM),
        scratch_shapes=[block, pltpu.SemaphoreType.DMA((3,))],
        input_output_aliases={0: 0},
        compiler_params=limit(8),
        cost_estimate=cost(mat_flops, mat_bytes),
        name="level_last",
    )(sol, other, bias, d_hi, d_lo, d_part, total)
    return sol, seen.reshape(width)


def solution(mesh):
    in_specs = (
        P(None, "rows", "parts"),
        P(None, "rows", None),
        P(None, "rows", None, None),
        P(None, "rows", None),
        P("rows"),
    )
    out_specs = (P(None, "rows", "parts"), P("parts"))
    return jax.shard_map(body, mesh=mesh, in_specs=in_specs, out_specs=out_specs, check_vma=False)
```
